32 devices in a mesh: gx: 2 (over x), gy: 16 (over z, y, core).
Axes of the slice: x: 2, y: 2, z: 4, core: 2. Of those that a mesh axis runs over, the one named last changes fastest.
Arguments:
- density: float32 [1, 2048, 2048], P(None, 'gy', 'gx'), may hold values from 0.35 to 2.5, as said below
- xmomentum: float32 [1, 2048, 2048], P(None, 'gy', 'gx'), may hold values from -2.5 to 2.5
- ymomentum: float32 [1, 2048, 2048], P(None, 'gy', 'gx'), may hold values from -2.5 to 2.5
- shear_shift: int32 [1], replicated, may hold values from 0 to 2047
Outputs:
- density_new: float32 [1, 2048, 2048], P(None, 'gy', 'gx')
- xmomentum_new: float32 [1, 2048, 2048], P(None, 'gy', 'gx')
- ymomentum_new: float32 [1, 2048, 2048], P(None, 'gy', 'gx')
- potential: float32 [1, 2048, 2048], P(None, 'gy', 'gx')
The draws below stay inside these ranges and needn't reach their ends.
Inputs may be any that keep to these rules, and one draw needn't show every extreme that they name: Every density is positive.
All inputs are finite; a program needn't handle non-finite values.
Results may differ from the reference program's by a relative error of at most 0.00065.
Values sent between devices are 32-bit elements; how exact they have to be, the bound alone decides.
A program may use at most 64 MiB of HBM per device.

```python
import jax
import jax.numpy as jnp

NX = 2048
NY = 2048
PLANES = 1


def draw_density(key, part):
    rough = jax.random.uniform(jax.random.fold_in(key, 7), (PLANES, NY, NX), jnp.float32, -0.6, 0.6)
    values = jnp.exp(rough)
    return values


def block_levels(rng, extent, cuts, least, high):
    level, own = 1.0, jax.random.fold_in(rng, 6)
    for axis_at, blocks in cuts:
        heights = jnp.exp(jax.random.uniform(jax.random.fold_in(own, axis_at), (blocks,), jnp.float32, least / len(cuts), high / len(cuts)))
        level = level * jnp.repeat(heights, extent[axis_at] // blocks).reshape([-1 if axis == axis_at else 1 for axis in range(len(extent))])
    return level


def normal_values(own_key, shape, width, most, pieces=(), kind=jnp.bfloat16):
    gain = block_levels(own_key, shape, pieces, -0.22, 0.18) if pieces else 1.0
    result = jax.random.normal(own_key, shape, jnp.float32) * width * gain
    return jnp.minimum(jnp.maximum(result, -most), most).astype(kind)


def setup_inputs(seed: int = 0) -> dict:
    arg_keys = jax.random.split(jax.random.key(seed), 5)
    density = draw_density(jax.random.fold_in(arg_keys[4], 71), 0)
    xmomentum = normal_values(arg_keys[1], (PLANES, NY, NX), 0.4, 2.5, ((1, 16), (2, 2)), jnp.float32)
    ymomentum = normal_values(arg_keys[2], (PLANES, NY, NX), 0.4, 2.5, ((1, 16), (2, 2)), jnp.float32)
    shear_shift = jax.random.randint(arg_keys[3], (1,), 0, NY).astype(jnp.int32)
    return dict(density=density, xmomentum=xmomentum, ymomentum=ymomentum, shear_shift=shear_shift)


sound_speed = 1.0
time_step = 0.15
omega_rate = 0.5
shear_rate = 1.5
thickness = 0.5

def flux_of(state, normal):
    velocity = state[normal] / state[0]
    parts = [state[0] * velocity, state[1] * velocity, state[2] * velocity]
    parts[normal] = parts[normal] + sound_speed * sound_speed * state[0]
    return jnp.stack(parts)

def rusanov(left_state, right_state, normal):
    speed = jnp.maximum(jnp.abs(left_state[normal] / left_state[0]), jnp.abs(right_state[normal] / right_state[0])) + sound_speed
    return 0.5 * (flux_of(left_state, normal) + flux_of(right_state, normal)) - 0.5 * speed[None] * (right_state - left_state)

def advance(padded):
    flux_x = rusanov(padded[:, :, 1:-1, :-1], padded[:, :, 1:-1, 1:], 1)
    flux_y = rusanov(padded[:, :, :-1, 1:-1], padded[:, :, 1:, 1:-1], 2)
    state = padded[:, :, 1:-1, 1:-1]
    change = flux_x[..., 1:] - flux_x[..., :-1] + flux_y[:, :, 1:, :] - flux_y[:, :, :-1, :]
    updated = state - time_step * change
    density_new = updated[0]
    xmomentum_new = updated[1] + time_step * 2.0 * omega_rate * state[2]
    ymomentum_new = updated[2] - time_step * (2.0 - shear_rate) * omega_rate * state[1]
    return (density_new, xmomentum_new, ymomentum_new)

def kernel_table(y_waves, x_waves, shift):
    sigma = y_waves * shift % NY
    y_signed = jnp.where(y_waves < NY // 2, y_waves, y_waves - NY)
    x_signed = jnp.where(x_waves < NX // 2, x_waves, x_waves - NX)
    wave_x = 2.0 * jnp.pi / NX * (x_signed[None, :].astype(jnp.float32) + sigma[:, None].astype(jnp.float32) / NY)
    wave_y = 2.0 * jnp.pi / NY * y_signed[:, None].astype(jnp.float32)
    magnitude = jnp.sqrt(wave_x * wave_x + wave_y * wave_y)
    anchor = (y_waves[:, None] == 0) & (x_waves[None, :] == 0)
    safe_mag = jnp.where(anchor, 1.0, magnitude)
    return jnp.where(anchor, 0.0, -jnp.exp(-thickness * safe_mag) / safe_mag)

def reference(density, xmomentum, ymomentum, shear_shift):
    fields = jnp.stack([density, xmomentum, ymomentum])
    shift = shear_shift[0]
    left_col = jnp.roll(fields[..., -1], -shift, axis=2)
    right_col = jnp.roll(fields[..., 0], shift, axis=2)
    widened = jnp.concatenate([left_col[..., None], fields, right_col[..., None]], axis=3)
    padded = jnp.concatenate([widened[:, :, -1:], widened, widened[:, :, :1]], axis=2)
    density_new, xmomentum_new, ymomentum_new = advance(padded)
    y_waves = jnp.arange(NY, dtype=jnp.int32)
    x_waves = jnp.arange(NX, dtype=jnp.int32)
    sigma = y_waves * shift % NY
    angle = (sigma[:, None] * x_waves[None, :] % (NX * NY)).astype(jnp.float32) * (2.0 * jnp.pi / (NX * NY))
    spectrum = jnp.fft.fft(density_new, axis=1)
    sheared = spectrum * jnp.exp(-1j * angle)[None]
    modes = jnp.fft.fft(sheared, axis=2) * kernel_table(y_waves, x_waves, shift)[None]
    returned = jnp.fft.ifft(modes, axis=2) * jnp.exp(1j * angle)[None]
    potential = jnp.real(jnp.fft.ifft(returned, axis=1)).astype(jnp.float32)
    return (density_new, xmomentum_new, ymomentum_new, potential)
```

```python
import functools

import jax
import jax.numpy as jnp
import ml_dtypes
import numpy as np
from jax import lax
from jax.experimental import pallas as pl
from jax.experimental.pallas import tpu as pltpu
from jax.sharding import PartitionSpec as P

sound_speed = 1.0
time_step = 0.15
omega_rate = 0.5
shear_rate = 1.5
thickness = 0.5

LANES = 128
MESH = pl.DeviceIdType.MESH
VMEM = pl.BlockSpec(memory_space=pltpu.VMEM)


def split_np(table):
    head = table.astype(np.float32).astype(ml_dtypes.bfloat16)
    tail = (table - head.astype(np.float64)).astype(np.float32).astype(ml_dtypes.bfloat16)
    return np.stack([head, tail])


def split(value):
    head = value.astype(jnp.bfloat16)
    return head, (value - head.astype(jnp.float32)).astype(jnp.bfloat16)


def dot3(left, right, dims):
    def one(a, b):
        return lax.dot_general(a, b, (dims, ((), ())), preferred_element_type=jnp.float32)

    return one(left[0], right[0]) + (one(left[0], right[1]) + one(left[1], right[0]))


def exchange_kernel(count, gy, whole, src, dst, send, recv, own):
    radial = lax.axis_index("gx")
    azimuth = lax.axis_index("gy")
    me = radial * gy + azimuth if whole else azimuth

    def place(step):
        peer = lax.rem(me + step, count)
        device = (lax.div(peer, gy), lax.rem(peer, gy)) if whole else (radial, peer)
        return peer, device

    barrier = pltpu.get_barrier_semaphore()

    def greet(step, _):
        pl.semaphore_signal(barrier, inc=1, device_id=place(step)[1], device_id_type=MESH)
        return _

    def copy(step):
        peer, device = place(step)
        return pltpu.make_async_remote_copy(
            src_ref=src.at[peer],
            dst_ref=dst.at[me],
            send_sem=send.at[step],
            recv_sem=recv.at[step],
            device_id=device,
            device_id_type=MESH,
        )

    def start(step, _):
        copy(step).start()
        return _

    def finish(step, _):
        copy(step).wait()
        return _

    lax.fori_loop(1, count, greet, 0)
    mine = pltpu.make_async_copy(src.at[me], dst.at[me], own)
    mine.start()
    pl.semaphore_wait(barrier, count - 1)
    lax.fori_loop(1, count, start, 0)
    mine.wait()
    lax.fori_loop(1, count, finish, 0)


def exchange(blocks, gy, whole, ident):
    count = blocks.shape[0]
    return pl.pallas_call(
        functools.partial(exchange_kernel, count, gy, whole),
        out_shape=jax.ShapeDtypeStruct(blocks.shape, blocks.dtype),
        in_specs=[VMEM],
        out_specs=VMEM,
        scratch_shapes=[
            pltpu.SemaphoreType.DMA((count,)),
            pltpu.SemaphoreType.DMA((count,)),
            pltpu.SemaphoreType.DMA,
        ],
        compiler_params=pltpu.CompilerParams(collective_id=ident, has_side_effects=True),
    )(blocks)


def halo_kernel(gx, gy, d_ref, x_ref, y_ref, cols, rows, colbuf, rowbuf, csend, crecv, rsend, rrecv):
    radial = lax.axis_index("gx")
    azimuth = lax.axis_index("gy")
    before = lax.rem(radial + gx - 1, gx)
    after = lax.rem(radial + 1, gx)
    below = lax.rem(azimuth + gy - 1, gy)
    above = lax.rem(azimuth + 1, gy)
    height, width = d_ref.shape
    barrier = pltpu.get_barrier_semaphore()

    def greet(step, _):
        there = lax.rem(azimuth + step, gy)
        pl.semaphore_signal(barrier, inc=1, device_id=(before, there), device_id_type=MESH)
        pl.semaphore_signal(barrier, inc=1, device_id=(after, there), device_id_type=MESH)
        return _

    lax.fori_loop(0, gy, greet, 0)
    pl.semaphore_signal(barrier, inc=1, device_id=(radial, below), device_id_type=MESH)
    pl.semaphore_signal(barrier, inc=1, device_id=(radial, above), device_id_type=MESH)
    rowbuf[...] = jnp.zeros_like(rowbuf)
    colbuf[...] = jnp.zeros_like(colbuf)
    for at, ref in enumerate((d_ref, x_ref, y_ref)):
        rowbuf[0, at : at + 1, :] = ref[0:1, :]
        rowbuf[1, at : at + 1, :] = ref[height - 1 : height, :]
        colbuf[0, at : at + 1, :] = ref[:, 0:LANES].T[0:1, :]
        colbuf[1, at : at + 1, :] = ref[:, width - LANES : width].T[LANES - 1 : LANES, :]
    pl.semaphore_wait(barrier, 2 * gy + 2)

    def row_copy(side):
        return pltpu.make_async_remote_copy(
            src_ref=rowbuf.at[side],
            dst_ref=rows.at[1 - side],
            send_sem=rsend.at[side],
            recv_sem=rrecv.at[side],
            device_id=(radial, below if side == 0 else above),
            device_id_type=MESH,
        )

    def col_copy(side, step):
        there = lax.rem(azimuth + step, gy)
        return pltpu.make_async_remote_copy(
            src_ref=colbuf.at[side],
            dst_ref=cols.at[1 - side, azimuth],
            send_sem=csend.at[side, step],
            recv_sem=crecv.at[side, step],
            device_id=(before if side == 0 else after, there),
            device_id_type=MESH,
        )

    def start(step, _):
        col_copy(0, step).start()
        col_copy(1, step).start()
        return _

    def finish(step, _):
        col_copy(0, step).wait()
        col_copy(1, step).wait()
        return _

    row_copy(0).start()
    row_copy(1).start()
    lax.fori_loop(0, gy, start, 0)
    row_copy(0).wait()
    row_copy(1).wait()
    lax.fori_loop(0, gy, finish, 0)


def halo(fields, gx, gy, ident):
    height, width = fields[0].shape
    return pl.pallas_call(
        functools.partial(halo_kernel, gx, gy),
        out_shape=(
            jax.ShapeDtypeStruct((2, gy, 8, height), jnp.float32),
            jax.ShapeDtypeStruct((2, 8, width), jnp.float32),
        ),
        in_specs=[VMEM] * 3,
        out_specs=(VMEM, VMEM),
        scratch_shapes=[
            pltpu.VMEM((2, 8, height), jnp.float32),
            pltpu.VMEM((2, 8, width), jnp.float32),
            pltpu.SemaphoreType.DMA((2, gy)),
            pltpu.SemaphoreType.DMA((2, gy)),
            pltpu.SemaphoreType.DMA((2,)),
            pltpu.SemaphoreType.DMA((2,)),
        ],
        compiler_params=pltpu.CompilerParams(collective_id=ident, has_side_effects=True),
    )(*fields)


def flux_of(state, normal):
    velocity = state[normal] / state[0]
    parts = [state[0] * velocity, state[1] * velocity, state[2] * velocity]
    parts[normal] = parts[normal] + sound_speed * sound_speed * state[0]
    return parts, jnp.abs(velocity)


def rusanov(left, right, left_flux, right_flux, left_speed, right_speed):
    speed = jnp.maximum(left_speed, right_speed) + sound_speed
    return [
        0.5 * (fl + fr) - 0.5 * speed * (r - l)
        for l, r, fl, fr in zip(left, right, left_flux, right_flux)
    ]


def gas_update(now, down, up, west, east):
    change = [None] * 3
    for low, high, normal in ((west, east, 1), (down, up, 2)):
        low_f, low_s = flux_of(low, normal)
        mid_f, mid_s = flux_of(now, normal)
        high_f, high_s = flux_of(high, normal)
        left = rusanov(low, now, low_f, mid_f, low_s, mid_s)
        right = rusanov(now, high, mid_f, high_f, mid_s, high_s)
        for f in range(3):
            term = right[f] - left[f]
            change[f] = term if change[f] is None else change[f] + term
    return (
        now[0] - time_step * change[0],
        now[1] - time_step * change[1] + time_step * 2.0 * omega_rate * now[2],
        now[2] - time_step * change[2] - time_step * (2.0 - shear_rate) * omega_rate * now[1],
    )


def gas_kernel(d_ref, x_ref, y_ref, rows, cols, d_out, x_out, y_out):
    height, width = d_ref.shape
    refs = (d_ref, x_ref, y_ref)
    blocks = height // 8
    ghost = cols[...]
    ghost = jnp.concatenate([ghost[0], ghost[1]], axis=0).T
    sub = lax.broadcasted_iota(jnp.int32, (8, width), 0)
    lane = lax.broadcasted_iota(jnp.int32, (8, width), 1)
    for block in range(blocks):
        at = block * 8
        now = [ref[at : at + 8, :] for ref in refs]
        sides = ghost[at : at + 8]
        down, up, west, east = [], [], [], []
        for f in range(3):
            edge = refs[f][at - 1 : at, :] if block else rows[0, f : f + 1, :]
            down.append(jnp.where(sub == 0, edge, pltpu.roll(now[f], 1, 0)))
            edge = refs[f][at + 8 : at + 9, :] if block < blocks - 1 else rows[1, f : f + 1, :]
            up.append(jnp.where(sub == 7, edge, pltpu.roll(now[f], 7, 0)))
            west.append(jnp.where(lane == 0, sides[:, f : f + 1], pltpu.roll(now[f], 1, 1)))
            east.append(
                jnp.where(lane == width - 1, sides[:, 8 + f : 9 + f], pltpu.roll(now[f], width - 1, 1))
            )
        fresh = gas_update(now, down, up, west, east)
        d_out[at : at + 8, :], x_out[at : at + 8, :], y_out[at : at + 8, :] = fresh


def gas(fields, rows, cols):
    shape = jax.ShapeDtypeStruct(fields[0].shape, jnp.float32)
    return pl.pallas_call(
        gas_kernel,
        out_shape=(shape, shape, shape),
        in_specs=[VMEM] * 5,
        out_specs=(VMEM, VMEM, VMEM),
    )(*fields, rows, cols)


def unpack_kernel(d_ref, x_ref, y_ref, src, d_out, x_out, y_out, out):
    d_out[...] = d_ref[...]
    x_out[...] = x_ref[...]
    y_out[...] = y_ref[...]
    gy, packed, _ = src.shape
    low = lax.broadcasted_iota(jnp.int32, (packed, LANES), 1) < LANES // 2
    for tile in range(gy // 2):
        span = slice(tile * LANES, (tile + 1) * LANES)
        near, far = src[2 * tile], src[2 * tile + 1]
        out[0:packed, span] = jnp.where(low, near, flip(far))
        out[packed : 2 * packed, span] = jnp.where(low, flip(near), far)


def unpack(fields, blocks):
    shape = jax.ShapeDtypeStruct(fields[0].shape, jnp.float32)
    return pl.pallas_call(
        unpack_kernel,
        out_shape=(shape,) * 4,
        in_specs=[VMEM] * 4,
        out_specs=(VMEM,) * 4,
    )(*fields, blocks)


def slot_wave(group, index, gy, height):
    half = height // 2
    first = jnp.where(index < half, gy * index, gy // 2 + gy * (index - half))
    return jnp.where(group == 0, first, group + gy * index)


def azimuth_table(gy, height):
    ny = gy * height
    b = np.arange(height)
    out = np.zeros((gy // 2, 2 * height, 2 * height))
    for group in range(1, gy // 2):
        m = group + gy * np.arange(height)
        angle = 2.0 * np.pi * ((m[:, None] * b[None, :]) % ny) / ny
        c, s = np.cos(angle), np.sin(angle)
        out[group] = np.block([[c, s], [-s, c]])
    half = height // 2
    for part, residue in enumerate((0, gy // 2)):
        m = residue + gy * np.arange(half)
        angle = 2.0 * np.pi * ((m[:, None] * b[None, :]) % ny) / ny
        c, s = np.cos(angle), -np.sin(angle)
        if part == 0:
            s[0] = 1.0 - 2.0 * (b % 2)
        out[0, part * half : (part + 1) * half, part * height : (part + 1) * height] = c
        out[0, height + part * half : height + (part + 1) * half, part * height : (part + 1) * height] = s
    return split_np(out)


def azimuth_kernel(xb, src, table, out, stage):
    gy, packed, _ = src.shape
    height = table.shape[2] // 2
    fold = height // packed
    lane = lax.broadcasted_iota(jnp.int32, (height, LANES), 1)
    half = gy // 2
    step = 8 if packed % 8 == 0 else packed

    def put(group, base, at, value):
        for h in range(fold):
            row = base + h * packed + at
            stage[group, row : row + step, :] = (
                value if h == 0 else pltpu.roll(value, LANES - h * xb, 1)
            )

    for at in range(0, packed, step):
        f = [src[a, at : at + step, :] for a in range(gy)]
        plus = [None] + [f[a] + f[gy - a] for a in range(1, half)]
        minus = [None] + [f[a] - f[gy - a] for a in range(1, half)]
        for g in range(half + 1):
            re = f[0] + f[half] if g % 2 == 0 else f[0] - f[half]
            im = None
            for a in range(1, half):
                re = re + float(np.cos(2.0 * np.pi * ((a * g) % gy) / gy)) * plus[a]
                if 0 < g < half:
                    term = float(-np.sin(2.0 * np.pi * ((a * g) % gy) / gy)) * minus[a]
                    im = term if im is None else im + term
            if g == half:
                put(0, height, at, re)
            else:
                put(g, 0, at, re)
                if g:
                    put(g, height, at, im)
    for g in range(half):
        both = dot3((table[0, g], table[1, g]), split(stage[g]), ((1,), (0,)))
        out[g] = jnp.where(lane < xb, both[:height], pltpu.roll(both[height:], xb, 1))


def azimuth_forward(blocks, table, xb):
    gy, packed, _ = blocks.shape
    height = table.shape[2] // 2
    return pl.pallas_call(
        functools.partial(azimuth_kernel, xb),
        out_shape=jax.ShapeDtypeStruct((gy // 2, height, LANES), jnp.float32),
        in_specs=[VMEM] * 2,
        out_specs=VMEM,
        scratch_shapes=[pltpu.VMEM((gy // 2, 2 * height, LANES), jnp.float32)],
    )(blocks, table)


def azimuth_back_kernel(xb, src, table, out, stage):
    gy, packed, _ = out.shape
    height = table.shape[2] // 2
    fold = height // packed
    half = gy // 2
    step = 8 if packed % 8 == 0 else packed
    lane = lax.broadcasted_iota(jnp.int32, (step, LANES), 1)
    for g in range(half):
        value = src[g]
        value = jnp.concatenate([value, pltpu.roll(value, LANES - xb, 1)], axis=0)
        stage[g] = dot3((table[0, g], table[1, g]), split(value), ((0,), (0,)))

    def take(group, base, at):
        total = None
        for h in range(fold):
            row = base + h * packed + at
            value = stage[group, row : row + step, :]
            value = value if h == 0 else pltpu.roll(value, h * xb, 1)
            total = value if h == 0 else jnp.where(lane < h * xb, total, value)
        return total

    for at in range(0, packed, step):
        re = [take(g, 0, at) for g in range(half)]
        im = [None] + [take(g, height, at) for g in range(1, half)]
        last = take(0, height, at)
        for a in range(half + 1):
            even = re[0] + last if a % 2 == 0 else re[0] - last
            odd = None
            for g in range(1, half):
                angle = 2.0 * np.pi * ((a * g) % gy) / gy
                even = even + float(np.cos(angle)) * re[g]
                if 0 < a < half:
                    term = float(np.sin(angle)) * im[g]
                    odd = term if odd is None else odd + term
            if odd is None:
                out[a, at : at + step, :] = even
            else:
                out[a, at : at + step, :] = even - odd
                out[gy - a, at : at + step, :] = even + odd


def azimuth_back(slots, table, xb, gy, packed):
    height = table.shape[2] // 2
    return pl.pallas_call(
        functools.partial(azimuth_back_kernel, xb),
        out_shape=jax.ShapeDtypeStruct((gy, packed, LANES), jnp.float32),
        in_specs=[VMEM] * 2,
        out_specs=VMEM,
        scratch_shapes=[pltpu.VMEM((gy // 2, 2 * height, LANES), jnp.float32)],
    )(slots, table)


def flip(value):
    return pltpu.roll(value, LANES // 2, value.ndim - 1)


def fft_packed(parts, sign, signs):
    count = len(parts)
    if count == 1:
        return parts
    even = fft_packed(parts[0::2], sign, signs)
    odd = fft_packed(parts[1::2], sign, signs)
    low, high = [], []
    for k in range(count // 2):
        value = odd[k]
        if k:
            angle = sign * 2.0 * np.pi * k / count
            turned = flip(value) * signs
            if 4 * k == count:
                value = turned * float(np.sin(angle))
            else:
                value = value * float(np.cos(angle)) + turned * float(np.sin(angle))
        low.append(even[k] + value)
        high.append(even[k] - value)
    return low + high


def radial_tables(nx):
    wide = LANES // 2
    outer = nx // wide
    j = np.arange(wide)
    angle = 2.0 * np.pi * (np.outer(np.arange(outer), j) % nx) / nx
    c, s = np.cos(angle), np.sin(angle)
    turn = np.stack([np.concatenate([c, c], 1), np.concatenate([s, -s], 1)])
    angle = 2.0 * np.pi * (np.outer(j, j) % wide) / wide
    c, s = np.cos(angle), np.sin(angle)
    return turn.astype(np.float32), split_np(np.block([[c, -s], [s, c]]))


def radial_kernel(nx, ny, lines, src, wave, sigma, outer_turn, inner_turn, turn, table, out, stage):
    outer = src.shape[0]
    padded = stage.shape[1]
    half = LANES // 2
    gy = lax.axis_size("gy")
    first = jnp.logical_and(lax.axis_index("gx") == 0, lax.axis_index("gy") == 0)
    keep = jnp.where(first, 0.0, 1.0)
    lane8 = lax.broadcasted_iota(jnp.int32, (8, LANES), 1)
    sub8 = lax.broadcasted_iota(jnp.int32, (8, LANES), 0)
    signs = jnp.where(lane8 < half, -1.0, 1.0)
    low = lane8 < half

    def load(d, at):
        if at + 8 <= lines:
            value = src[d, at : at + 8, :]
            if at == 0:
                value = jnp.where(jnp.logical_and(sub8 == 0, lane8 >= half), value * keep, value)
            return value
        top = src[d, 0:1, :]
        extra = jnp.where(low[0:1], flip(jnp.broadcast_to(top, (8, LANES)))[0:1], 0.0)
        if at >= lines:
            return jnp.where(sub8 == 0, extra, 0.0)
        body = jnp.concatenate([src[d, at:lines, :], jnp.zeros((8 - lines + at, LANES), jnp.float32)], 0)
        if at == 0:
            body = jnp.where(jnp.logical_and(sub8 == 0, lane8 >= half), body * keep, body)
        return jnp.where(sub8 == lines - at, extra, body)

    def turned(value, c, s):
        return value * c + flip(value) * s

    for at in range(0, padded, 8):
        ci, si = inner_turn[0, at : at + 8, :], inner_turn[1, at : at + 8, :]
        parts = []
        for d in range(outer):
            co = outer_turn[0, at : at + 8, d : d + 1]
            so = outer_turn[1, at : at + 8, d : d + 1]
            parts.append(turned(load(d, at), co, -so * signs))
        parts = fft_packed(parts, -1.0, signs)
        for n in range(outer):
            value = turned(parts[n], ci, -si * signs)
            stage[n, at : at + 8, :] = turned(value, turn[0, n : n + 1, :], turn[1, n : n + 1, :])

    column = lax.broadcasted_iota(jnp.int32, (padded, LANES), 1)
    column = jnp.where(column < half, column, column - half)
    m = jnp.broadcast_to(wave[:, 0:1], (padded, LANES))
    shear = jnp.broadcast_to(sigma[:, 0:1], (padded, LANES)).astype(jnp.float32) / ny
    signed = jnp.where(m < ny // 2, m, m - ny).astype(jnp.float32)
    wave_y = 2.0 * jnp.pi / ny * signed
    wave_y = wave_y * wave_y
    weight = jnp.where(jnp.logical_or(m == 0, m == ny // 2), 1.0, 2.0) / (nx * ny)

    def convolve(n, _):
        modes = dot3(split(stage[n]), (table[0], table[1]), ((1,), (0,)))
        x_wave = n + outer * column
        x_signed = jnp.where(x_wave < nx // 2, x_wave, x_wave - nx).astype(jnp.float32)
        wave_x = 2.0 * jnp.pi / nx * (x_signed + shear)
        magnitude = jnp.sqrt(wave_x * wave_x + wave_y)
        anchor = jnp.logical_and(m == 0, x_wave == 0)
        safe = jnp.where(anchor, 1.0, magnitude)
        green = jnp.where(anchor, 0.0, -jnp.exp(-thickness * safe) / safe)
        modes = modes * (green * weight)
        stage[n] = dot3(split(modes), (table[0], table[1]), ((1,), (1,)))
        return _

    lax.fori_loop(0, outer, convolve, 0)

    for at in range(0, lines, 8):
        high = min(at + 8, lines)
        ci, si = inner_turn[0, at : at + 8, :], inner_turn[1, at : at + 8, :]
        more = lines - lines % 8
        parts = []
        for n in range(outer):
            value = turned(stage[n, at : at + 8, :], turn[0, n : n + 1, :], -turn[1, n : n + 1, :])
            parts.append(turned(value, ci, si * signs))
        parts = fft_packed(parts, 1.0, signs)
        if at == 0:
            ce, se = inner_turn[0, more : more + 8, :], inner_turn[1, more : more + 8, :]
            extras = []
            for n in range(outer):
                value = turned(stage[n, more : more + 8, :], turn[0, n : n + 1, :], -turn[1, n : n + 1, :])
                extras.append(turned(value, ce, se * signs))
            extras = fft_packed(extras, 1.0, signs)
        for d in range(outer):
            co = outer_turn[0, at : at + 8, d : d + 1]
            so = outer_turn[1, at : at + 8, d : d + 1]
            value = turned(parts[d], co, so * signs)
            if at == 0:
                co = outer_turn[0, more : more + 8, d : d + 1]
                so = outer_turn[1, more : more + 8, d : d + 1]
                extra = flip(turned(extras[d], co, so * signs))[lines % 8 : lines % 8 + 1]
                mask = jnp.logical_and(jnp.logical_and(sub8 == 0, lane8 >= half), first)
                value = jnp.where(mask, extra, value)
            out[d, at:high, :] = value[: high - at]


def radial(blocks, wave, sigma, outer_turn, inner_turn, turn, table, nx, ny):
    outer, lines, _ = blocks.shape
    padded = wave.shape[0]
    return pl.pallas_call(
        functools.partial(radial_kernel, nx, ny, lines),
        out_shape=jax.ShapeDtypeStruct(blocks.shape, jnp.float32),
        in_specs=[VMEM] * 7,
        out_specs=VMEM,
        scratch_shapes=[pltpu.VMEM((outer, padded, LANES), jnp.float32)],
    )(blocks, wave, sigma, outer_turn, inner_turn, turn, table)


def modulo(value, size):
    return value & (size - 1) if size & (size - 1) == 0 else lax.rem(value, size)


def fused_kernel(
    nx, ny, shift_ref, d_ref, x_ref, y_ref, y_source, turn, x_table, d_final, x_final, y_final, out,
    d_out, x_out, y_out, y_table, table_sem, field_sem,
    cols, rows, colbuf, colbuf2, rowbuf, outer_turn, inner_turn, src,
    got1, stage, give2, got2, green, mid, extra, give3, got3, give4,
    csend, crecv, rsend, rrecv, send1, recv1, send2, recv2, send3, recv3, send4, recv4,
):
    gx, gy = lax.axis_size("gx"), lax.axis_size("gy")
    radial_at, azimuth = lax.axis_index("gx"), lax.axis_index("gy")
    count = gx * gy
    me = radial_at * gy + azimuth
    height, width = d_ref.shape
    packed = src.shape[1]
    half_gy = gy // 2
    outer, lines, _ = got2.shape
    padded = inner_turn.shape[1]
    wide = LANES // 2
    step1 = packed // 4
    parts2 = lines // 8
    first = me == 0
    keep = jnp.where(first, 0.0, 1.0)
    lane8 = lax.broadcasted_iota(jnp.int32, (8, LANES), 1)
    sub8 = lax.broadcasted_iota(jnp.int32, (8, LANES), 0)
    signs = jnp.where(lane8 < wide, -1.0, 1.0)
    low = lane8 < wide
    fields = (d_ref, x_ref, y_ref)
    fresh = (d_out, x_out, y_out)
    before = lax.rem(radial_at + gx - 1, gx)
    after = lax.rem(radial_at + 1, gx)
    below = lax.rem(azimuth + gy - 1, gy)
    above = lax.rem(azimuth + 1, gy)
    inner_edge = radial_at == 0
    outer_edge = radial_at == gx - 1

    def device_of(peer):
        return lax.div(peer, gy), lax.rem(peer, gy)

    table_load = pltpu.make_async_copy(y_source, y_table, table_sem)
    table_load.start()
    cols[...] = jnp.zeros_like(cols)
    barrier = pltpu.get_barrier_semaphore()

    def greet(k, _):
        there = device_of(lax.rem(me + k, count))
        pl.semaphore_signal(barrier, inc=1, device_id=there, device_id_type=MESH)
        return _

    lax.fori_loop(1, count, greet, 0)

    rowbuf[...] = jnp.zeros_like(rowbuf)
    colbuf[...] = jnp.zeros_like(colbuf)
    for at, ref in enumerate(fields):
        rowbuf[0, at : at + 1, :] = ref[0:1, :]
        rowbuf[1, at : at + 1, :] = ref[height - 1 : height, :]
        colbuf[0, at : at + 1, :] = ref[:, 0:LANES].T[0:1, :]
        colbuf[1, at : at + 1, :] = ref[:, width - LANES : width].T[LANES - 1 : LANES, :]

    def row_copy(side):
        return pltpu.make_async_remote_copy(
            src_ref=rowbuf.at[side],
            dst_ref=rows.at[1 - side],
            send_sem=rsend.at[side],
            recv_sem=rrecv.at[side],
            device_id=(radial_at, below if side == 0 else above),
            device_id_type=MESH,
        )

    def col_copy(side, k):
        return pltpu.make_async_remote_copy(
            src_ref=colbuf.at[side],
            dst_ref=cols.at[1 - side, azimuth],
            send_sem=csend.at[side],
            recv_sem=crecv.at[side],
            device_id=(before if side == 0 else after, lax.rem(azimuth + k, gy)),
            device_id_type=MESH,
        )

    outgoing = (jnp.where(inner_edge, gy, 1), jnp.where(outer_edge, gy, 1))

    def col_start(side):
        def body(k, _):
            col_copy(side, k).start()
            return _

        lax.fori_loop(0, outgoing[side], body, 0)

    def col_wait(side, many, sem):
        @pl.when(many)
        def _all():
            pltpu.make_async_copy(cols.at[side], cols.at[side], sem.at[side]).wait()

        @pl.when(jnp.logical_not(many))
        def _one():
            pltpu.make_async_copy(cols.at[side, 0], cols.at[side, 0], sem.at[side]).wait()

    def line_copy(give, got, send, recv, rows, part, k):
        peer = lax.rem(azimuth + k, gy)
        span = pl.ds(pl.multiple_of(part * rows, rows), rows)
        return pltpu.make_async_remote_copy(
            src_ref=give.at[peer, span],
            dst_ref=got.at[azimuth, span],
            send_sem=send,
            recv_sem=recv.at[part],
            device_id=(radial_at, peer),
            device_id_type=MESH,
        )

    def all_copy(give, got, send, recv, rows, part, k):
        peer = lax.rem(me + k, count)
        span = pl.ds(pl.multiple_of(part * rows, rows), rows)
        return pltpu.make_async_remote_copy(
            src_ref=give.at[peer, span],
            dst_ref=got.at[me, span],
            send_sem=send,
            recv_sem=recv.at[part],
            device_id=device_of(peer),
            device_id_type=MESH,
        )

    def each(copy, peers):
        def body(k, _):
            copy(k).start()
            return _

        lax.fori_loop(peers // 2, peers, body, 0)
        lax.fori_loop(1, peers // 2, body, 0)

    def arrive(got, recv, rows, part):
        span = pl.ds(pl.multiple_of(part * rows, rows), rows)
        whole = got.at[pl.ds(0, got.shape[0] - 1), span]
        pltpu.make_async_copy(whole, whole, recv.at[part]).wait()

    def leave(give, send):
        whole = give.at[pl.ds(0, give.shape[0] - 1)]
        pltpu.make_async_copy(whole, whole, send).wait()

    one = functools.partial(line_copy, src, got1, send1, recv1, step1)
    two = functools.partial(all_copy, give2, got2, send2, recv2, 8)
    three = functools.partial(all_copy, give3, got3, send3, recv3, 8)
    four = functools.partial(line_copy, give4, out, send4, recv4, step1)

    pl.semaphore_wait(barrier, count - 1)
    for side in range(2):
        row_copy(side).start()
        col_start(side)

    blocks = height // 8
    sub_wide = lax.broadcasted_iota(jnp.int32, (8, width), 0)
    lane_wide = lax.broadcasted_iota(jnp.int32, (8, width), 1)

    def inner_rows(block, _):
        span = pl.ds(pl.multiple_of(block * 8, 8), 8)
        span_down = pl.ds(pl.multiple_of(block * 8 - 8, 8), 8)
        span_up = pl.ds(pl.multiple_of(block * 8 + 8, 8), 8)
        now = [ref[span, :] for ref in fields]
        down = [
            jnp.where(sub_wide == 0, pltpu.roll(ref[span_down, :], 1, 0), pltpu.roll(value, 1, 0))
            for ref, value in zip(fields, now)
        ]
        up = [
            jnp.where(sub_wide == 7, pltpu.roll(ref[span_up, :], 7, 0), pltpu.roll(value, 7, 0))
            for ref, value in zip(fields, now)
        ]
        west = [pltpu.roll(value, 1, 1) for value in now]
        east = [pltpu.roll(value, width - 1, 1) for value in now]
        for ref, value in zip(fresh, gas_update(now, down, up, west, east)):
            ref[span, :] = value
        return _

    lax.fori_loop(1, blocks - 1, inner_rows, 0)

    column = lax.broadcasted_iota(jnp.int32, (padded, LANES), 1)
    row = lax.broadcasted_iota(jnp.int32, (padded, LANES), 0)
    group = lax.div(me * lines, height)
    index = lax.rem(me * lines, height) + row
    half = height // 2
    at_zero = jnp.where(index < half, gy * index, gy // 2 + gy * (index - half))
    m = jnp.where(group == 0, at_zero, group + gy * index)
    m = jnp.where(row == lines, ny // 2, jnp.where(row > lines, 1, m))
    shift = shift_ref[0]
    sigma = modulo(m * shift, ny)
    column = jnp.where(column < wide, column, column - wide)
    unit = 2.0 * jnp.pi / (nx * ny)
    points = (column * wide, column)
    for turns, point in zip((outer_turn, inner_turn), points):
        angle = modulo(sigma * point, nx * ny).astype(jnp.float32) * unit
        turns[0] = jnp.cos(angle)
        turns[1] = jnp.sin(angle)
    shear = sigma.astype(jnp.float32) / ny
    signed = jnp.where(m < ny // 2, m, m - ny).astype(jnp.float32)
    wave_y = 2.0 * jnp.pi / ny * signed
    wave_y = wave_y * wave_y
    weight = jnp.where(jnp.logical_or(m == 0, m == ny // 2), 1.0, 2.0) / (nx * ny)

    def fill(n, _):
        x_wave = n + outer * column
        x_signed = jnp.where(x_wave < nx // 2, x_wave, x_wave - nx).astype(jnp.float32)
        wave_x = 2.0 * jnp.pi / nx * (x_signed + shear)
        magnitude = jnp.sqrt(wave_x * wave_x + wave_y)
        anchor = jnp.logical_and(m == 0, x_wave == 0)
        safe = jnp.where(anchor, 1.0, magnitude)
        green[n] = jnp.where(anchor, 0.0, -jnp.exp(-thickness * safe) / safe) * weight
        return _

    for side in range(2):
        row_copy(side).wait_recv()
        col_wait(side, outer_edge if side == 0 else inner_edge, crecv)
    here = azimuth * height

    def slid(side, amount, wraps):
        line = jnp.concatenate([cols[side, a] for a in range(gy)], axis=1)
        line = pltpu.roll(line, amount, 1)[:, :height]
        return jnp.where(wraps, line, cols[side, azimuth])

    ghost = jnp.concatenate(
        [
            slid(0, lax.rem(2 * ny - here - shift, ny), inner_edge),
            slid(1, lax.rem(ny - here + shift, ny), outer_edge),
        ],
        axis=0,
    ).T
    colbuf2[...] = ghost
    for block in (0, blocks - 1):
        at = block * 8
        now = [ref[at : at + 8, :] for ref in fields]
        sides = ghost[at : at + 8]
        down, up, west, east = [], [], [], []
        for f in range(3):
            edge = fields[f][at - 1 : at, :] if block else rows[0, f : f + 1, :]
            down.append(jnp.where(sub_wide == 0, edge, pltpu.roll(now[f], 1, 0)))
            edge = fields[f][at + 8 : at + 9, :] if block == 0 else rows[1, f : f + 1, :]
            up.append(jnp.where(sub_wide == 7, edge, pltpu.roll(now[f], 7, 0)))
            west.append(jnp.where(lane_wide == 0, sides[:, f : f + 1], pltpu.roll(now[f], 1, 1)))
            edge = pltpu.roll(now[f], width - 1, 1)
            east.append(jnp.where(lane_wide == width - 1, sides[:, 8 + f : 9 + f], edge))
        for ref, value in zip(fresh, gas_update(now, down, up, west, east)):
            ref[at : at + 8, :] = value
    sub2 = lax.broadcasted_iota(jnp.int32, (8, 2 * LANES), 0)
    lane2 = lax.broadcasted_iota(jnp.int32, (8, 2 * LANES), 1)

    def side_cells(block, _):
        span = pl.ds(pl.multiple_of(block * 8, 8), 8)
        span_down = pl.ds(pl.multiple_of(block * 8 - 8, 8), 8)
        span_up = pl.ds(pl.multiple_of(block * 8 + 8, 8), 8)
        sides = colbuf2[span, :]
        for end in range(2):
            start_lane = 0 if end == 0 else width - 2 * LANES
            window = slice(start_lane, start_lane + 2 * LANES)
            now, down, up, west, east = [], [], [], [], []
            for f, ref in enumerate(fields):
                value = ref[span, window]
                now.append(value)
                edge = pltpu.roll(ref[span_down, window], 1, 0)
                down.append(jnp.where(sub2 == 0, edge, pltpu.roll(value, 1, 0)))
                edge = pltpu.roll(ref[span_up, window], 7, 0)
                up.append(jnp.where(sub2 == 7, edge, pltpu.roll(value, 7, 0)))
                left = pltpu.roll(value, 1, 1)
                right = pltpu.roll(value, 2 * LANES - 1, 1)
                if end == 0:
                    left = jnp.where(lane2 == 0, sides[:, f : f + 1], left)
                else:
                    right = jnp.where(lane2 == 2 * LANES - 1, sides[:, 8 + f : 9 + f], right)
                west.append(left)
                east.append(right)
            target = slice(0, LANES) if end == 0 else slice(width - LANES, width)
            kept = slice(0, LANES) if end == 0 else slice(LANES, 2 * LANES)
            for ref, value in zip(fresh, gas_update(now, down, up, west, east)):
                ref[span, target] = value[:, kept]
        return _

    lax.fori_loop(1, blocks - 1, side_cells, 0)

    finals = [
        pltpu.make_async_copy(ref, final, field_sem.at[f])
        for f, (ref, final) in enumerate(zip(fresh, (d_final, x_final, y_final)))
    ]

    for part in range(4):
        for at in range(part * step1, (part + 1) * step1, 8):
            for tile in range(width // LANES):
                span = slice(tile * LANES, (tile + 1) * LANES)
                near = d_out[at : at + 8, span]
                far = d_out[at + packed : at + packed + 8, span]
                src[2 * tile, at : at + 8, :] = jnp.where(low, near, flip(far))
                src[2 * tile + 1, at : at + 8, :] = jnp.where(low, flip(near), far)
        each(functools.partial(one, part), gy)
    for final in finals:
        final.start()
    got1[azimuth] = src[azimuth]
    lax.fori_loop(0, outer, fill, 0)
    table_load.wait()

    for part in range(4):
        arrive(got1, recv1, step1, part)
        for at in range(part * step1, (part + 1) * step1, 8):
            f = [got1[a, at : at + 8, :] for a in range(gy)]
            plus = [None] + [f[a] + f[gy - a] for a in range(1, half_gy)]
            minus = [None] + [f[a] - f[gy - a] for a in range(1, half_gy)]

            def put(group, base, value):
                stage[group, base + at : base + at + 8, :] = value
                stage[group, base + packed + at : base + packed + at + 8, :] = flip(value)

            for g in range(half_gy + 1):
                re = f[0] + f[half_gy] if g % 2 == 0 else f[0] - f[half_gy]
                im = None
                for a in range(1, half_gy):
                    angle = 2.0 * np.pi * ((a * g) % gy) / gy
                    re = re + float(np.cos(angle)) * plus[a]
                    if 0 < g < half_gy:
                        term = float(-np.sin(angle)) * minus[a]
                        im = term if im is None else im + term
                if g == half_gy:
                    put(0, height, re)
                else:
                    put(g, 0, re)
                    if g:
                        put(g, height, im)
    lane = lax.broadcasted_iota(jnp.int32, (height, LANES), 1)
    ratio = height // lines
    for g in range(half_gy):
        both = dot3((y_table[0, g], y_table[1, g]), split(stage[g]), ((1,), (0,)))
        value = jnp.where(lane < wide, both[:height], flip(both[height:]))
        for q in range(ratio):
            give2[g * ratio + q] = value[q * lines : (q + 1) * lines]
    for part in range(parts2):
        each(functools.partial(two, part), count)
    got2[me] = give2[me]

    def turned(value, c, s):
        return value * c + flip(value) * s

    def solve(load, rows, store):
        ci, si = inner_turn[0, rows, :], inner_turn[1, rows, :] * signs
        co, so = outer_turn[0, rows, :], outer_turn[1, rows, :]
        parts = [turned(load(d), co[:, d : d + 1], -so[:, d : d + 1] * signs) for d in range(outer)]
        parts = fft_packed(parts, -1.0, signs)
        for n in range(outer):
            value = turned(parts[n], ci, -si)
            mid[n] = turned(value, turn[0, n : n + 1, :], turn[1, n : n + 1, :])
        modes = dot3(split(mid[...].reshape(outer * 8, LANES)), (x_table[0], x_table[1]), ((1,), (0,)))
        modes = modes * green[:, rows, :].reshape(outer * 8, LANES)
        modes = dot3(split(modes), (x_table[0], x_table[1]), ((1,), (1,)))
        mid[...] = modes.reshape(outer, 8, LANES)
        parts = []
        for n in range(outer):
            value = turned(mid[n], turn[0, n : n + 1, :], -turn[1, n : n + 1, :])
            parts.append(turned(value, ci, si))
        parts = fft_packed(parts, 1.0, signs)
        for d in range(outer):
            store(d, turned(parts[d], co[:, d : d + 1], so[:, d : d + 1] * signs))

    def load_extra(d):
        return jnp.where(jnp.logical_and(sub8 == 0, low), flip(got2[d, 0:8, :]), 0.0)

    def store_extra(d, value):
        extra[d] = flip(value)

    def chunk(part, _):
        arrive(got2, recv2, 8, part)
        rows = pl.ds(pl.multiple_of(part * 8, 8), 8)

        @pl.when(jnp.logical_and(part == 0, first))
        def _extra():
            solve(load_extra, pl.ds(lines, 8), store_extra)

        corner = jnp.logical_and(jnp.logical_and(sub8 == 0, lane8 >= wide), part == 0)
        damp = jnp.where(corner, keep, 1.0)
        mine = jnp.logical_and(corner, first)

        def load(d):
            return got2[d, rows, :] * damp

        def store(d, value):
            give3[d, rows, :] = jnp.where(mine, extra[d], value)

        solve(load, rows, store)
        each(functools.partial(three, part), count)
        return _

    lax.fori_loop(0, parts2, chunk, 0)
    got3[me] = give3[me]
    for part in range(parts2):
        arrive(got3, recv3, 8, part)

    for g in range(half_gy):
        value = got3[g * ratio : (g + 1) * ratio].reshape(height, LANES)
        value = jnp.concatenate([value, flip(value)], axis=0)
        stage[g] = dot3((y_table[0, g], y_table[1, g]), split(value), ((0,), (0,)))

    def take(group, base, at):
        near = stage[group, base + at : base + at + 8, :]
        far = stage[group, base + packed + at : base + packed + at + 8, :]
        return jnp.where(low, near, flip(far))

    for part in range(4):
        for at in range(part * step1, (part + 1) * step1, 8):
            re = [take(g, 0, at) for g in range(half_gy)]
            im = [None] + [take(g, height, at) for g in range(1, half_gy)]
            last = take(0, height, at)
            for a in range(half_gy + 1):
                even = re[0] + last if a % 2 == 0 else re[0] - last
                odd = None
                for g in range(1, half_gy):
                    angle = 2.0 * np.pi * ((a * g) % gy) / gy
                    even = even + float(np.cos(angle)) * re[g]
                    if 0 < a < half_gy:
                        term = float(np.sin(angle)) * im[g]
                        odd = term if odd is None else odd + term
                if odd is None:
                    give4[a, at : at + 8, :] = even
                else:
                    give4[a, at : at + 8, :] = even - odd
                    give4[gy - a, at : at + 8, :] = even + odd
        each(functools.partial(four, part), gy)
    out[azimuth] = give4[azimuth]
    for final in finals:
        final.wait()
    for side in range(2):
        row_copy(side).wait_send()
        col_wait(side, inner_edge if side == 0 else outer_edge, csend)
    leave(src, send1)
    leave(give2, send2)
    leave(give3, send3)
    for part in range(4):
        arrive(out, recv4, step1, part)
    leave(give4, send4)


def fused_step(shift, fields, tables, nx, ny, gx, gy, ident):
    height, width = fields[0].shape
    packed = height // 2
    count = gx * gy
    lines = ny // 2 // count
    padded = lines + 8
    f32 = jnp.float32
    blocks = (gy, packed, LANES)
    sems = [pltpu.SemaphoreType.DMA((2,))] * 4
    for parts in (4, lines // 8, lines // 8, 4):
        sems += [pltpu.SemaphoreType.DMA, pltpu.SemaphoreType.DMA((parts,))]
    shape = jax.ShapeDtypeStruct((height, width), f32)
    return pl.pallas_call(
        functools.partial(fused_kernel, nx, ny),
        out_shape=(shape, shape, shape, jax.ShapeDtypeStruct(blocks, f32)),
        in_specs=[pl.BlockSpec(memory_space=pltpu.SMEM)]
        + [VMEM] * 3
        + [pl.BlockSpec(memory_space=pl.ANY)]
        + [VMEM] * (len(tables) - 1),
        out_specs=(pl.BlockSpec(memory_space=pl.ANY),) * 3 + (VMEM,),
        scratch_shapes=[pltpu.VMEM((height, width), f32)] * 3
        + [
            pltpu.VMEM(tables[0].shape, tables[0].dtype),
            pltpu.SemaphoreType.DMA,
            pltpu.SemaphoreType.DMA((3,)),
            pltpu.VMEM((2, gy, 8, height), f32),
            pltpu.VMEM((2, 8, width), f32),
            pltpu.VMEM((2, 8, height), f32),
            pltpu.VMEM((height, 16), f32),
            pltpu.VMEM((2, 8, width), f32),
            pltpu.VMEM((2, padded, LANES), f32),
            pltpu.VMEM((2, padded, LANES), f32),
            pltpu.VMEM(blocks, f32),
            pltpu.VMEM(blocks, f32),
            pltpu.VMEM((gy // 2, 2 * height, LANES), f32),
            pltpu.VMEM((count, lines, LANES), f32),
            pltpu.VMEM((count, lines, LANES), f32),
            pltpu.VMEM((count, padded, LANES), f32),
            pltpu.VMEM((count, 8, LANES), f32),
            pltpu.VMEM((count, 8, LANES), f32),
            pltpu.VMEM((count, lines, LANES), f32),
            pltpu.VMEM((count, lines, LANES), f32),
            pltpu.VMEM(blocks, f32),
        ]
        + sems,
        compiler_params=pltpu.CompilerParams(collective_id=ident, has_side_effects=True),
    )(shift, *fields, *tables)


def shards(density, xmomentum, ymomentum, shear_shift):
    gx, gy = lax.axis_size("gx"), lax.axis_size("gy")
    here_x, here_y = lax.axis_index("gx"), lax.axis_index("gy")
    height, width = density.shape[1:]
    nx, ny = width * gx, height * gy
    count = gx * gy
    xb = width // gy
    lines = ny // 2 // count
    shift = shear_shift[0]
    fields = [density[0], xmomentum[0], ymomentum[0]]

    fold = LANES // xb
    packed = height // fold
    wide = LANES // 2
    outer = nx // wide
    group = wide // xb
    y_table = jnp.asarray(azimuth_table(gy, height))
    turn, table = radial_tables(nx)
    turn, table = jnp.asarray(turn), jnp.asarray(table)
    if group == 1 and packed % 32 == 0 and lines % 8 == 0 and height % lines == 0:
        results = fused_step(shear_shift, fields, (y_table, turn, table), nx, ny, gx, gy, 1)
        return tuple(r[None] for r in unpack(results[:3], results[3]))

    cols, rows = halo(fields, gx, gy, 0)
    cols = jnp.transpose(cols, (0, 2, 1, 3)).reshape(2, 8, ny)
    cols = jnp.concatenate([cols, cols], axis=2)
    start_left = (here_y * height + jnp.where(here_x == 0, shift, 0)) % ny
    start_right = (here_y * height - jnp.where(here_x == gx - 1, shift, 0)) % ny
    ghost = jnp.stack(
        [
            lax.dynamic_slice_in_dim(cols[0], start_left, height, 1),
            lax.dynamic_slice_in_dim(cols[1], start_right, height, 1),
        ]
    )
    density_new, xmomentum_new, ymomentum_new = gas(fields, rows, ghost)
    padded = (lines + 8) // 8 * 8
    row = jnp.arange(padded, dtype=jnp.int32)
    slot = (here_x * gy + here_y) * lines + row
    wave = slot_wave(slot // height, slot % height, gy, height)
    wave = jnp.where(row == lines, ny // 2, jnp.where(row > lines, 1, wave))
    sigma = wave * shift % ny
    unit = 2.0 * jnp.pi / (nx * ny)

    def phases(points):
        angle = (sigma[:, None] * points[None, :] % (nx * ny)).astype(jnp.float32) * unit
        return jnp.stack([jnp.cos(angle), jnp.sin(angle)])

    lane = jnp.arange(LANES, dtype=jnp.int32)
    outer_turn = phases(jnp.where(lane < outer, lane, 0) * wide)
    inner_turn = phases(lane % wide)
    full = (padded, LANES)
    line_tables = (
        jnp.broadcast_to(wave[:, None], full),
        jnp.broadcast_to(sigma[:, None], full),
        outer_turn,
        inner_turn,
        turn,
        table,
    )

    blocks = jnp.transpose(density_new.reshape(fold, packed, gy, xb), (2, 1, 0, 3))
    blocks = exchange(blocks.reshape(gy, packed, LANES), gy, False, 1)
    slots = azimuth_forward(blocks, y_table, xb)
    slots = slots[:, :, : 2 * xb].reshape(count, lines, 2 * xb)
    slots = exchange(slots, gy, True, 2)
    if group > 1:
        slots = slots.reshape(outer, group, lines, 2, xb)
        slots = jnp.transpose(slots, (0, 2, 3, 1, 4)).reshape(outer, lines, LANES)
    solved = radial(slots, *line_tables, nx, ny)
    if group > 1:
        solved = solved.reshape(outer, lines, 2, group, xb)
        solved = jnp.transpose(solved, (0, 3, 1, 2, 4)).reshape(count, lines, 2 * xb)
    solved = exchange(solved, gy, True, 3).reshape(gy // 2, height, 2 * xb)
    solved = jnp.pad(solved, ((0, 0), (0, 0), (0, LANES - 2 * xb)))
    lined = azimuth_back(solved, y_table, xb, gy, packed)
    lined = exchange(lined, gy, False, 4)
    potential = jnp.transpose(lined.reshape(gy, packed, fold, xb), (2, 1, 0, 3))
    potential = potential.reshape(height, width)
    return (density_new[None], xmomentum_new[None], ymomentum_new[None], potential[None])


def solution(mesh):
    split_spec = P(None, "gy", "gx")
    return jax.shard_map(
        shards,
        mesh=mesh,
        in_specs=(split_spec, split_spec, split_spec, P()),
        out_specs=(split_spec,) * 4,
        check_vma=False,
    )
```

```python
import functools

import jax
import jax.numpy as jnp
import ml_dtypes
import numpy as np
from jax import lax
from jax.experimental import pallas as pl
from jax.experimental.pallas import tpu as pltpu
from jax.sharding import PartitionSpec as P

sound_speed = 1.0
time_step = 0.15
omega_rate = 0.5
shear_rate = 1.5
thickness = 0.5

LANES = 128
MESH = pl.DeviceIdType.MESH
VMEM = pl.BlockSpec(memory_space=pltpu.VMEM)
HBM = pl.BlockSpec(memory_space=pl.ANY)


def split_np(table):
    head = table.astype(np.float32).astype(ml_dtypes.bfloat16)
    tail = (table - head.astype(np.float64)).astype(np.float32).astype(ml_dtypes.bfloat16)
    return np.stack([head, tail])


def split(value):
    head = value.astype(jnp.bfloat16)
    return head, (value - head.astype(jnp.float32)).astype(jnp.bfloat16)


def dot3(left, right, dims):
    def one(a, b):
        return lax.dot_general(a, b, (dims, ((), ())), preferred_element_type=jnp.float32)

    return one(left[0], right[0]) + (one(left[0], right[1]) + one(left[1], right[0]))


def exchange_kernel(count, gy, whole, src, dst, send, recv, own):
    radial = lax.axis_index("gx")
    azimuth = lax.axis_index("gy")
    me = radial * gy + azimuth if whole else azimuth

    def place(step):
        peer = lax.rem(me + step, count)
        device = (lax.div(peer, gy), lax.rem(peer, gy)) if whole else (radial, peer)
        return peer, device

    barrier = pltpu.get_barrier_semaphore()

    def greet(step, _):
        pl.semaphore_signal(barrier, inc=1, device_id=place(step)[1], device_id_type=MESH)
        return _

    def copy(step):
        peer, device = place(step)
        return pltpu.make_async_remote_copy(
            src_ref=src.at[peer],
            dst_ref=dst.at[me],
            send_sem=send.at[step],
            recv_sem=recv.at[step],
            device_id=device,
            device_id_type=MESH,
        )

    def start(step, _):
        copy(step).start()
        return _

    def finish(step, _):
        copy(step).wait()
        return _

    lax.fori_loop(1, count, greet, 0)
    mine = pltpu.make_async_copy(src.at[me], dst.at[me], own)
    mine.start()
    pl.semaphore_wait(barrier, count - 1)
    lax.fori_loop(1, count, start, 0)
    mine.wait()
    lax.fori_loop(1, count, finish, 0)


def exchange(blocks, gy, whole, ident):
    count = blocks.shape[0]
    return pl.pallas_call(
        functools.partial(exchange_kernel, count, gy, whole),
        out_shape=jax.ShapeDtypeStruct(blocks.shape, blocks.dtype),
        in_specs=[VMEM],
        out_specs=VMEM,
        scratch_shapes=[
            pltpu.SemaphoreType.DMA((count,)),
            pltpu.SemaphoreType.DMA((count,)),
            pltpu.SemaphoreType.DMA,
        ],
        compiler_params=pltpu.CompilerParams(collective_id=ident, has_side_effects=True),
    )(blocks)


def halo_kernel(gx, gy, d_ref, x_ref, y_ref, cols, rows, colbuf, rowbuf, csend, crecv, rsend, rrecv):
    radial = lax.axis_index("gx")
    azimuth = lax.axis_index("gy")
    before = lax.rem(radial + gx - 1, gx)
    after = lax.rem(radial + 1, gx)
    below = lax.rem(azimuth + gy - 1, gy)
    above = lax.rem(azimuth + 1, gy)
    height, width = d_ref.shape
    barrier = pltpu.get_barrier_semaphore()

    def greet(step, _):
        there = lax.rem(azimuth + step, gy)
        pl.semaphore_signal(barrier, inc=1, device_id=(before, there), device_id_type=MESH)
        pl.semaphore_signal(barrier, inc=1, device_id=(after, there), device_id_type=MESH)
        return _

    lax.fori_loop(0, gy, greet, 0)
    pl.semaphore_signal(barrier, inc=1, device_id=(radial, below), device_id_type=MESH)
    pl.semaphore_signal(barrier, inc=1, device_id=(radial, above), device_id_type=MESH)
    rowbuf[...] = jnp.zeros_like(rowbuf)
    colbuf[...] = jnp.zeros_like(colbuf)
    for at, ref in enumerate((d_ref, x_ref, y_ref)):
        rowbuf[0, at : at + 1, :] = ref[0:1, :]
        rowbuf[1, at : at + 1, :] = ref[height - 1 : height, :]
        colbuf[0, at : at + 1, :] = ref[:, 0:LANES].T[0:1, :]
        colbuf[1, at : at + 1, :] = ref[:, width - LANES : width].T[LANES - 1 : LANES, :]
    pl.semaphore_wait(barrier, 2 * gy + 2)

    def row_copy(side):
        return pltpu.make_async_remote_copy(
            src_ref=rowbuf.at[side],
            dst_ref=rows.at[1 - side],
            send_sem=rsend.at[side],
            recv_sem=rrecv.at[side],
            device_id=(radial, below if side == 0 else above),
            device_id_type=MESH,
        )

    def col_copy(side, step):
        there = lax.rem(azimuth + step, gy)
        return pltpu.make_async_remote_copy(
            src_ref=colbuf.at[side],
            dst_ref=cols.at[1 - side, azimuth],
            send_sem=csend.at[side, step],
            recv_sem=crecv.at[side, step],
            device_id=(before if side == 0 else after, there),
            device_id_type=MESH,
        )

    def start(step, _):
        col_copy(0, step).start()
        col_copy(1, step).start()
        return _

    def finish(step, _):
        col_copy(0, step).wait()
        col_copy(1, step).wait()
        return _

    row_copy(0).start()
    row_copy(1).start()
    lax.fori_loop(0, gy, start, 0)
    row_copy(0).wait()
    row_copy(1).wait()
    lax.fori_loop(0, gy, finish, 0)


def halo(fields, gx, gy, ident):
    height, width = fields[0].shape
    return pl.pallas_call(
        functools.partial(halo_kernel, gx, gy),
        out_shape=(
            jax.ShapeDtypeStruct((2, gy, 8, height), jnp.float32),
            jax.ShapeDtypeStruct((2, 8, width), jnp.float32),
        ),
        in_specs=[VMEM] * 3,
        out_specs=(VMEM, VMEM),
        scratch_shapes=[
            pltpu.VMEM((2, 8, height), jnp.float32),
            pltpu.VMEM((2, 8, width), jnp.float32),
            pltpu.SemaphoreType.DMA((2, gy)),
            pltpu.SemaphoreType.DMA((2, gy)),
            pltpu.SemaphoreType.DMA((2,)),
            pltpu.SemaphoreType.DMA((2,)),
        ],
        compiler_params=pltpu.CompilerParams(collective_id=ident, has_side_effects=True),
    )(*fields)


def flux_of(state, normal):
    velocity = state[normal] / state[0]
    parts = [state[0] * velocity, state[1] * velocity, state[2] * velocity]
    parts[normal] = parts[normal] + sound_speed * sound_speed * state[0]
    return parts, jnp.abs(velocity)


def rusanov(left, right, left_flux, right_flux, left_speed, right_speed):
    speed = jnp.maximum(left_speed, right_speed) + sound_speed
    return [
        0.5 * (fl + fr) - 0.5 * speed * (r - l)
        for l, r, fl, fr in zip(left, right, left_flux, right_flux)
    ]


def mass_flux(low, high, low_momentum, high_momentum, low_speed, high_speed):
    speed = jnp.maximum(low_speed, high_speed) + sound_speed
    return 0.5 * (low_momentum + high_momentum) - 0.5 * speed * (high - low)


def gas_update(now, down, up, west, east):
    change = [None] * 3
    for low, high, normal in ((west, east, 1), (down, up, 2)):
        low_f, low_s = flux_of(low, normal)
        mid_f, mid_s = flux_of(now, normal)
        high_f, high_s = flux_of(high, normal)
        left = rusanov(low, now, low_f, mid_f, low_s, mid_s)
        right = rusanov(now, high, mid_f, high_f, mid_s, high_s)
        for f in range(3):
            term = right[f] - left[f]
            change[f] = term if change[f] is None else change[f] + term
    return (
        now[0] - time_step * change[0],
        now[1] - time_step * change[1] + time_step * 2.0 * omega_rate * now[2],
        now[2] - time_step * change[2] - time_step * (2.0 - shear_rate) * omega_rate * now[1],
    )


def gas_kernel(d_ref, x_ref, y_ref, rows, cols, d_out, x_out, y_out):
    height, width = d_ref.shape
    refs = (d_ref, x_ref, y_ref)
    blocks = height // 8
    ghost = cols[...]
    ghost = jnp.concatenate([ghost[0], ghost[1]], axis=0).T
    sub = lax.broadcasted_iota(jnp.int32, (8, width), 0)
    lane = lax.broadcasted_iota(jnp.int32, (8, width), 1)
    for block in range(blocks):
        at = block * 8
        now = [ref[at : at + 8, :] for ref in refs]
        sides = ghost[at : at + 8]
        down, up, west, east = [], [], [], []
        for f in range(3):
            edge = refs[f][at - 1 : at, :] if block else rows[0, f : f + 1, :]
            down.append(jnp.where(sub == 0, edge, pltpu.roll(now[f], 1, 0)))
            edge = refs[f][at + 8 : at + 9, :] if block < blocks - 1 else rows[1, f : f + 1, :]
            up.append(jnp.where(sub == 7, edge, pltpu.roll(now[f], 7, 0)))
            west.append(jnp.where(lane == 0, sides[:, f : f + 1], pltpu.roll(now[f], 1, 1)))
            east.append(
                jnp.where(lane == width - 1, sides[:, 8 + f : 9 + f], pltpu.roll(now[f], width - 1, 1))
            )
        fresh = gas_update(now, down, up, west, east)
        d_out[at : at + 8, :], x_out[at : at + 8, :], y_out[at : at + 8, :] = fresh


def gas(fields, rows, cols):
    shape = jax.ShapeDtypeStruct(fields[0].shape, jnp.float32)
    return pl.pallas_call(
        gas_kernel,
        out_shape=(shape, shape, shape),
        in_specs=[VMEM] * 5,
        out_specs=(VMEM, VMEM, VMEM),
    )(*fields, rows, cols)


def unpack_kernel(d_in, x_in, y_in, src_in, d_out, x_out, y_out, out, d, x, y, src, packed_out, get, put):
    gy, packed, _ = src.shape
    low = lax.broadcasted_iota(jnp.int32, (packed, LANES), 1) < LANES // 2
    sources, buffers, targets = (src_in, d_in, x_in, y_in), (src, d, x, y), (out, d_out, x_out, y_out)
    gets = [pltpu.make_async_copy(a, b, get.at[f]) for f, (a, b) in enumerate(zip(sources, buffers))]
    puts = [
        pltpu.make_async_copy(a, b, put.at[f])
        for f, (a, b) in enumerate(zip((packed_out,) + buffers[1:], targets))
    ]
    for copy in gets:
        copy.start()
    gets[0].wait()
    for tile in range(gy // 2):
        span = slice(tile * LANES, (tile + 1) * LANES)
        near, far = src[2 * tile], src[2 * tile + 1]
        packed_out[0:packed, span] = jnp.where(low, near, flip(far))
        packed_out[packed : 2 * packed, span] = jnp.where(low, flip(near), far)
    puts[0].start()
    for f in range(1, 4):
        gets[f].wait()
        puts[f].start()
    for copy in puts:
        copy.wait()


def unpack(fields, blocks):
    shape = jax.ShapeDtypeStruct(fields[0].shape, jnp.float32)
    return pl.pallas_call(
        unpack_kernel,
        out_shape=(shape,) * 4,
        in_specs=[HBM] * 4,
        out_specs=(HBM,) * 4,
        scratch_shapes=[pltpu.VMEM(fields[0].shape, jnp.float32)] * 3
        + [pltpu.VMEM(blocks.shape, jnp.float32), pltpu.VMEM(fields[0].shape, jnp.float32)]
        + [pltpu.SemaphoreType.DMA((4,))] * 2,
    )(*fields, blocks)


def slot_wave(group, index, gy, height):
    half = height // 2
    first = jnp.where(index < half, gy * index, gy // 2 + gy * (index - half))
    return jnp.where(group == 0, first, group + gy * index)


def azimuth_table(gy, height):
    ny = gy * height
    b = np.arange(height)
    out = np.zeros((gy // 2, 2 * height, 2 * height))
    for group in range(1, gy // 2):
        m = group + gy * np.arange(height)
        angle = 2.0 * np.pi * ((m[:, None] * b[None, :]) % ny) / ny
        c, s = np.cos(angle), np.sin(angle)
        out[group] = np.block([[c, s], [-s, c]])
    half = height // 2
    for part, residue in enumerate((0, gy // 2)):
        m = residue + gy * np.arange(half)
        angle = 2.0 * np.pi * ((m[:, None] * b[None, :]) % ny) / ny
        c, s = np.cos(angle), -np.sin(angle)
        if part == 0:
            s[0] = 1.0 - 2.0 * (b % 2)
        out[0, part * half : (part + 1) * half, part * height : (part + 1) * height] = c
        out[0, height + part * half : height + (part + 1) * half, part * height : (part + 1) * height] = s
    return split_np(out)


def azimuth_kernel(xb, src, table, out, stage):
    gy, packed, _ = src.shape
    height = table.shape[2] // 2
    fold = height // packed
    lane = lax.broadcasted_iota(jnp.int32, (height, LANES), 1)
    half = gy // 2
    step = 8 if packed % 8 == 0 else packed

    def put(group, base, at, value):
        for h in range(fold):
            row = base + h * packed + at
            stage[group, row : row + step, :] = (
                value if h == 0 else pltpu.roll(value, LANES - h * xb, 1)
            )

    for at in range(0, packed, step):
        f = [src[a, at : at + step, :] for a in range(gy)]
        plus = [None] + [f[a] + f[gy - a] for a in range(1, half)]
        minus = [None] + [f[a] - f[gy - a] for a in range(1, half)]
        for g in range(half + 1):
            re = f[0] + f[half] if g % 2 == 0 else f[0] - f[half]
            im = None
            for a in range(1, half):
                re = re + float(np.cos(2.0 * np.pi * ((a * g) % gy) / gy)) * plus[a]
                if 0 < g < half:
                    term = float(-np.sin(2.0 * np.pi * ((a * g) % gy) / gy)) * minus[a]
                    im = term if im is None else im + term
            if g == half:
                put(0, height, at, re)
            else:
                put(g, 0, at, re)
                if g:
                    put(g, height, at, im)
    for g in range(half):
        both = dot3((table[0, g], table[1, g]), split(stage[g]), ((1,), (0,)))
        out[g] = jnp.where(lane < xb, both[:height], pltpu.roll(both[height:], xb, 1))


def azimuth_forward(blocks, table, xb):
    gy, packed, _ = blocks.shape
    height = table.shape[2] // 2
    return pl.pallas_call(
        functools.partial(azimuth_kernel, xb),
        out_shape=jax.ShapeDtypeStruct((gy // 2, height, LANES), jnp.float32),
        in_specs=[VMEM] * 2,
        out_specs=VMEM,
        scratch_shapes=[pltpu.VMEM((gy // 2, 2 * height, LANES), jnp.float32)],
    )(blocks, table)


def azimuth_back_kernel(xb, src, table, out, stage):
    gy, packed, _ = out.shape
    height = table.shape[2] // 2
    fold = height // packed
    half = gy // 2
    step = 8 if packed % 8 == 0 else packed
    lane = lax.broadcasted_iota(jnp.int32, (step, LANES), 1)
    for g in range(half):
        value = src[g]
        value = jnp.concatenate([value, pltpu.roll(value, LANES - xb, 1)], axis=0)
        stage[g] = dot3((table[0, g], table[1, g]), split(value), ((0,), (0,)))

    def take(group, base, at):
        total = None
        for h in range(fold):
            row = base + h * packed + at
            value = stage[group, row : row + step, :]
            value = value if h == 0 else pltpu.roll(value, h * xb, 1)
            total = value if h == 0 else jnp.where(lane < h * xb, total, value)
        return total

    for at in range(0, packed, step):
        re = [take(g, 0, at) for g in range(half)]
        im = [None] + [take(g, height, at) for g in range(1, half)]
        last = take(0, height, at)
        for a in range(half + 1):
            even = re[0] + last if a % 2 == 0 else re[0] - last
            odd = None
            for g in range(1, half):
                angle = 2.0 * np.pi * ((a * g) % gy) / gy
                even = even + float(np.cos(angle)) * re[g]
                if 0 < a < half:
                    term = float(np.sin(angle)) * im[g]
                    odd = term if odd is None else odd + term
            if odd is None:
                out[a, at : at + step, :] = even
            else:
                out[a, at : at + step, :] = even - odd
                out[gy - a, at : at + step, :] = even + odd


def azimuth_back(slots, table, xb, gy, packed):
    height = table.shape[2] // 2
    return pl.pallas_call(
        functools.partial(azimuth_back_kernel, xb),
        out_shape=jax.ShapeDtypeStruct((gy, packed, LANES), jnp.float32),
        in_specs=[VMEM] * 2,
        out_specs=VMEM,
        scratch_shapes=[pltpu.VMEM((gy // 2, 2 * height, LANES), jnp.float32)],
    )(slots, table)


def flip(value):
    return pltpu.roll(value, LANES // 2, value.ndim - 1)


def fft_packed(parts, sign, signs):
    count = len(parts)
    if count == 1:
        return parts
    even = fft_packed(parts[0::2], sign, signs)
    odd = fft_packed(parts[1::2], sign, signs)
    low, high = [], []
    for k in range(count // 2):
        value = odd[k]
        if k:
            angle = sign * 2.0 * np.pi * k / count
            turned = flip(value) * signs
            if 4 * k == count:
                value = turned * float(np.sin(angle))
            else:
                value = value * float(np.cos(angle)) + turned * float(np.sin(angle))
        low.append(even[k] + value)
        high.append(even[k] - value)
    return low + high


def radial_tables(nx):
    wide = LANES // 2
    outer = nx // wide
    j = np.arange(wide)
    angle = 2.0 * np.pi * (np.outer(np.arange(outer), j) % nx) / nx
    c, s = np.cos(angle), np.sin(angle)
    turn = np.stack([np.concatenate([c, c], 1), np.concatenate([s, -s], 1)])
    angle = 2.0 * np.pi * (np.outer(j, j) % wide) / wide
    c, s = np.cos(angle), np.sin(angle)
    return turn.astype(np.float32), split_np(np.block([[c, -s], [s, c]]))


def radial_kernel(nx, ny, lines, src, wave, sigma, outer_turn, inner_turn, turn, table, out, stage):
    outer = src.shape[0]
    padded = stage.shape[1]
    half = LANES // 2
    gy = lax.axis_size("gy")
    first = jnp.logical_and(lax.axis_index("gx") == 0, lax.axis_index("gy") == 0)
    keep = jnp.where(first, 0.0, 1.0)
    lane8 = lax.broadcasted_iota(jnp.int32, (8, LANES), 1)
    sub8 = lax.broadcasted_iota(jnp.int32, (8, LANES), 0)
    signs = jnp.where(lane8 < half, -1.0, 1.0)
    low = lane8 < half

    def load(d, at):
        if at + 8 <= lines:
            value = src[d, at : at + 8, :]
            if at == 0:
                value = jnp.where(jnp.logical_and(sub8 == 0, lane8 >= half), value * keep, value)
            return value
        top = src[d, 0:1, :]
        extra = jnp.where(low[0:1], flip(jnp.broadcast_to(top, (8, LANES)))[0:1], 0.0)
        if at >= lines:
            return jnp.where(sub8 == 0, extra, 0.0)
        body = jnp.concatenate([src[d, at:lines, :], jnp.zeros((8 - lines + at, LANES), jnp.float32)], 0)
        if at == 0:
            body = jnp.where(jnp.logical_and(sub8 == 0, lane8 >= half), body * keep, body)
        return jnp.where(sub8 == lines - at, extra, body)

    def turned(value, c, s):
        return value * c + flip(value) * s

    for at in range(0, padded, 8):
        ci, si = inner_turn[0, at : at + 8, :], inner_turn[1, at : at + 8, :]
        parts = []
        for d in range(outer):
            co = outer_turn[0, at : at + 8, d : d + 1]
            so = outer_turn[1, at : at + 8, d : d + 1]
            parts.append(turned(load(d, at), co, -so * signs))
        parts = fft_packed(parts, -1.0, signs)
        for n in range(outer):
            value = turned(parts[n], ci, -si * signs)
            stage[n, at : at + 8, :] = turned(value, turn[0, n : n + 1, :], turn[1, n : n + 1, :])

    column = lax.broadcasted_iota(jnp.int32, (padded, LANES), 1)
    column = jnp.where(column < half, column, column - half)
    m = jnp.broadcast_to(wave[:, 0:1], (padded, LANES))
    shear = jnp.broadcast_to(sigma[:, 0:1], (padded, LANES)).astype(jnp.float32) / ny
    signed = jnp.where(m < ny // 2, m, m - ny).astype(jnp.float32)
    wave_y = 2.0 * jnp.pi / ny * signed
    wave_y = wave_y * wave_y
    weight = jnp.where(jnp.logical_or(m == 0, m == ny // 2), 1.0, 2.0) / (nx * ny)

    def convolve(n, _):
        modes = dot3(split(stage[n]), (table[0], table[1]), ((1,), (0,)))
        x_wave = n + outer * column
        x_signed = jnp.where(x_wave < nx // 2, x_wave, x_wave - nx).astype(jnp.float32)
        wave_x = 2.0 * jnp.pi / nx * (x_signed + shear)
        magnitude = jnp.sqrt(wave_x * wave_x + wave_y)
        anchor = jnp.logical_and(m == 0, x_wave == 0)
        safe = jnp.where(anchor, 1.0, magnitude)
        green = jnp.where(anchor, 0.0, -jnp.exp(-thickness * safe) / safe)
        modes = modes * (green * weight)
        stage[n] = dot3(split(modes), (table[0], table[1]), ((1,), (1,)))
        return _

    lax.fori_loop(0, outer, convolve, 0)

    for at in range(0, lines, 8):
        high = min(at + 8, lines)
        ci, si = inner_turn[0, at : at + 8, :], inner_turn[1, at : at + 8, :]
        more = lines - lines % 8
        parts = []
        for n in range(outer):
            value = turned(stage[n, at : at + 8, :], turn[0, n : n + 1, :], -turn[1, n : n + 1, :])
            parts.append(turned(value, ci, si * signs))
        parts = fft_packed(parts, 1.0, signs)
        if at == 0:
            ce, se = inner_turn[0, more : more + 8, :], inner_turn[1, more : more + 8, :]
            extras = []
            for n in range(outer):
                value = turned(stage[n, more : more + 8, :], turn[0, n : n + 1, :], -turn[1, n : n + 1, :])
                extras.append(turned(value, ce, se * signs))
            extras = fft_packed(extras, 1.0, signs)
        for d in range(outer):
            co = outer_turn[0, at : at + 8, d : d + 1]
            so = outer_turn[1, at : at + 8, d : d + 1]
            value = turned(parts[d], co, so * signs)
            if at == 0:
                co = outer_turn[0, more : more + 8, d : d + 1]
                so = outer_turn[1, more : more + 8, d : d + 1]
                extra = flip(turned(extras[d], co, so * signs))[lines % 8 : lines % 8 + 1]
                mask = jnp.logical_and(jnp.logical_and(sub8 == 0, lane8 >= half), first)
                value = jnp.where(mask, extra, value)
            out[d, at:high, :] = value[: high - at]


def radial(blocks, wave, sigma, outer_turn, inner_turn, turn, table, nx, ny):
    outer, lines, _ = blocks.shape
    padded = wave.shape[0]
    return pl.pallas_call(
        functools.partial(radial_kernel, nx, ny, lines),
        out_shape=jax.ShapeDtypeStruct(blocks.shape, jnp.float32),
        in_specs=[VMEM] * 7,
        out_specs=VMEM,
        scratch_shapes=[pltpu.VMEM((outer, padded, LANES), jnp.float32)],
    )(blocks, wave, sigma, outer_turn, inner_turn, turn, table)


def modulo(value, size):
    return value & (size - 1) if size & (size - 1) == 0 else lax.rem(value, size)


def fused_kernel(
    nx, ny, shift_in, d_in, x_in, y_in, y_table_in, turn_in, x_table_in, d_final, x_final, y_final, out,
    shift_ref, d_ref, x_ref, y_ref, d_out, x_out, y_out, y_table, turn, x_table,
    shift_sem, load_sem, table_sem, field_sem, own_sem,
    cols, rows, colbuf, colbuf2, rowbuf, outer_turn, inner_turn, src,
    got1, stage, give2, got2, green, mid, extra, give3, got3, give4,
    csend, crecv, rsend, rrecv, send1, recv1, send2, recv2, send3, recv3, send4, recv4,
):
    gx, gy = lax.axis_size("gx"), lax.axis_size("gy")
    radial_at, azimuth = lax.axis_index("gx"), lax.axis_index("gy")
    count = gx * gy
    me = radial_at * gy + azimuth
    height, width = d_ref.shape
    packed = src.shape[1]
    half_gy = gy // 2
    outer, lines, _ = got2.shape
    padded = inner_turn.shape[1]
    wide = LANES // 2
    step1 = packed // 4
    parts2 = lines // 8
    first = me == 0
    keep = jnp.where(first, 0.0, 1.0)
    lane8 = lax.broadcasted_iota(jnp.int32, (8, LANES), 1)
    sub8 = lax.broadcasted_iota(jnp.int32, (8, LANES), 0)
    signs = jnp.where(lane8 < wide, -1.0, 1.0)
    low = lane8 < wide
    fields = (d_ref, x_ref, y_ref)
    fresh = (d_out, x_out, y_out)
    before = lax.rem(radial_at + gx - 1, gx)
    after = lax.rem(radial_at + 1, gx)
    below = lax.rem(azimuth + gy - 1, gy)
    above = lax.rem(azimuth + 1, gy)
    inner_edge = radial_at == 0
    outer_edge = radial_at == gx - 1

    def device_of(peer):
        return lax.div(peer, gy), lax.rem(peer, gy)

    loads = [
        pltpu.make_async_copy(source, ref, load_sem.at[f])
        for f, (source, ref) in enumerate(zip((d_in, x_in, y_in), fields))
    ]
    shift_load = pltpu.make_async_copy(shift_in, shift_ref, shift_sem)
    table_loads = [
        pltpu.make_async_copy(source, ref, table_sem.at[f])
        for f, (source, ref) in enumerate(zip((y_table_in, turn_in, x_table_in), (y_table, turn, x_table)))
    ]
    cols[...] = jnp.zeros_like(cols)
    barrier = pltpu.get_barrier_semaphore()

    def greet(k, _):
        there = device_of(lax.rem(me + k, count))
        pl.semaphore_signal(barrier, inc=1, device_id=there, device_id_type=MESH)
        return _

    for load in loads:
        load.start()
    shift_load.start()
    lax.fori_loop(1, count, greet, 0)
    for load in table_loads:
        load.start()

    rowbuf[...] = jnp.zeros_like(rowbuf)
    colbuf[...] = jnp.zeros_like(colbuf)
    for load in loads:
        load.wait()
    for at, ref in enumerate(fields):
        rowbuf[0, at : at + 1, :] = ref[0:1, :]
        rowbuf[1, at : at + 1, :] = ref[height - 1 : height, :]
        colbuf[0, at : at + 1, :] = ref[:, 0:LANES].T[0:1, :]
        colbuf[1, at : at + 1, :] = ref[:, width - LANES : width].T[LANES - 1 : LANES, :]

    def row_copy(side):
        return pltpu.make_async_remote_copy(
            src_ref=rowbuf.at[side],
            dst_ref=rows.at[1 - side],
            send_sem=rsend.at[side],
            recv_sem=rrecv.at[side],
            device_id=(radial_at, below if side == 0 else above),
            device_id_type=MESH,
        )

    def col_copy(side, k):
        return pltpu.make_async_remote_copy(
            src_ref=colbuf.at[side],
            dst_ref=cols.at[1 - side, azimuth],
            send_sem=csend.at[side],
            recv_sem=crecv.at[side],
            device_id=(before if side == 0 else after, lax.rem(azimuth + k, gy)),
            device_id_type=MESH,
        )

    outgoing = (jnp.where(inner_edge, gy, 1), jnp.where(outer_edge, gy, 1))

    def col_start(side):
        def body(k, _):
            col_copy(side, k).start()
            return _

        lax.fori_loop(0, outgoing[side], body, 0)

    def col_wait(side, many, sem):
        @pl.when(many)
        def _all():
            pltpu.make_async_copy(cols.at[side], cols.at[side], sem.at[side]).wait()

        @pl.when(jnp.logical_not(many))
        def _one():
            pltpu.make_async_copy(cols.at[side, 0], cols.at[side, 0], sem.at[side]).wait()

    def line_copy(give, got, send, recv, rows, part, k):
        peer = lax.rem(azimuth + k, gy)
        span = pl.ds(pl.multiple_of(part * rows, rows), rows)
        return pltpu.make_async_remote_copy(
            src_ref=give.at[peer, span],
            dst_ref=got.at[azimuth, span],
            send_sem=send,
            recv_sem=recv.at[part],
            device_id=(radial_at, peer),
            device_id_type=MESH,
        )

    def all_copy(give, got, send, recv, rows, part, k):
        peer = lax.rem(me + k, count)
        span = pl.ds(pl.multiple_of(part * rows, rows), rows)
        return pltpu.make_async_remote_copy(
            src_ref=give.at[peer, span],
            dst_ref=got.at[me, span],
            send_sem=send,
            recv_sem=recv.at[part],
            device_id=device_of(peer),
            device_id_type=MESH,
        )

    def each(copy, peers):
        def body(k, _):
            copy(k).start()
            return _

        lax.fori_loop(peers // 2, peers, body, 0)
        lax.fori_loop(1, peers // 2, body, 0)

    def arrive(got, recv, rows, part):
        span = pl.ds(pl.multiple_of(part * rows, rows), rows)
        whole = got.at[pl.ds(0, got.shape[0] - 1), span]
        pltpu.make_async_copy(whole, whole, recv.at[part]).wait()

    def leave(give, send):
        whole = give.at[pl.ds(0, give.shape[0] - 1)]
        pltpu.make_async_copy(whole, whole, send).wait()

    one = functools.partial(line_copy, src, got1, send1, recv1, step1)
    two = functools.partial(all_copy, give2, got2, send2, recv2, 8)
    three = functools.partial(all_copy, give3, got3, send3, recv3, 8)
    four = functools.partial(line_copy, give4, out, send4, recv4, step1)

    pl.semaphore_wait(barrier, count - 1)
    for side in range(2):
        row_copy(side).start()
        col_start(side)

    blocks = height // 8
    sub_wide = lax.broadcasted_iota(jnp.int32, (8, width), 0)
    lane_wide = lax.broadcasted_iota(jnp.int32, (8, width), 1)

    def density_rows(span, edge_down, edge_up):
        now = [ref[span, :] for ref in fields]
        rho, along, across = now
        speed = jnp.abs(along / rho)
        west = mass_flux(
            pltpu.roll(rho, 1, 1), rho, pltpu.roll(along, 1, 1), along, pltpu.roll(speed, 1, 1), speed
        )
        west = jnp.where(lane_wide == 0, 0.0, west)
        change = pltpu.roll(west, width - 1, 1) - west
        down = [
            jnp.where(sub_wide == 0, edge_down[f], pltpu.roll(now[f], 1, 0)) for f in (0, 2)
        ]
        up = [jnp.where(sub_wide == 7, edge_up[f], pltpu.roll(now[f], 7, 0)) for f in (0, 2)]
        speed = jnp.abs(across / rho)
        low_speed, high_speed = jnp.abs(down[1] / down[0]), jnp.abs(up[1] / up[0])
        change = change + (
            mass_flux(rho, up[0], across, up[1], speed, high_speed)
            - mass_flux(down[0], rho, down[1], across, low_speed, speed)
        )
        d_out[span, :] = rho - time_step * change

    def density_inner(block, _):
        span = pl.ds(pl.multiple_of(block * 8, 8), 8)
        span_down = pl.ds(pl.multiple_of(block * 8 - 8, 8), 8)
        span_up = pl.ds(pl.multiple_of(block * 8 + 8, 8), 8)
        density_rows(
            span,
            [pltpu.roll(ref[span_down, :], 1, 0) for ref in fields],
            [pltpu.roll(ref[span_up, :], 7, 0) for ref in fields],
        )
        return _

    lax.fori_loop(1, blocks - 1, density_inner, 0)
    shift_load.wait()

    column = lax.broadcasted_iota(jnp.int32, (padded, LANES), 1)
    row = lax.broadcasted_iota(jnp.int32, (padded, LANES), 0)
    group = lax.div(me * lines, height)
    index = lax.rem(me * lines, height) + row
    half = height // 2
    at_zero = jnp.where(index < half, gy * index, gy // 2 + gy * (index - half))
    m = jnp.where(group == 0, at_zero, group + gy * index)
    m = jnp.where(row == lines, ny // 2, jnp.where(row > lines, 1, m))
    shift = shift_ref[0]
    sigma = modulo(m * shift, ny)
    column = jnp.where(column < wide, column, column - wide)
    unit = 2.0 * jnp.pi / (nx * ny)
    points = (column * wide, column)
    for turns, point in zip((outer_turn, inner_turn), points):
        angle = modulo(sigma * point, nx * ny).astype(jnp.float32) * unit
        turns[0] = jnp.cos(angle)
        turns[1] = jnp.sin(angle)
    shear = sigma.astype(jnp.float32) / ny
    signed = jnp.where(m < ny // 2, m, m - ny).astype(jnp.float32)
    wave_y = 2.0 * jnp.pi / ny * signed
    wave_y = wave_y * wave_y
    weight = jnp.where(jnp.logical_or(m == 0, m == ny // 2), 1.0, 2.0) / (nx * ny)

    def fill(n, _):
        x_wave = n + outer * column
        x_signed = jnp.where(x_wave < nx // 2, x_wave, x_wave - nx).astype(jnp.float32)
        wave_x = 2.0 * jnp.pi / nx * (x_signed + shear)
        magnitude = jnp.sqrt(wave_x * wave_x + wave_y)
        anchor = jnp.logical_and(m == 0, x_wave == 0)
        safe = jnp.where(anchor, 1.0, magnitude)
        green[n] = jnp.where(anchor, 0.0, -jnp.exp(-thickness * safe) / safe) * weight
        return _

    for side in range(2):
        row_copy(side).wait_recv()
        col_wait(side, outer_edge if side == 0 else inner_edge, crecv)
    here = azimuth * height

    def slid(side, amount, wraps):
        line = jnp.concatenate([cols[side, a] for a in range(gy)], axis=1)
        line = pltpu.roll(line, amount, 1)[:, :height]
        return jnp.where(wraps, line, cols[side, azimuth])

    ghost = jnp.concatenate(
        [
            slid(0, lax.rem(2 * ny - here - shift, ny), inner_edge),
            slid(1, lax.rem(ny - here + shift, ny), outer_edge),
        ],
        axis=0,
    ).T
    colbuf2[...] = ghost
    for block in (0, blocks - 1):
        at = block * 8
        edge_down = [ref[at - 1 : at, :] if block else rows[0, f : f + 1, :] for f, ref in enumerate(fields)]
        edge_up = [ref[at + 8 : at + 9, :] if block == 0 else rows[1, f : f + 1, :] for f, ref in enumerate(fields)]
        density_rows(slice(at, at + 8), edge_down, edge_up)
    lane_tile = lax.broadcasted_iota(jnp.int32, (height, LANES), 1)
    for end in range(2):
        span = slice(0, LANES) if end == 0 else slice(width - LANES, width)
        mine = (d_ref[:, span], x_ref[:, span])
        other = (ghost[:, 8 * end : 8 * end + 1], ghost[:, 8 * end + 1 : 8 * end + 2])
        low_cell, high_cell = (other, mine) if end == 0 else (mine, other)
        flux = mass_flux(
            low_cell[0], high_cell[0], low_cell[1], high_cell[1],
            jnp.abs(low_cell[1] / low_cell[0]), jnp.abs(high_cell[1] / high_cell[0]),
        )
        flux = jnp.where(lane_tile == (0 if end == 0 else LANES - 1), time_step * flux, 0.0)
        d_out[:, span] = d_out[:, span] + flux if end == 0 else d_out[:, span] - flux

    finals = [
        pltpu.make_async_copy(ref, final, field_sem.at[f])
        for f, (ref, final) in enumerate(zip(fresh, (d_final, x_final, y_final)))
    ]

    for part in range(4):
        for at in range(part * step1, (part + 1) * step1, 8):
            for tile in range(width // LANES):
                span = slice(tile * LANES, (tile + 1) * LANES)
                near = d_out[at : at + 8, span]
                far = d_out[at + packed : at + packed + 8, span]
                src[2 * tile, at : at + 8, :] = jnp.where(low, near, flip(far))
                src[2 * tile + 1, at : at + 8, :] = jnp.where(low, flip(near), far)
        each(functools.partial(one, part), gy)
    finals[0].start()
    got1[azimuth] = src[azimuth]

    def inner_rows(block, _):
        span = pl.ds(pl.multiple_of(block * 8, 8), 8)
        span_down = pl.ds(pl.multiple_of(block * 8 - 8, 8), 8)
        span_up = pl.ds(pl.multiple_of(block * 8 + 8, 8), 8)
        now = [ref[span, :] for ref in fields]
        down = [
            jnp.where(sub_wide == 0, pltpu.roll(ref[span_down, :], 1, 0), pltpu.roll(value, 1, 0))
            for ref, value in zip(fields, now)
        ]
        up = [
            jnp.where(sub_wide == 7, pltpu.roll(ref[span_up, :], 7, 0), pltpu.roll(value, 7, 0))
            for ref, value in zip(fields, now)
        ]
        west = [pltpu.roll(value, 1, 1) for value in now]
        east = [pltpu.roll(value, width - 1, 1) for value in now]
        for ref, value in zip(fresh[1:], gas_update(now, down, up, west, east)[1:]):
            ref[span, :] = value
        return _

    lax.fori_loop(1, blocks - 1, inner_rows, 0)

    for block in (0, blocks - 1):
        at = block * 8
        now = [ref[at : at + 8, :] for ref in fields]
        sides = colbuf2[at : at + 8]
        down, up, west, east = [], [], [], []
        for f in range(3):
            edge = fields[f][at - 1 : at, :] if block else rows[0, f : f + 1, :]
            down.append(jnp.where(sub_wide == 0, edge, pltpu.roll(now[f], 1, 0)))
            edge = fields[f][at + 8 : at + 9, :] if block == 0 else rows[1, f : f + 1, :]
            up.append(jnp.where(sub_wide == 7, edge, pltpu.roll(now[f], 7, 0)))
            west.append(jnp.where(lane_wide == 0, sides[:, f : f + 1], pltpu.roll(now[f], 1, 1)))
            edge = pltpu.roll(now[f], width - 1, 1)
            east.append(jnp.where(lane_wide == width - 1, sides[:, 8 + f : 9 + f], edge))
        for ref, value in zip(fresh[1:], gas_update(now, down, up, west, east)[1:]):
            ref[at : at + 8, :] = value
    sub2 = lax.broadcasted_iota(jnp.int32, (8, 2 * LANES), 0)
    lane2 = lax.broadcasted_iota(jnp.int32, (8, 2 * LANES), 1)

    def side_cells(block, _):
        span = pl.ds(pl.multiple_of(block * 8, 8), 8)
        span_down = pl.ds(pl.multiple_of(block * 8 - 8, 8), 8)
        span_up = pl.ds(pl.multiple_of(block * 8 + 8, 8), 8)
        sides = colbuf2[span, :]
        for end in range(2):
            start_lane = 0 if end == 0 else width - 2 * LANES
            window = slice(start_lane, start_lane + 2 * LANES)
            now, down, up, west, east = [], [], [], [], []
            for f, ref in enumerate(fields):
                value = ref[span, window]
                now.append(value)
                edge = pltpu.roll(ref[span_down, window], 1, 0)
                down.append(jnp.where(sub2 == 0, edge, pltpu.roll(value, 1, 0)))
                edge = pltpu.roll(ref[span_up, window], 7, 0)
                up.append(jnp.where(sub2 == 7, edge, pltpu.roll(value, 7, 0)))
                left = pltpu.roll(value, 1, 1)
                right = pltpu.roll(value, 2 * LANES - 1, 1)
                if end == 0:
                    left = jnp.where(lane2 == 0, sides[:, f : f + 1], left)
                else:
                    right = jnp.where(lane2 == 2 * LANES - 1, sides[:, 8 + f : 9 + f], right)
                west.append(left)
                east.append(right)
            target = slice(0, LANES) if end == 0 else slice(width - LANES, width)
            kept = slice(0, LANES) if end == 0 else slice(LANES, 2 * LANES)
            for ref, value in zip(fresh[1:], gas_update(now, down, up, west, east)[1:]):
                ref[span, target] = value[:, kept]
        return _

    lax.fori_loop(1, blocks - 1, side_cells, 0)

    for final in finals[1:]:
        final.start()
    lax.fori_loop(0, outer, fill, 0)
    for load in table_loads:
        load.wait()

    for part in range(4):
        arrive(got1, recv1, step1, part)
        for at in range(part * step1, (part + 1) * step1, 8):
            f = [got1[a, at : at + 8, :] for a in range(gy)]
            plus = [None] + [f[a] + f[gy - a] for a in range(1, half_gy)]
            minus = [None] + [f[a] - f[gy - a] for a in range(1, half_gy)]

            def put(group, base, value):
                stage[group, base + at : base + at + 8, :] = value
                stage[group, base + packed + at : base + packed + at + 8, :] = flip(value)

            for g in range(half_gy + 1):
                re = f[0] + f[half_gy] if g % 2 == 0 else f[0] - f[half_gy]
                im = None
                for a in range(1, half_gy):
                    angle = 2.0 * np.pi * ((a * g) % gy) / gy
                    re = re + float(np.cos(angle)) * plus[a]
                    if 0 < g < half_gy:
                        term = float(-np.sin(angle)) * minus[a]
                        im = term if im is None else im + term
                if g == half_gy:
                    put(0, height, re)
                else:
                    put(g, 0, re)
                    if g:
                        put(g, height, im)
    lane = lax.broadcasted_iota(jnp.int32, (height, LANES), 1)
    ratio = height // lines
    for g in range(half_gy):
        both = dot3((y_table[0, g], y_table[1, g]), split(stage[g]), ((1,), (0,)))
        value = jnp.where(lane < wide, both[:height], flip(both[height:]))
        for q in range(ratio):
            give2[g * ratio + q] = value[q * lines : (q + 1) * lines]
    for part in range(parts2):
        each(functools.partial(two, part), count)
    got2[me] = give2[me]

    def turned(value, c, s):
        return value * c + flip(value) * s

    def solve(load, rows, store):
        ci, si = inner_turn[0, rows, :], inner_turn[1, rows, :] * signs
        co, so = outer_turn[0, rows, :], outer_turn[1, rows, :]
        parts = [turned(load(d), co[:, d : d + 1], -so[:, d : d + 1] * signs) for d in range(outer)]
        parts = fft_packed(parts, -1.0, signs)
        for n in range(outer):
            value = turned(parts[n], ci, -si)
            mid[n] = turned(value, turn[0, n : n + 1, :], turn[1, n : n + 1, :])
        modes = dot3(split(mid[...].reshape(outer * 8, LANES)), (x_table[0], x_table[1]), ((1,), (0,)))
        modes = modes * green[:, rows, :].reshape(outer * 8, LANES)
        modes = dot3(split(modes), (x_table[0], x_table[1]), ((1,), (1,)))
        mid[...] = modes.reshape(outer, 8, LANES)
        parts = []
        for n in range(outer):
            value = turned(mid[n], turn[0, n : n + 1, :], -turn[1, n : n + 1, :])
            parts.append(turned(value, ci, si))
        parts = fft_packed(parts, 1.0, signs)
        for d in range(outer):
            store(d, turned(parts[d], co[:, d : d + 1], so[:, d : d + 1] * signs))

    def load_extra(d):
        return jnp.where(jnp.logical_and(sub8 == 0, low), flip(got2[d, 0:8, :]), 0.0)

    def store_extra(d, value):
        extra[d] = flip(value)

    def chunk(part, _):
        arrive(got2, recv2, 8, part)
        rows = pl.ds(pl.multiple_of(part * 8, 8), 8)

        @pl.when(jnp.logical_and(part == 0, first))
        def _extra():
            solve(load_extra, pl.ds(lines, 8), store_extra)

        corner = jnp.logical_and(jnp.logical_and(sub8 == 0, lane8 >= wide), part == 0)
        damp = jnp.where(corner, keep, 1.0)
        mine = jnp.logical_and(corner, first)

        def load(d):
            return got2[d, rows, :] * damp

        def store(d, value):
            give3[d, rows, :] = jnp.where(mine, extra[d], value)

        solve(load, rows, store)
        each(functools.partial(three, part), count)
        return _

    lax.fori_loop(0, parts2, chunk, 0)
    got3[me] = give3[me]
    for part in range(parts2):
        arrive(got3, recv3, 8, part)

    for g in range(half_gy):
        value = got3[g * ratio : (g + 1) * ratio].reshape(height, LANES)
        value = jnp.concatenate([value, flip(value)], axis=0)
        stage[g] = dot3((y_table[0, g], y_table[1, g]), split(value), ((0,), (0,)))

    def take(group, base, at):
        near = stage[group, base + at : base + at + 8, :]
        far = stage[group, base + packed + at : base + packed + at + 8, :]
        return jnp.where(low, near, flip(far))

    for part in range(4):
        for at in range(part * step1, (part + 1) * step1, 8):
            re = [take(g, 0, at) for g in range(half_gy)]
            im = [None] + [take(g, height, at) for g in range(1, half_gy)]
            last = take(0, height, at)
            for a in range(half_gy + 1):
                even = re[0] + last if a % 2 == 0 else re[0] - last
                odd = None
                for g in range(1, half_gy):
                    angle = 2.0 * np.pi * ((a * g) % gy) / gy
                    even = even + float(np.cos(angle)) * re[g]
                    if 0 < a < half_gy:
                        term = float(np.sin(angle)) * im[g]
                        odd = term if odd is None else odd + term
                if odd is None:
                    give4[a, at : at + 8, :] = even
                else:
                    give4[a, at : at + 8, :] = even - odd
                    give4[gy - a, at : at + 8, :] = even + odd
        each(functools.partial(four, part), gy)
    own = pltpu.make_async_copy(give4.at[azimuth], out.at[azimuth], own_sem)
    own.start()
    for final in finals:
        final.wait()
    for side in range(2):
        row_copy(side).wait_send()
        col_wait(side, inner_edge if side == 0 else outer_edge, csend)
    leave(src, send1)
    leave(give2, send2)
    leave(give3, send3)
    for part in range(4):
        arrive(out, recv4, step1, part)
    leave(give4, send4)
    own.wait()


def fused_step(shift, fields, tables, nx, ny, gx, gy, ident):
    height, width = fields[0].shape
    packed = height // 2
    count = gx * gy
    lines = ny // 2 // count
    padded = lines + 8
    f32 = jnp.float32
    blocks = (gy, packed, LANES)
    sems = [pltpu.SemaphoreType.DMA((2,))] * 4
    for parts in (4, lines // 8, lines // 8, 4):
        sems += [pltpu.SemaphoreType.DMA, pltpu.SemaphoreType.DMA((parts,))]
    shape = jax.ShapeDtypeStruct((height, width), f32)
    return pl.pallas_call(
        functools.partial(fused_kernel, nx, ny),
        out_shape=(shape, shape, shape, jax.ShapeDtypeStruct(blocks, f32)),
        in_specs=[HBM] * 7,
        out_specs=(HBM,) * 4,
        scratch_shapes=[pltpu.SMEM((1,), jnp.int32)]
        + [pltpu.VMEM((height, width), f32)] * 6
        + [pltpu.VMEM(table.shape, table.dtype) for table in tables]
        + [
            pltpu.SemaphoreType.DMA,
            pltpu.SemaphoreType.DMA((3,)),
            pltpu.SemaphoreType.DMA((3,)),
            pltpu.SemaphoreType.DMA((3,)),
            pltpu.SemaphoreType.DMA,
            pltpu.VMEM((2, gy, 8, height), f32),
            pltpu.VMEM((2, 8, width), f32),
            pltpu.VMEM((2, 8, height), f32),
            pltpu.VMEM((height, 16), f32),
            pltpu.VMEM((2, 8, width), f32),
            pltpu.VMEM((2, padded, LANES), f32),
            pltpu.VMEM((2, padded, LANES), f32),
            pltpu.VMEM(blocks, f32),
            pltpu.VMEM(blocks, f32),
            pltpu.VMEM((gy // 2, 2 * height, LANES), f32),
            pltpu.VMEM((count, lines, LANES), f32),
            pltpu.VMEM((count, lines, LANES), f32),
            pltpu.VMEM((count, padded, LANES), f32),
            pltpu.VMEM((count, 8, LANES), f32),
            pltpu.VMEM((count, 8, LANES), f32),
            pltpu.VMEM((count, lines, LANES), f32),
            pltpu.VMEM((count, lines, LANES), f32),
            pltpu.VMEM(blocks, f32),
        ]
        + sems,
        compiler_params=pltpu.CompilerParams(collective_id=ident, has_side_effects=True),
    )(shift, *fields, *tables)


def shards(density, xmomentum, ymomentum, shear_shift):
    gx, gy = lax.axis_size("gx"), lax.axis_size("gy")
    here_x, here_y = lax.axis_index("gx"), lax.axis_index("gy")
    height, width = density.shape[1:]
    nx, ny = width * gx, height * gy
    count = gx * gy
    xb = width // gy
    lines = ny // 2 // count
    shift = shear_shift[0]
    fields = [density[0], xmomentum[0], ymomentum[0]]

    fold = LANES // xb
    packed = height // fold
    wide = LANES // 2
    outer = nx // wide
    group = wide // xb
    y_table = jnp.asarray(azimuth_table(gy, height))
    turn, table = radial_tables(nx)
    turn, table = jnp.asarray(turn), jnp.asarray(table)
    if group == 1 and packed % 32 == 0 and lines % 8 == 0 and height % lines == 0:
        results = fused_step(shear_shift, fields, (y_table, turn, table), nx, ny, gx, gy, 1)
        return tuple(r[None] for r in unpack(results[:3], results[3]))

    cols, rows = halo(fields, gx, gy, 0)
    cols = jnp.transpose(cols, (0, 2, 1, 3)).reshape(2, 8, ny)
    cols = jnp.concatenate([cols, cols], axis=2)
    start_left = (here_y * height + jnp.where(here_x == 0, shift, 0)) % ny
    start_right = (here_y * height - jnp.where(here_x == gx - 1, shift, 0)) % ny
    ghost = jnp.stack(
        [
            lax.dynamic_slice_in_dim(cols[0], start_left, height, 1),
            lax.dynamic_slice_in_dim(cols[1], start_right, height, 1),
        ]
    )
    density_new, xmomentum_new, ymomentum_new = gas(fields, rows, ghost)
    padded = (lines + 8) // 8 * 8
    row = jnp.arange(padded, dtype=jnp.int32)
    slot = (here_x * gy + here_y) * lines + row
    wave = slot_wave(slot // height, slot % height, gy, height)
    wave = jnp.where(row == lines, ny // 2, jnp.where(row > lines, 1, wave))
    sigma = wave * shift % ny
    unit = 2.0 * jnp.pi / (nx * ny)

    def phases(points):
        angle = (sigma[:, None] * points[None, :] % (nx * ny)).astype(jnp.float32) * unit
        return jnp.stack([jnp.cos(angle), jnp.sin(angle)])

    lane = jnp.arange(LANES, dtype=jnp.int32)
    outer_turn = phases(jnp.where(lane < outer, lane, 0) * wide)
    inner_turn = phases(lane % wide)
    full = (padded, LANES)
    line_tables = (
        jnp.broadcast_to(wave[:, None], full),
        jnp.broadcast_to(sigma[:, None], full),
        outer_turn,
        inner_turn,
        turn,
        table,
    )

    blocks = jnp.transpose(density_new.reshape(fold, packed, gy, xb), (2, 1, 0, 3))
    blocks = exchange(blocks.reshape(gy, packed, LANES), gy, False, 1)
    slots = azimuth_forward(blocks, y_table, xb)
    slots = slots[:, :, : 2 * xb].reshape(count, lines, 2 * xb)
    slots = exchange(slots, gy, True, 2)
    if group > 1:
        slots = slots.reshape(outer, group, lines, 2, xb)
        slots = jnp.transpose(slots, (0, 2, 3, 1, 4)).reshape(outer, lines, LANES)
    solved = radial(slots, *line_tables, nx, ny)
    if group > 1:
        solved = solved.reshape(outer, lines, 2, group, xb)
        solved = jnp.transpose(solved, (0, 3, 1, 2, 4)).reshape(count, lines, 2 * xb)
    solved = exchange(solved, gy, True, 3).reshape(gy // 2, height, 2 * xb)
    solved = jnp.pad(solved, ((0, 0), (0, 0), (0, LANES - 2 * xb)))
    lined = azimuth_back(solved, y_table, xb, gy, packed)
    lined = exchange(lined, gy, False, 4)
    potential = jnp.transpose(lined.reshape(gy, packed, fold, xb), (2, 1, 0, 3))
    potential = potential.reshape(height, width)
    return (density_new[None], xmomentum_new[None], ymomentum_new[None], potential[None])


def solution(mesh):
    split_spec = P(None, "gy", "gx")
    return jax.shard_map(
        shards,
        mesh=mesh,
        in_specs=(split_spec, split_spec, split_spec, P()),
        out_specs=(split_spec,) * 4,
        check_vma=False,
    )
```

```python
import functools

import jax
import jax.numpy as jnp
import ml_dtypes
import numpy as np
from jax import lax
from jax.experimental import pallas as pl
from jax.experimental.pallas import tpu as pltpu
from jax.sharding import PartitionSpec as P

sound_speed = 1.0
time_step = 0.15
omega_rate = 0.5
shear_rate = 1.5
thickness = 0.5

LANES = 128
MESH = pl.DeviceIdType.MESH
VMEM = pl.BlockSpec(memory_space=pltpu.VMEM)
HBM = pl.BlockSpec(memory_space=pl.ANY)


def split_np(table):
    head = table.astype(np.float32).astype(ml_dtypes.bfloat16)
    tail = (table - head.astype(np.float64)).astype(np.float32).astype(ml_dtypes.bfloat16)
    return np.stack([head, tail])


def split(value):
    head = value.astype(jnp.bfloat16)
    return head, (value - head.astype(jnp.float32)).astype(jnp.bfloat16)


def dot3(left, right, dims):
    def one(a, b):
        return lax.dot_general(a, b, (dims, ((), ())), preferred_element_type=jnp.float32)

    return one(left[0], right[0]) + (one(left[0], right[1]) + one(left[1], right[0]))


def exchange_kernel(count, gy, whole, src, dst, send, recv, own):
    radial = lax.axis_index("gx")
    azimuth = lax.axis_index("gy")
    me = radial * gy + azimuth if whole else azimuth

    def place(step):
        peer = lax.rem(me + step, count)
        device = (lax.div(peer, gy), lax.rem(peer, gy)) if whole else (radial, peer)
        return peer, device

    barrier = pltpu.get_barrier_semaphore()

    def greet(step, _):
        pl.semaphore_signal(barrier, inc=1, device_id=place(step)[1], device_id_type=MESH)
        return _

    def copy(step):
        peer, device = place(step)
        return pltpu.make_async_remote_copy(
            src_ref=src.at[peer],
            dst_ref=dst.at[me],
            send_sem=send.at[step],
            recv_sem=recv.at[step],
            device_id=device,
            device_id_type=MESH,
        )

    def start(step, _):
        copy(step).start()
        return _

    def finish(step, _):
        copy(step).wait()
        return _

    lax.fori_loop(1, count, greet, 0)
    mine = pltpu.make_async_copy(src.at[me], dst.at[me], own)
    mine.start()
    pl.semaphore_wait(barrier, count - 1)
    lax.fori_loop(1, count, start, 0)
    mine.wait()
    lax.fori_loop(1, count, finish, 0)


def exchange(blocks, gy, whole, ident):
    count = blocks.shape[0]
    return pl.pallas_call(
        functools.partial(exchange_kernel, count, gy, whole),
        out_shape=jax.ShapeDtypeStruct(blocks.shape, blocks.dtype),
        in_specs=[VMEM],
        out_specs=VMEM,
        scratch_shapes=[
            pltpu.SemaphoreType.DMA((count,)),
            pltpu.SemaphoreType.DMA((count,)),
            pltpu.SemaphoreType.DMA,
        ],
        compiler_params=pltpu.CompilerParams(collective_id=ident, has_side_effects=True),
    )(blocks)


def halo_kernel(gx, gy, d_ref, x_ref, y_ref, cols, rows, colbuf, rowbuf, csend, crecv, rsend, rrecv):
    radial = lax.axis_index("gx")
    azimuth = lax.axis_index("gy")
    before = lax.rem(radial + gx - 1, gx)
    after = lax.rem(radial + 1, gx)
    below = lax.rem(azimuth + gy - 1, gy)
    above = lax.rem(azimuth + 1, gy)
    height, width = d_ref.shape
    barrier = pltpu.get_barrier_semaphore()

    def greet(step, _):
        there = lax.rem(azimuth + step, gy)
        pl.semaphore_signal(barrier, inc=1, device_id=(before, there), device_id_type=MESH)
        pl.semaphore_signal(barrier, inc=1, device_id=(after, there), device_id_type=MESH)
        return _

    lax.fori_loop(0, gy, greet, 0)
    pl.semaphore_signal(barrier, inc=1, device_id=(radial, below), device_id_type=MESH)
    pl.semaphore_signal(barrier, inc=1, device_id=(radial, above), device_id_type=MESH)
    rowbuf[...] = jnp.zeros_like(rowbuf)
    colbuf[...] = jnp.zeros_like(colbuf)
    for at, ref in enumerate((d_ref, x_ref, y_ref)):
        rowbuf[0, at : at + 1, :] = ref[0:1, :]
        rowbuf[1, at : at + 1, :] = ref[height - 1 : height, :]
        colbuf[0, at : at + 1, :] = ref[:, 0:LANES].T[0:1, :]
        colbuf[1, at : at + 1, :] = ref[:, width - LANES : width].T[LANES - 1 : LANES, :]
    pl.semaphore_wait(barrier, 2 * gy + 2)

    def row_copy(side):
        return pltpu.make_async_remote_copy(
            src_ref=rowbuf.at[side],
            dst_ref=rows.at[1 - side],
            send_sem=rsend.at[side],
            recv_sem=rrecv.at[side],
            device_id=(radial, below if side == 0 else above),
            device_id_type=MESH,
        )

    def col_copy(side, step):
        there = lax.rem(azimuth + step, gy)
        return pltpu.make_async_remote_copy(
            src_ref=colbuf.at[side],
            dst_ref=cols.at[1 - side, azimuth],
            send_sem=csend.at[side, step],
            recv_sem=crecv.at[side, step],
            device_id=(before if side == 0 else after, there),
            device_id_type=MESH,
        )

    def start(step, _):
        col_copy(0, step).start()
        col_copy(1, step).start()
        return _

    def finish(step, _):
        col_copy(0, step).wait()
        col_copy(1, step).wait()
        return _

    row_copy(0).start()
    row_copy(1).start()
    lax.fori_loop(0, gy, start, 0)
    row_copy(0).wait()
    row_copy(1).wait()
    lax.fori_loop(0, gy, finish, 0)


def halo(fields, gx, gy, ident):
    height, width = fields[0].shape
    return pl.pallas_call(
        functools.partial(halo_kernel, gx, gy),
        out_shape=(
            jax.ShapeDtypeStruct((2, gy, 8, height), jnp.float32),
            jax.ShapeDtypeStruct((2, 8, width), jnp.float32),
        ),
        in_specs=[VMEM] * 3,
        out_specs=(VMEM, VMEM),
        scratch_shapes=[
            pltpu.VMEM((2, 8, height), jnp.float32),
            pltpu.VMEM((2, 8, width), jnp.float32),
            pltpu.SemaphoreType.DMA((2, gy)),
            pltpu.SemaphoreType.DMA((2, gy)),
            pltpu.SemaphoreType.DMA((2,)),
            pltpu.SemaphoreType.DMA((2,)),
        ],
        compiler_params=pltpu.CompilerParams(collective_id=ident, has_side_effects=True),
    )(*fields)


def flux_of(state, normal):
    velocity = state[normal] / state[0]
    parts = [state[0] * velocity, state[1] * velocity, state[2] * velocity]
    parts[normal] = parts[normal] + sound_speed * sound_speed * state[0]
    return parts, jnp.abs(velocity)


def rusanov(left, right, left_flux, right_flux, left_speed, right_speed):
    speed = jnp.maximum(left_speed, right_speed) + sound_speed
    return [
        0.5 * (fl + fr) - 0.5 * speed * (r - l)
        for l, r, fl, fr in zip(left, right, left_flux, right_flux)
    ]


def mass_flux(low, high, low_momentum, high_momentum, low_speed, high_speed):
    speed = jnp.maximum(low_speed, high_speed) + sound_speed
    return 0.5 * (low_momentum + high_momentum) - 0.5 * speed * (high - low)


def gas_update(now, down, up, west, east):
    change = [None] * 3
    for low, high, normal in ((west, east, 1), (down, up, 2)):
        low_f, low_s = flux_of(low, normal)
        mid_f, mid_s = flux_of(now, normal)
        high_f, high_s = flux_of(high, normal)
        left = rusanov(low, now, low_f, mid_f, low_s, mid_s)
        right = rusanov(now, high, mid_f, high_f, mid_s, high_s)
        for f in range(3):
            term = right[f] - left[f]
            change[f] = term if change[f] is None else change[f] + term
    return (
        now[0] - time_step * change[0],
        now[1] - time_step * change[1] + time_step * 2.0 * omega_rate * now[2],
        now[2] - time_step * change[2] - time_step * (2.0 - shear_rate) * omega_rate * now[1],
    )


def gas_kernel(d_ref, x_ref, y_ref, rows, cols, d_out, x_out, y_out):
    height, width = d_ref.shape
    refs = (d_ref, x_ref, y_ref)
    blocks = height // 8
    ghost = cols[...]
    ghost = jnp.concatenate([ghost[0], ghost[1]], axis=0).T
    sub = lax.broadcasted_iota(jnp.int32, (8, width), 0)
    lane = lax.broadcasted_iota(jnp.int32, (8, width), 1)
    for block in range(blocks):
        at = block * 8
        now = [ref[at : at + 8, :] for ref in refs]
        sides = ghost[at : at + 8]
        down, up, west, east = [], [], [], []
        for f in range(3):
            edge = refs[f][at - 1 : at, :] if block else rows[0, f : f + 1, :]
            down.append(jnp.where(sub == 0, edge, pltpu.roll(now[f], 1, 0)))
            edge = refs[f][at + 8 : at + 9, :] if block < blocks - 1 else rows[1, f : f + 1, :]
            up.append(jnp.where(sub == 7, edge, pltpu.roll(now[f], 7, 0)))
            west.append(jnp.where(lane == 0, sides[:, f : f + 1], pltpu.roll(now[f], 1, 1)))
            east.append(
                jnp.where(lane == width - 1, sides[:, 8 + f : 9 + f], pltpu.roll(now[f], width - 1, 1))
            )
        fresh = gas_update(now, down, up, west, east)
        d_out[at : at + 8, :], x_out[at : at + 8, :], y_out[at : at + 8, :] = fresh


def gas(fields, rows, cols):
    shape = jax.ShapeDtypeStruct(fields[0].shape, jnp.float32)
    return pl.pallas_call(
        gas_kernel,
        out_shape=(shape, shape, shape),
        in_specs=[VMEM] * 5,
        out_specs=(VMEM, VMEM, VMEM),
    )(*fields, rows, cols)


def unpack_kernel(d_in, x_in, y_in, src_in, d_out, x_out, y_out, out, d, x, y, src, packed_out, get, put):
    gy, packed, _ = src.shape
    low = lax.broadcasted_iota(jnp.int32, (packed, LANES), 1) < LANES // 2
    sources, buffers, targets = (src_in, d_in, x_in, y_in), (src, d, x, y), (out, d_out, x_out, y_out)
    gets = [pltpu.make_async_copy(a, b, get.at[f]) for f, (a, b) in enumerate(zip(sources, buffers))]
    puts = [
        pltpu.make_async_copy(a, b, put.at[f])
        for f, (a, b) in enumerate(zip((packed_out,) + buffers[1:], targets))
    ]
    for copy in gets:
        copy.start()
    gets[0].wait()
    for tile in range(gy // 2):
        span = slice(tile * LANES, (tile + 1) * LANES)
        near, far = src[2 * tile], src[2 * tile + 1]
        packed_out[0:packed, span] = jnp.where(low, near, flip(far))
        packed_out[packed : 2 * packed, span] = jnp.where(low, flip(near), far)
    puts[0].start()
    for f in range(1, 4):
        gets[f].wait()
        puts[f].start()
    for copy in puts:
        copy.wait()


def unpack(fields, blocks):
    shape = jax.ShapeDtypeStruct(fields[0].shape, jnp.float32)
    return pl.pallas_call(
        unpack_kernel,
        out_shape=(shape,) * 4,
        in_specs=[HBM] * 4,
        out_specs=(HBM,) * 4,
        scratch_shapes=[pltpu.VMEM(fields[0].shape, jnp.float32)] * 3
        + [pltpu.VMEM(blocks.shape, jnp.float32), pltpu.VMEM(fields[0].shape, jnp.float32)]
        + [pltpu.SemaphoreType.DMA((4,))] * 2,
    )(*fields, blocks)


def slot_wave(group, index, gy, height):
    half = height // 2
    first = jnp.where(index < half, gy * index, gy // 2 + gy * (index - half))
    return jnp.where(group == 0, first, group + gy * index)


def azimuth_table(gy, height):
    ny = gy * height
    b = np.arange(height)
    out = np.zeros((gy // 2, 2 * height, 2 * height))
    for group in range(1, gy // 2):
        m = group + gy * np.arange(height)
        angle = 2.0 * np.pi * ((m[:, None] * b[None, :]) % ny) / ny
        c, s = np.cos(angle), np.sin(angle)
        out[group] = np.block([[c, s], [-s, c]])
    half = height // 2
    for part, residue in enumerate((0, gy // 2)):
        m = residue + gy * np.arange(half)
        angle = 2.0 * np.pi * ((m[:, None] * b[None, :]) % ny) / ny
        c, s = np.cos(angle), -np.sin(angle)
        if part == 0:
            s[0] = 1.0 - 2.0 * (b % 2)
        out[0, part * half : (part + 1) * half, part * height : (part + 1) * height] = c
        out[0, height + part * half : height + (part + 1) * half, part * height : (part + 1) * height] = s
    return split_np(out)


def azimuth_kernel(xb, src, table, out, stage):
    gy, packed, _ = src.shape
    height = table.shape[2] // 2
    fold = height // packed
    lane = lax.broadcasted_iota(jnp.int32, (height, LANES), 1)
    half = gy // 2
    step = 8 if packed % 8 == 0 else packed

    def put(group, base, at, value):
        for h in range(fold):
            row = base + h * packed + at
            stage[group, row : row + step, :] = (
                value if h == 0 else pltpu.roll(value, LANES - h * xb, 1)
            )

    for at in range(0, packed, step):
        f = [src[a, at : at + step, :] for a in range(gy)]
        plus = [None] + [f[a] + f[gy - a] for a in range(1, half)]
        minus = [None] + [f[a] - f[gy - a] for a in range(1, half)]
        for g in range(half + 1):
            re = f[0] + f[half] if g % 2 == 0 else f[0] - f[half]
            im = None
            for a in range(1, half):
                re = re + float(np.cos(2.0 * np.pi * ((a * g) % gy) / gy)) * plus[a]
                if 0 < g < half:
                    term = float(-np.sin(2.0 * np.pi * ((a * g) % gy) / gy)) * minus[a]
                    im = term if im is None else im + term
            if g == half:
                put(0, height, at, re)
            else:
                put(g, 0, at, re)
                if g:
                    put(g, height, at, im)
    for g in range(half):
        both = dot3((table[0, g], table[1, g]), split(stage[g]), ((1,), (0,)))
        out[g] = jnp.where(lane < xb, both[:height], pltpu.roll(both[height:], xb, 1))


def azimuth_forward(blocks, table, xb):
    gy, packed, _ = blocks.shape
    height = table.shape[2] // 2
    return pl.pallas_call(
        functools.partial(azimuth_kernel, xb),
        out_shape=jax.ShapeDtypeStruct((gy // 2, height, LANES), jnp.float32),
        in_specs=[VMEM] * 2,
        out_specs=VMEM,
        scratch_shapes=[pltpu.VMEM((gy // 2, 2 * height, LANES), jnp.float32)],
    )(blocks, table)


def azimuth_back_kernel(xb, src, table, out, stage):
    gy, packed, _ = out.shape
    height = table.shape[2] // 2
    fold = height // packed
    half = gy // 2
    step = 8 if packed % 8 == 0 else packed
    lane = lax.broadcasted_iota(jnp.int32, (step, LANES), 1)
    for g in range(half):
        value = src[g]
        value = jnp.concatenate([value, pltpu.roll(value, LANES - xb, 1)], axis=0)
        stage[g] = dot3((table[0, g], table[1, g]), split(value), ((0,), (0,)))

    def take(group, base, at):
        total = None
        for h in range(fold):
            row = base + h * packed + at
            value = stage[group, row : row + step, :]
            value = value if h == 0 else pltpu.roll(value, h * xb, 1)
            total = value if h == 0 else jnp.where(lane < h * xb, total, value)
        return total

    for at in range(0, packed, step):
        re = [take(g, 0, at) for g in range(half)]
        im = [None] + [take(g, height, at) for g in range(1, half)]
        last = take(0, height, at)
        for a in range(half + 1):
            even = re[0] + last if a % 2 == 0 else re[0] - last
            odd = None
            for g in range(1, half):
                angle = 2.0 * np.pi * ((a * g) % gy) / gy
                even = even + float(np.cos(angle)) * re[g]
                if 0 < a < half:
                    term = float(np.sin(angle)) * im[g]
                    odd = term if odd is None else odd + term
            if odd is None:
                out[a, at : at + step, :] = even
            else:
                out[a, at : at + step, :] = even - odd
                out[gy - a, at : at + step, :] = even + odd


def azimuth_back(slots, table, xb, gy, packed):
    height = table.shape[2] // 2
    return pl.pallas_call(
        functools.partial(azimuth_back_kernel, xb),
        out_shape=jax.ShapeDtypeStruct((gy, packed, LANES), jnp.float32),
        in_specs=[VMEM] * 2,
        out_specs=VMEM,
        scratch_shapes=[pltpu.VMEM((gy // 2, 2 * height, LANES), jnp.float32)],
    )(slots, table)


def flip(value):
    return pltpu.roll(value, LANES // 2, value.ndim - 1)


def fft_packed(parts, sign, signs):
    count = len(parts)
    if count == 1:
        return parts
    even = fft_packed(parts[0::2], sign, signs)
    odd = fft_packed(parts[1::2], sign, signs)
    low, high = [], []
    for k in range(count // 2):
        value = odd[k]
        if k:
            angle = sign * 2.0 * np.pi * k / count
            turned = flip(value) * signs
            if 4 * k == count:
                value = turned * float(np.sin(angle))
            else:
                value = value * float(np.cos(angle)) + turned * float(np.sin(angle))
        low.append(even[k] + value)
        high.append(even[k] - value)
    return low + high


def radial_tables(nx):
    wide = LANES // 2
    outer = nx // wide
    j = np.arange(wide)
    angle = 2.0 * np.pi * (np.outer(np.arange(outer), j) % nx) / nx
    c, s = np.cos(angle), np.sin(angle)
    turn = np.stack([np.concatenate([c, c], 1), np.concatenate([s, -s], 1)])
    angle = 2.0 * np.pi * (np.outer(j, j) % wide) / wide
    c, s = np.cos(angle), np.sin(angle)
    return turn.astype(np.float32), split_np(np.block([[c, -s], [s, c]]))


def radial_kernel(nx, ny, lines, src, wave, sigma, outer_turn, inner_turn, turn, table, out, stage):
    outer = src.shape[0]
    padded = stage.shape[1]
    half = LANES // 2
    gy = lax.axis_size("gy")
    first = jnp.logical_and(lax.axis_index("gx") == 0, lax.axis_index("gy") == 0)
    keep = jnp.where(first, 0.0, 1.0)
    lane8 = lax.broadcasted_iota(jnp.int32, (8, LANES), 1)
    sub8 = lax.broadcasted_iota(jnp.int32, (8, LANES), 0)
    signs = jnp.where(lane8 < half, -1.0, 1.0)
    low = lane8 < half

    def load(d, at):
        if at + 8 <= lines:
            value = src[d, at : at + 8, :]
            if at == 0:
                value = jnp.where(jnp.logical_and(sub8 == 0, lane8 >= half), value * keep, value)
            return value
        top = src[d, 0:1, :]
        extra = jnp.where(low[0:1], flip(jnp.broadcast_to(top, (8, LANES)))[0:1], 0.0)
        if at >= lines:
            return jnp.where(sub8 == 0, extra, 0.0)
        body = jnp.concatenate([src[d, at:lines, :], jnp.zeros((8 - lines + at, LANES), jnp.float32)], 0)
        if at == 0:
            body = jnp.where(jnp.logical_and(sub8 == 0, lane8 >= half), body * keep, body)
        return jnp.where(sub8 == lines - at, extra, body)

    def turned(value, c, s):
        return value * c + flip(value) * s

    for at in range(0, padded, 8):
        ci, si = inner_turn[0, at : at + 8, :], inner_turn[1, at : at + 8, :]
        parts = []
        for d in range(outer):
            co = outer_turn[0, at : at + 8, d : d + 1]
            so = outer_turn[1, at : at + 8, d : d + 1]
            parts.append(turned(load(d, at), co, -so * signs))
        parts = fft_packed(parts, -1.0, signs)
        for n in range(outer):
            value = turned(parts[n], ci, -si * signs)
            stage[n, at : at + 8, :] = turned(value, turn[0, n : n + 1, :], turn[1, n : n + 1, :])

    column = lax.broadcasted_iota(jnp.int32, (padded, LANES), 1)
    column = jnp.where(column < half, column, column - half)
    m = jnp.broadcast_to(wave[:, 0:1], (padded, LANES))
    shear = jnp.broadcast_to(sigma[:, 0:1], (padded, LANES)).astype(jnp.float32) / ny
    signed = jnp.where(m < ny // 2, m, m - ny).astype(jnp.float32)
    wave_y = 2.0 * jnp.pi / ny * signed
    wave_y = wave_y * wave_y
    weight = jnp.where(jnp.logical_or(m == 0, m == ny // 2), 1.0, 2.0) / (nx * ny)

    def convolve(n, _):
        modes = dot3(split(stage[n]), (table[0], table[1]), ((1,), (0,)))
        x_wave = n + outer * column
        x_signed = jnp.where(x_wave < nx // 2, x_wave, x_wave - nx).astype(jnp.float32)
        wave_x = 2.0 * jnp.pi / nx * (x_signed + shear)
        magnitude = jnp.sqrt(wave_x * wave_x + wave_y)
        anchor = jnp.logical_and(m == 0, x_wave == 0)
        safe = jnp.where(anchor, 1.0, magnitude)
        green = jnp.where(anchor, 0.0, -jnp.exp(-thickness * safe) / safe)
        modes = modes * (green * weight)
        stage[n] = dot3(split(modes), (table[0], table[1]), ((1,), (1,)))
        return _

    lax.fori_loop(0, outer, convolve, 0)

    for at in range(0, lines, 8):
        high = min(at + 8, lines)
        ci, si = inner_turn[0, at : at + 8, :], inner_turn[1, at : at + 8, :]
        more = lines - lines % 8
        parts = []
        for n in range(outer):
            value = turned(stage[n, at : at + 8, :], turn[0, n : n + 1, :], -turn[1, n : n + 1, :])
            parts.append(turned(value, ci, si * signs))
        parts = fft_packed(parts, 1.0, signs)
        if at == 0:
            ce, se = inner_turn[0, more : more + 8, :], inner_turn[1, more : more + 8, :]
            extras = []
            for n in range(outer):
                value = turned(stage[n, more : more + 8, :], turn[0, n : n + 1, :], -turn[1, n : n + 1, :])
                extras.append(turned(value, ce, se * signs))
            extras = fft_packed(extras, 1.0, signs)
        for d in range(outer):
            co = outer_turn[0, at : at + 8, d : d + 1]
            so = outer_turn[1, at : at + 8, d : d + 1]
            value = turned(parts[d], co, so * signs)
            if at == 0:
                co = outer_turn[0, more : more + 8, d : d + 1]
                so = outer_turn[1, more : more + 8, d : d + 1]
                extra = flip(turned(extras[d], co, so * signs))[lines % 8 : lines % 8 + 1]
                mask = jnp.logical_and(jnp.logical_and(sub8 == 0, lane8 >= half), first)
                value = jnp.where(mask, extra, value)
            out[d, at:high, :] = value[: high - at]


def radial(blocks, wave, sigma, outer_turn, inner_turn, turn, table, nx, ny):
    outer, lines, _ = blocks.shape
    padded = wave.shape[0]
    return pl.pallas_call(
        functools.partial(radial_kernel, nx, ny, lines),
        out_shape=jax.ShapeDtypeStruct(blocks.shape, jnp.float32),
        in_specs=[VMEM] * 7,
        out_specs=VMEM,
        scratch_shapes=[pltpu.VMEM((outer, padded, LANES), jnp.float32)],
    )(blocks, wave, sigma, outer_turn, inner_turn, turn, table)


def modulo(value, size):
    return value & (size - 1) if size & (size - 1) == 0 else lax.rem(value, size)


def fused_kernel(
    nx, ny, shift_in, d_in, x_in, y_in, y_table_in, turn_in, x_table_in, d_final, x_final, y_final, out,
    shift_ref, d_ref, x_ref, y_ref, d_out, x_out, y_out, y_table, turn, x_table,
    shift_sem, load_sem, table_sem, field_sem, own_sem,
    cols, rows, colbuf, colbuf2, rowbuf, outer_turn, inner_turn, src,
    got1, stage, give2, got2, green, mid, extra, give3, got3, give4,
    csend, crecv, rsend, rrecv, send1, recv1, send2, recv2, send3, recv3, send4, recv4,
):
    gx, gy = lax.axis_size("gx"), lax.axis_size("gy")
    radial_at, azimuth = lax.axis_index("gx"), lax.axis_index("gy")
    count = gx * gy
    me = radial_at * gy + azimuth
    height, width = d_ref.shape
    packed = src.shape[1]
    half_gy = gy // 2
    outer, lines, _ = got2.shape
    padded = inner_turn.shape[1]
    wide = LANES // 2
    step1 = packed // 4
    parts2 = lines // 8
    first = me == 0
    keep = jnp.where(first, 0.0, 1.0)
    lane8 = lax.broadcasted_iota(jnp.int32, (8, LANES), 1)
    sub8 = lax.broadcasted_iota(jnp.int32, (8, LANES), 0)
    signs = jnp.where(lane8 < wide, -1.0, 1.0)
    low = lane8 < wide
    fields = (d_ref, x_ref, y_ref)
    fresh = (d_out, x_out, y_out)
    before = lax.rem(radial_at + gx - 1, gx)
    after = lax.rem(radial_at + 1, gx)
    below = lax.rem(azimuth + gy - 1, gy)
    above = lax.rem(azimuth + 1, gy)
    inner_edge = radial_at == 0
    outer_edge = radial_at == gx - 1

    def device_of(peer):
        return lax.div(peer, gy), lax.rem(peer, gy)

    loads = [
        pltpu.make_async_copy(source, ref, load_sem.at[f])
        for f, (source, ref) in enumerate(zip((d_in, x_in, y_in), fields))
    ]
    shift_load = pltpu.make_async_copy(shift_in, shift_ref, shift_sem)
    table_loads = [
        pltpu.make_async_copy(source, ref, table_sem.at[f])
        for f, (source, ref) in enumerate(zip((y_table_in, turn_in, x_table_in), (y_table, turn, x_table)))
    ]
    cols[...] = jnp.zeros_like(cols)
    barrier = pltpu.get_barrier_semaphore()

    def greet(k, _):
        there = device_of(lax.rem(me + k, count))
        pl.semaphore_signal(barrier, inc=1, device_id=there, device_id_type=MESH)
        return _

    for load in loads:
        load.start()
    shift_load.start()
    lax.fori_loop(1, count, greet, 0)
    for load in table_loads:
        load.start()

    rowbuf[...] = jnp.zeros_like(rowbuf)
    colbuf[...] = jnp.zeros_like(colbuf)
    for load in loads:
        load.wait()
    for at, ref in enumerate(fields):
        rowbuf[0, at : at + 1, :] = ref[0:1, :]
        rowbuf[1, at : at + 1, :] = ref[height - 1 : height, :]
        colbuf[0, at : at + 1, :] = ref[:, 0:LANES].T[0:1, :]
        colbuf[1, at : at + 1, :] = ref[:, width - LANES : width].T[LANES - 1 : LANES, :]

    def row_copy(side):
        return pltpu.make_async_remote_copy(
            src_ref=rowbuf.at[side],
            dst_ref=rows.at[1 - side],
            send_sem=rsend.at[side],
            recv_sem=rrecv.at[side],
            device_id=(radial_at, below if side == 0 else above),
            device_id_type=MESH,
        )

    def col_copy(side, k):
        return pltpu.make_async_remote_copy(
            src_ref=colbuf.at[side],
            dst_ref=cols.at[1 - side, azimuth],
            send_sem=csend.at[side],
            recv_sem=crecv.at[side],
            device_id=(before if side == 0 else after, lax.rem(azimuth + k, gy)),
            device_id_type=MESH,
        )

    outgoing = (jnp.where(inner_edge, gy, 1), jnp.where(outer_edge, gy, 1))

    def col_start(side):
        def body(k, _):
            col_copy(side, k).start()
            return _

        lax.fori_loop(0, outgoing[side], body, 0)

    def col_wait(side, many, sem):
        @pl.when(many)
        def _all():
            pltpu.make_async_copy(cols.at[side], cols.at[side], sem.at[side]).wait()

        @pl.when(jnp.logical_not(many))
        def _one():
            pltpu.make_async_copy(cols.at[side, 0], cols.at[side, 0], sem.at[side]).wait()

    def line_copy(give, got, send, recv, rows, part, k):
        peer = lax.rem(azimuth + k, gy)
        span = pl.ds(pl.multiple_of(part * rows, rows), rows)
        return pltpu.make_async_remote_copy(
            src_ref=give.at[peer, span],
            dst_ref=got.at[azimuth, span],
            send_sem=send,
            recv_sem=recv.at[part],
            device_id=(radial_at, peer),
            device_id_type=MESH,
        )

    def all_copy(give, got, send, recv, rows, part, k):
        peer = lax.rem(me + k, count)
        span = pl.ds(pl.multiple_of(part * rows, rows), rows)
        return pltpu.make_async_remote_copy(
            src_ref=give.at[peer, span],
            dst_ref=got.at[me, span],
            send_sem=send,
            recv_sem=recv.at[part],
            device_id=device_of(peer),
            device_id_type=MESH,
        )

    def each(copy, peers):
        def body(k, _):
            copy(k).start()
            return _

        lax.fori_loop(peers // 2, peers, body, 0)
        lax.fori_loop(1, peers // 2, body, 0)

    def arrive(got, recv, rows, part):
        span = pl.ds(pl.multiple_of(part * rows, rows), rows)
        whole = got.at[pl.ds(0, got.shape[0] - 1), span]
        pltpu.make_async_copy(whole, whole, recv.at[part]).wait()

    def leave(give, send):
        whole = give.at[pl.ds(0, give.shape[0] - 1)]
        pltpu.make_async_copy(whole, whole, send).wait()

    one = functools.partial(line_copy, src, got1, send1, recv1, step1)
    two = functools.partial(all_copy, give2, got2, send2, recv2, 8)
    three = functools.partial(all_copy, give3, got3, send3, recv3, 8)
    four = functools.partial(line_copy, give4, out, send4, recv4, step1)

    pl.semaphore_wait(barrier, count - 1)
    for side in range(2):
        row_copy(side).start()
        col_start(side)

    blocks = height // 8
    sub_wide = lax.broadcasted_iota(jnp.int32, (8, width), 0)
    lane_wide = lax.broadcasted_iota(jnp.int32, (8, width), 1)

    def density_rows(span, edge_down, edge_up):
        now = [ref[span, :] for ref in fields]
        rho, along, across = now
        speed = jnp.abs(along / rho)
        west = mass_flux(
            pltpu.roll(rho, 1, 1), rho, pltpu.roll(along, 1, 1), along, pltpu.roll(speed, 1, 1), speed
        )
        west = jnp.where(lane_wide == 0, 0.0, west)
        change = pltpu.roll(west, width - 1, 1) - west
        down = [
            jnp.where(sub_wide == 0, edge_down[f], pltpu.roll(now[f], 1, 0)) for f in (0, 2)
        ]
        up = [jnp.where(sub_wide == 7, edge_up[f], pltpu.roll(now[f], 7, 0)) for f in (0, 2)]
        speed = jnp.abs(across / rho)
        low_speed, high_speed = jnp.abs(down[1] / down[0]), jnp.abs(up[1] / up[0])
        change = change + (
            mass_flux(rho, up[0], across, up[1], speed, high_speed)
            - mass_flux(down[0], rho, down[1], across, low_speed, speed)
        )
        d_out[span, :] = rho - time_step * change

    def density_inner(block, _):
        span = pl.ds(pl.multiple_of(block * 8, 8), 8)
        span_down = pl.ds(pl.multiple_of(block * 8 - 8, 8), 8)
        span_up = pl.ds(pl.multiple_of(block * 8 + 8, 8), 8)
        density_rows(
            span,
            [pltpu.roll(ref[span_down, :], 1, 0) for ref in fields],
            [pltpu.roll(ref[span_up, :], 7, 0) for ref in fields],
        )
        return _

    lax.fori_loop(1, blocks - 1, density_inner, 0)
    shift_load.wait()

    column = lax.broadcasted_iota(jnp.int32, (padded, LANES), 1)
    row = lax.broadcasted_iota(jnp.int32, (padded, LANES), 0)
    group = lax.div(me * lines, height)
    index = lax.rem(me * lines, height) + row
    half = height // 2
    at_zero = jnp.where(index < half, gy * index, gy // 2 + gy * (index - half))
    m = jnp.where(group == 0, at_zero, group + gy * index)
    m = jnp.where(row == lines, ny // 2, jnp.where(row > lines, 1, m))
    shift = shift_ref[0]
    sigma = modulo(m * shift, ny)
    column = jnp.where(column < wide, column, column - wide)
    unit = 2.0 * jnp.pi / (nx * ny)
    points = (column * wide, column)
    for turns, point in zip((outer_turn, inner_turn), points):
        angle = modulo(sigma * point, nx * ny).astype(jnp.float32) * unit
        turns[0] = jnp.cos(angle)
        turns[1] = jnp.sin(angle)
    shear = sigma.astype(jnp.float32) / ny
    signed = jnp.where(m < ny // 2, m, m - ny).astype(jnp.float32)
    wave_y = 2.0 * jnp.pi / ny * signed
    wave_y = wave_y * wave_y
    weight = jnp.where(jnp.logical_or(m == 0, m == ny // 2), 1.0, 2.0) / (nx * ny)

    def fill(n, _):
        x_wave = n + outer * column
        x_signed = jnp.where(x_wave < nx // 2, x_wave, x_wave - nx).astype(jnp.float32)
        wave_x = 2.0 * jnp.pi / nx * (x_signed + shear)
        magnitude = jnp.sqrt(wave_x * wave_x + wave_y)
        anchor = jnp.logical_and(m == 0, x_wave == 0)
        safe = jnp.where(anchor, 1.0, magnitude)
        green[n] = jnp.where(anchor, 0.0, -jnp.exp(-thickness * safe) / safe) * weight
        return _

    for side in range(2):
        row_copy(side).wait_recv()
    for block in (0, blocks - 1):
        at = block * 8
        edge_down = [ref[at - 1 : at, :] if block else rows[0, f : f + 1, :] for f, ref in enumerate(fields)]
        edge_up = [ref[at + 8 : at + 9, :] if block == 0 else rows[1, f : f + 1, :] for f, ref in enumerate(fields)]
        density_rows(slice(at, at + 8), edge_down, edge_up)
    def pack(peer, at):
        span = slice(peer // 2 * LANES, (peer // 2 + 1) * LANES)
        near = d_out[at : at + 8, span]
        far = d_out[at + packed : at + packed + 8, span]
        src[peer, at : at + 8, :] = jnp.where(low, flip(near) if peer % 2 else near, far if peer % 2 else flip(far))

    ends = (0, gy - 1)
    for part in range(4):
        for at in range(part * step1, (part + 1) * step1, 8):
            for peer in range(1, gy - 1):
                pack(peer, at)

        def send(k, _):
            peer = lax.rem(azimuth + k, gy)

            @pl.when(jnp.logical_and(peer != ends[0], peer != ends[1]))
            def _middle():
                one(part, k).start()

            return _

        lax.fori_loop(gy // 2, gy, send, 0)
        lax.fori_loop(1, gy // 2, send, 0)

    for side in range(2):
        col_wait(side, outer_edge if side == 0 else inner_edge, crecv)
    here = azimuth * height

    def slid(side, amount, wraps):
        line = jnp.concatenate([cols[side, a] for a in range(gy)], axis=1)
        line = pltpu.roll(line, amount, 1)[:, :height]
        return jnp.where(wraps, line, cols[side, azimuth])

    ghost = jnp.concatenate(
        [
            slid(0, lax.rem(2 * ny - here - shift, ny), inner_edge),
            slid(1, lax.rem(ny - here + shift, ny), outer_edge),
        ],
        axis=0,
    ).T
    colbuf2[...] = ghost
    lane_tile = lax.broadcasted_iota(jnp.int32, (height, LANES), 1)
    for end in range(2):
        span = slice(0, LANES) if end == 0 else slice(width - LANES, width)
        mine = (d_ref[:, span], x_ref[:, span])
        other = (ghost[:, 8 * end : 8 * end + 1], ghost[:, 8 * end + 1 : 8 * end + 2])
        low_cell, high_cell = (other, mine) if end == 0 else (mine, other)
        flux = mass_flux(
            low_cell[0], high_cell[0], low_cell[1], high_cell[1],
            jnp.abs(low_cell[1] / low_cell[0]), jnp.abs(high_cell[1] / high_cell[0]),
        )
        flux = jnp.where(lane_tile == (0 if end == 0 else LANES - 1), time_step * flux, 0.0)
        d_out[:, span] = d_out[:, span] + flux if end == 0 else d_out[:, span] - flux

    for at in range(0, packed, 8):
        for end in ends:
            pack(end, at)
    for end in ends:

        @pl.when(azimuth != end)
        def _end():
            for part in range(4):
                one(part, lax.rem(end - azimuth + gy, gy)).start()

    finals = [
        pltpu.make_async_copy(ref, final, field_sem.at[f])
        for f, (ref, final) in enumerate(zip(fresh, (d_final, x_final, y_final)))
    ]

    finals[0].start()
    got1[azimuth] = src[azimuth]

    def inner_rows(block, _):
        span = pl.ds(pl.multiple_of(block * 8, 8), 8)
        span_down = pl.ds(pl.multiple_of(block * 8 - 8, 8), 8)
        span_up = pl.ds(pl.multiple_of(block * 8 + 8, 8), 8)
        now = [ref[span, :] for ref in fields]
        down = [
            jnp.where(sub_wide == 0, pltpu.roll(ref[span_down, :], 1, 0), pltpu.roll(value, 1, 0))
            for ref, value in zip(fields, now)
        ]
        up = [
            jnp.where(sub_wide == 7, pltpu.roll(ref[span_up, :], 7, 0), pltpu.roll(value, 7, 0))
            for ref, value in zip(fields, now)
        ]
        west = [pltpu.roll(value, 1, 1) for value in now]
        east = [pltpu.roll(value, width - 1, 1) for value in now]
        for ref, value in zip(fresh[1:], gas_update(now, down, up, west, east)[1:]):
            ref[span, :] = value
        return _

    lax.fori_loop(1, blocks - 1, inner_rows, 0)

    for block in (0, blocks - 1):
        at = block * 8
        now = [ref[at : at + 8, :] for ref in fields]
        sides = colbuf2[at : at + 8]
        down, up, west, east = [], [], [], []
        for f in range(3):
            edge = fields[f][at - 1 : at, :] if block else rows[0, f : f + 1, :]
            down.append(jnp.where(sub_wide == 0, edge, pltpu.roll(now[f], 1, 0)))
            edge = fields[f][at + 8 : at + 9, :] if block == 0 else rows[1, f : f + 1, :]
            up.append(jnp.where(sub_wide == 7, edge, pltpu.roll(now[f], 7, 0)))
            west.append(jnp.where(lane_wide == 0, sides[:, f : f + 1], pltpu.roll(now[f], 1, 1)))
            edge = pltpu.roll(now[f], width - 1, 1)
            east.append(jnp.where(lane_wide == width - 1, sides[:, 8 + f : 9 + f], edge))
        for ref, value in zip(fresh[1:], gas_update(now, down, up, west, east)[1:]):
            ref[at : at + 8, :] = value
    sub2 = lax.broadcasted_iota(jnp.int32, (8, 2 * LANES), 0)
    lane2 = lax.broadcasted_iota(jnp.int32, (8, 2 * LANES), 1)

    def side_cells(block, _):
        span = pl.ds(pl.multiple_of(block * 8, 8), 8)
        span_down = pl.ds(pl.multiple_of(block * 8 - 8, 8), 8)
        span_up = pl.ds(pl.multiple_of(block * 8 + 8, 8), 8)
        sides = colbuf2[span, :]
        for end in range(2):
            start_lane = 0 if end == 0 else width - 2 * LANES
            window = slice(start_lane, start_lane + 2 * LANES)
            now, down, up, west, east = [], [], [], [], []
            for f, ref in enumerate(fields):
                value = ref[span, window]
                now.append(value)
                edge = pltpu.roll(ref[span_down, window], 1, 0)
                down.append(jnp.where(sub2 == 0, edge, pltpu.roll(value, 1, 0)))
                edge = pltpu.roll(ref[span_up, window], 7, 0)
                up.append(jnp.where(sub2 == 7, edge, pltpu.roll(value, 7, 0)))
                left = pltpu.roll(value, 1, 1)
                right = pltpu.roll(value, 2 * LANES - 1, 1)
                if end == 0:
                    left = jnp.where(lane2 == 0, sides[:, f : f + 1], left)
                else:
                    right = jnp.where(lane2 == 2 * LANES - 1, sides[:, 8 + f : 9 + f], right)
                west.append(left)
                east.append(right)
            target = slice(0, LANES) if end == 0 else slice(width - LANES, width)
            kept = slice(0, LANES) if end == 0 else slice(LANES, 2 * LANES)
            for ref, value in zip(fresh[1:], gas_update(now, down, up, west, east)[1:]):
                ref[span, target] = value[:, kept]
        return _

    lax.fori_loop(1, blocks - 1, side_cells, 0)

    for final in finals[1:]:
        final.start()
    lax.fori_loop(0, outer, fill, 0)
    for load in table_loads:
        load.wait()

    for part in range(4):
        arrive(got1, recv1, step1, part)
        for at in range(part * step1, (part + 1) * step1, 8):
            f = [got1[a, at : at + 8, :] for a in range(gy)]
            plus = [None] + [f[a] + f[gy - a] for a in range(1, half_gy)]
            minus = [None] + [f[a] - f[gy - a] for a in range(1, half_gy)]

            def put(group, base, value):
                stage[group, base + at : base + at + 8, :] = value
                stage[group, base + packed + at : base + packed + at + 8, :] = flip(value)

            for g in range(half_gy + 1):
                re = f[0] + f[half_gy] if g % 2 == 0 else f[0] - f[half_gy]
                im = None
                for a in range(1, half_gy):
                    angle = 2.0 * np.pi * ((a * g) % gy) / gy
                    re = re + float(np.cos(angle)) * plus[a]
                    if 0 < g < half_gy:
                        term = float(-np.sin(angle)) * minus[a]
                        im = term if im is None else im + term
                if g == half_gy:
                    put(0, height, re)
                else:
                    put(g, 0, re)
                    if g:
                        put(g, height, im)
    lane = lax.broadcasted_iota(jnp.int32, (height, LANES), 1)
    ratio = height // lines
    for g in range(half_gy):
        both = dot3((y_table[0, g], y_table[1, g]), split(stage[g]), ((1,), (0,)))
        value = jnp.where(lane < wide, both[:height], flip(both[height:]))
        for q in range(ratio):
            give2[g * ratio + q] = value[q * lines : (q + 1) * lines]
    for part in range(parts2):
        each(functools.partial(two, part), count)
    got2[me] = give2[me]

    def turned(value, c, s):
        return value * c + flip(value) * s

    def solve(load, rows, store):
        ci, si = inner_turn[0, rows, :], inner_turn[1, rows, :] * signs
        co, so = outer_turn[0, rows, :], outer_turn[1, rows, :]
        parts = [turned(load(d), co[:, d : d + 1], -so[:, d : d + 1] * signs) for d in range(outer)]
        parts = fft_packed(parts, -1.0, signs)
        for n in range(outer):
            value = turned(parts[n], ci, -si)
            mid[n] = turned(value, turn[0, n : n + 1, :], turn[1, n : n + 1, :])
        modes = dot3(split(mid[...].reshape(outer * 8, LANES)), (x_table[0], x_table[1]), ((1,), (0,)))
        modes = modes * green[:, rows, :].reshape(outer * 8, LANES)
        modes = dot3(split(modes), (x_table[0], x_table[1]), ((1,), (1,)))
        mid[...] = modes.reshape(outer, 8, LANES)
        parts = []
        for n in range(outer):
            value = turned(mid[n], turn[0, n : n + 1, :], -turn[1, n : n + 1, :])
            parts.append(turned(value, ci, si))
        parts = fft_packed(parts, 1.0, signs)
        for d in range(outer):
            store(d, turned(parts[d], co[:, d : d + 1], so[:, d : d + 1] * signs))

    def load_extra(d):
        return jnp.where(jnp.logical_and(sub8 == 0, low), flip(got2[d, 0:8, :]), 0.0)

    def store_extra(d, value):
        extra[d] = flip(value)

    def chunk(part, _):
        arrive(got2, recv2, 8, part)
        rows = pl.ds(pl.multiple_of(part * 8, 8), 8)

        @pl.when(jnp.logical_and(part == 0, first))
        def _extra():
            solve(load_extra, pl.ds(lines, 8), store_extra)

        corner = jnp.logical_and(jnp.logical_and(sub8 == 0, lane8 >= wide), part == 0)
        damp = jnp.where(corner, keep, 1.0)
        mine = jnp.logical_and(corner, first)

        def load(d):
            return got2[d, rows, :] * damp

        def store(d, value):
            give3[d, rows, :] = jnp.where(mine, extra[d], value)

        solve(load, rows, store)
        each(functools.partial(three, part), count)
        return _

    lax.fori_loop(0, parts2, chunk, 0)
    got3[me] = give3[me]
    for part in range(parts2):
        arrive(got3, recv3, 8, part)

    for g in range(half_gy):
        value = got3[g * ratio : (g + 1) * ratio].reshape(height, LANES)
        value = jnp.concatenate([value, flip(value)], axis=0)
        stage[g] = dot3((y_table[0, g], y_table[1, g]), split(value), ((0,), (0,)))

    def take(group, base, at):
        near = stage[group, base + at : base + at + 8, :]
        far = stage[group, base + packed + at : base + packed + at + 8, :]
        return jnp.where(low, near, flip(far))

    for part in range(4):
        for at in range(part * step1, (part + 1) * step1, 8):
            re = [take(g, 0, at) for g in range(half_gy)]
            im = [None] + [take(g, height, at) for g in range(1, half_gy)]
            last = take(0, height, at)
            for a in range(half_gy + 1):
                even = re[0] + last if a % 2 == 0 else re[0] - last
                odd = None
                for g in range(1, half_gy):
                    angle = 2.0 * np.pi * ((a * g) % gy) / gy
                    even = even + float(np.cos(angle)) * re[g]
                    if 0 < a < half_gy:
                        term = float(np.sin(angle)) * im[g]
                        odd = term if odd is None else odd + term
                if odd is None:
                    give4[a, at : at + 8, :] = even
                else:
                    give4[a, at : at + 8, :] = even - odd
                    give4[gy - a, at : at + 8, :] = even + odd
        each(functools.partial(four, part), gy)
    own = pltpu.make_async_copy(give4.at[azimuth], out.at[azimuth], own_sem)
    own.start()
    for final in finals:
        final.wait()
    for side in range(2):
        row_copy(side).wait_send()
        col_wait(side, inner_edge if side == 0 else outer_edge, csend)
    leave(src, send1)
    leave(give2, send2)
    leave(give3, send3)
    for part in range(4):
        arrive(out, recv4, step1, part)
    leave(give4, send4)
    own.wait()


def fused_step(shift, fields, tables, nx, ny, gx, gy, ident):
    height, width = fields[0].shape
    packed = height // 2
    count = gx * gy
    lines = ny // 2 // count
    padded = lines + 8
    f32 = jnp.float32
    blocks = (gy, packed, LANES)
    sems = [pltpu.SemaphoreType.DMA((2,))] * 4
    for parts in (4, lines // 8, lines // 8, 4):
        sems += [pltpu.SemaphoreType.DMA, pltpu.SemaphoreType.DMA((parts,))]
    shape = jax.ShapeDtypeStruct((height, width), f32)
    return pl.pallas_call(
        functools.partial(fused_kernel, nx, ny),
        out_shape=(shape, shape, shape, jax.ShapeDtypeStruct(blocks, f32)),
        in_specs=[HBM] * 7,
        out_specs=(HBM,) * 4,
        scratch_shapes=[pltpu.SMEM((1,), jnp.int32)]
        + [pltpu.VMEM((height, width), f32)] * 6
        + [pltpu.VMEM(table.shape, table.dtype) for table in tables]
        + [
            pltpu.SemaphoreType.DMA,
            pltpu.SemaphoreType.DMA((3,)),
            pltpu.SemaphoreType.DMA((3,)),
            pltpu.SemaphoreType.DMA((3,)),
            pltpu.SemaphoreType.DMA,
            pltpu.VMEM((2, gy, 8, height), f32),
            pltpu.VMEM((2, 8, width), f32),
            pltpu.VMEM((2, 8, height), f32),
            pltpu.VMEM((height, 16), f32),
            pltpu.VMEM((2, 8, width), f32),
            pltpu.VMEM((2, padded, LANES), f32),
            pltpu.VMEM((2, padded, LANES), f32),
            pltpu.VMEM(blocks, f32),
            pltpu.VMEM(blocks, f32),
            pltpu.VMEM((gy // 2, 2 * height, LANES), f32),
            pltpu.VMEM((count, lines, LANES), f32),
            pltpu.VMEM((count, lines, LANES), f32),
            pltpu.VMEM((count, padded, LANES), f32),
            pltpu.VMEM((count, 8, LANES), f32),
            pltpu.VMEM((count, 8, LANES), f32),
            pltpu.VMEM((count, lines, LANES), f32),
            pltpu.VMEM((count, lines, LANES), f32),
            pltpu.VMEM(blocks, f32),
        ]
        + sems,
        compiler_params=pltpu.CompilerParams(collective_id=ident, has_side_effects=True),
    )(shift, *fields, *tables)


def shards(density, xmomentum, ymomentum, shear_shift):
    gx, gy = lax.axis_size("gx"), lax.axis_size("gy")
    here_x, here_y = lax.axis_index("gx"), lax.axis_index("gy")
    height, width = density.shape[1:]
    nx, ny = width * gx, height * gy
    count = gx * gy
    xb = width // gy
    lines = ny // 2 // count
    shift = shear_shift[0]
    fields = [density[0], xmomentum[0], ymomentum[0]]

    fold = LANES // xb
    packed = height // fold
    wide = LANES // 2
    outer = nx // wide
    group = wide // xb
    y_table = jnp.asarray(azimuth_table(gy, height))
    turn, table = radial_tables(nx)
    turn, table = jnp.asarray(turn), jnp.asarray(table)
    if group == 1 and packed % 32 == 0 and lines % 8 == 0 and height % lines == 0:
        results = fused_step(shear_shift, fields, (y_table, turn, table), nx, ny, gx, gy, 1)
        return tuple(r[None] for r in unpack(results[:3], results[3]))

    cols, rows = halo(fields, gx, gy, 0)
    cols = jnp.transpose(cols, (0, 2, 1, 3)).reshape(2, 8, ny)
    cols = jnp.concatenate([cols, cols], axis=2)
    start_left = (here_y * height + jnp.where(here_x == 0, shift, 0)) % ny
    start_right = (here_y * height - jnp.where(here_x == gx - 1, shift, 0)) % ny
    ghost = jnp.stack(
        [
            lax.dynamic_slice_in_dim(cols[0], start_left, height, 1),
            lax.dynamic_slice_in_dim(cols[1], start_right, height, 1),
        ]
    )
    density_new, xmomentum_new, ymomentum_new = gas(fields, rows, ghost)
    padded = (lines + 8) // 8 * 8
    row = jnp.arange(padded, dtype=jnp.int32)
    slot = (here_x * gy + here_y) * lines + row
    wave = slot_wave(slot // height, slot % height, gy, height)
    wave = jnp.where(row == lines, ny // 2, jnp.where(row > lines, 1, wave))
    sigma = wave * shift % ny
    unit = 2.0 * jnp.pi / (nx * ny)

    def phases(points):
        angle = (sigma[:, None] * points[None, :] % (nx * ny)).astype(jnp.float32) * unit
        return jnp.stack([jnp.cos(angle), jnp.sin(angle)])

    lane = jnp.arange(LANES, dtype=jnp.int32)
    outer_turn = phases(jnp.where(lane < outer, lane, 0) * wide)
    inner_turn = phases(lane % wide)
    full = (padded, LANES)
    line_tables = (
        jnp.broadcast_to(wave[:, None], full),
        jnp.broadcast_to(sigma[:, None], full),
        outer_turn,
        inner_turn,
        turn,
        table,
    )

    blocks = jnp.transpose(density_new.reshape(fold, packed, gy, xb), (2, 1, 0, 3))
    blocks = exchange(blocks.reshape(gy, packed, LANES), gy, False, 1)
    slots = azimuth_forward(blocks, y_table, xb)
    slots = slots[:, :, : 2 * xb].reshape(count, lines, 2 * xb)
    slots = exchange(slots, gy, True, 2)
    if group > 1:
        slots = slots.reshape(outer, group, lines, 2, xb)
        slots = jnp.transpose(slots, (0, 2, 3, 1, 4)).reshape(outer, lines, LANES)
    solved = radial(slots, *line_tables, nx, ny)
    if group > 1:
        solved = solved.reshape(outer, lines, 2, group, xb)
        solved = jnp.transpose(solved, (0, 3, 1, 2, 4)).reshape(count, lines, 2 * xb)
    solved = exchange(solved, gy, True, 3).reshape(gy // 2, height, 2 * xb)
    solved = jnp.pad(solved, ((0, 0), (0, 0), (0, LANES - 2 * xb)))
    lined = azimuth_back(solved, y_table, xb, gy, packed)
    lined = exchange(lined, gy, False, 4)
    potential = jnp.transpose(lined.reshape(gy, packed, fold, xb), (2, 1, 0, 3))
    potential = potential.reshape(height, width)
    return (density_new[None], xmomentum_new[None], ymomentum_new[None], potential[None])


def solution(mesh):
    split_spec = P(None, "gy", "gx")
    return jax.shard_map(
        shards,
        mesh=mesh,
        in_specs=(split_spec, split_spec, split_spec, P()),
        out_specs=(split_spec,) * 4,
        check_vma=False,
    )
```

```python
import functools

import jax
import jax.numpy as jnp
import ml_dtypes
import numpy as np
from jax import lax
from jax.experimental import pallas as pl
from jax.experimental.pallas import tpu as pltpu
from jax.sharding import PartitionSpec as P

sound_speed = 1.0
time_step = 0.15
omega_rate = 0.5
shear_rate = 1.5
thickness = 0.5

LANES = 128
MESH = pl.DeviceIdType.MESH
VMEM = pl.BlockSpec(memory_space=pltpu.VMEM)
HBM = pl.BlockSpec(memory_space=pl.ANY)


def split_np(table):
    head = table.astype(np.float32).astype(ml_dtypes.bfloat16)
    tail = (table - head.astype(np.float64)).astype(np.float32).astype(ml_dtypes.bfloat16)
    return np.stack([head, tail])


def split(value):
    head = value.astype(jnp.bfloat16)
    return head, (value - head.astype(jnp.float32)).astype(jnp.bfloat16)


def dot3(left, right, dims):
    def one(a, b):
        return lax.dot_general(a, b, (dims, ((), ())), preferred_element_type=jnp.float32)

    return one(left[0], right[0]) + (one(left[0], right[1]) + one(left[1], right[0]))


def dot_wide(table, value, dims):
    def one(a, b):
        return lax.dot_general(a, b, (dims, ((), ())), preferred_element_type=jnp.float32)

    head, tail = split(value)
    both = one(table[0], jnp.concatenate([head, tail], axis=1))
    return both[:, :LANES] + (both[:, LANES:] + one(table[1], head))


def dot_square(value, table):
    both = jnp.dot(jnp.concatenate(split(value), axis=1), table, preferred_element_type=jnp.float32)
    return both[:, :LANES] + both[:, LANES:]


def square_np(table):
    def one(head, tail):
        return np.block([[head, tail], [head, np.zeros_like(tail)]])

    return np.stack([one(table[0], table[1]), one(table[0].T, table[1].T)])


def exchange_kernel(count, gy, whole, src, dst, send, recv, own):
    radial = lax.axis_index("gx")
    azimuth = lax.axis_index("gy")
    me = radial * gy + azimuth if whole else azimuth

    def place(step):
        peer = lax.rem(me + step, count)
        device = (lax.div(peer, gy), lax.rem(peer, gy)) if whole else (radial, peer)
        return peer, device

    barrier = pltpu.get_barrier_semaphore()

    def greet(step, _):
        pl.semaphore_signal(barrier, inc=1, device_id=place(step)[1], device_id_type=MESH)
        return _

    def copy(step):
        peer, device = place(step)
        return pltpu.make_async_remote_copy(
            src_ref=src.at[peer],
            dst_ref=dst.at[me],
            send_sem=send.at[step],
            recv_sem=recv.at[step],
            device_id=device,
            device_id_type=MESH,
        )

    def start(step, _):
        copy(step).start()
        return _

    def finish(step, _):
        copy(step).wait()
        return _

    lax.fori_loop(1, count, greet, 0)
    mine = pltpu.make_async_copy(src.at[me], dst.at[me], own)
    mine.start()
    pl.semaphore_wait(barrier, count - 1)
    lax.fori_loop(1, count, start, 0)
    mine.wait()
    lax.fori_loop(1, count, finish, 0)


def exchange(blocks, gy, whole, ident):
    count = blocks.shape[0]
    return pl.pallas_call(
        functools.partial(exchange_kernel, count, gy, whole),
        out_shape=jax.ShapeDtypeStruct(blocks.shape, blocks.dtype),
        in_specs=[VMEM],
        out_specs=VMEM,
        scratch_shapes=[
            pltpu.SemaphoreType.DMA((count,)),
            pltpu.SemaphoreType.DMA((count,)),
            pltpu.SemaphoreType.DMA,
        ],
        compiler_params=pltpu.CompilerParams(collective_id=ident, has_side_effects=True),
    )(blocks)


def halo_kernel(gx, gy, d_ref, x_ref, y_ref, cols, rows, colbuf, rowbuf, csend, crecv, rsend, rrecv):
    radial = lax.axis_index("gx")
    azimuth = lax.axis_index("gy")
    before = lax.rem(radial + gx - 1, gx)
    after = lax.rem(radial + 1, gx)
    below = lax.rem(azimuth + gy - 1, gy)
    above = lax.rem(azimuth + 1, gy)
    height, width = d_ref.shape
    barrier = pltpu.get_barrier_semaphore()

    def greet(step, _):
        there = lax.rem(azimuth + step, gy)
        pl.semaphore_signal(barrier, inc=1, device_id=(before, there), device_id_type=MESH)
        pl.semaphore_signal(barrier, inc=1, device_id=(after, there), device_id_type=MESH)
        return _

    lax.fori_loop(0, gy, greet, 0)
    pl.semaphore_signal(barrier, inc=1, device_id=(radial, below), device_id_type=MESH)
    pl.semaphore_signal(barrier, inc=1, device_id=(radial, above), device_id_type=MESH)
    rowbuf[...] = jnp.zeros_like(rowbuf)
    colbuf[...] = jnp.zeros_like(colbuf)
    for at, ref in enumerate((d_ref, x_ref, y_ref)):
        rowbuf[0, at : at + 1, :] = ref[0:1, :]
        rowbuf[1, at : at + 1, :] = ref[height - 1 : height, :]
        colbuf[0, at : at + 1, :] = ref[:, 0:LANES].T[0:1, :]
        colbuf[1, at : at + 1, :] = ref[:, width - LANES : width].T[LANES - 1 : LANES, :]
    pl.semaphore_wait(barrier, 2 * gy + 2)

    def row_copy(side):
        return pltpu.make_async_remote_copy(
            src_ref=rowbuf.at[side],
            dst_ref=rows.at[1 - side],
            send_sem=rsend.at[side],
            recv_sem=rrecv.at[side],
            device_id=(radial, below if side == 0 else above),
            device_id_type=MESH,
        )

    def col_copy(side, step):
        there = lax.rem(azimuth + step, gy)
        return pltpu.make_async_remote_copy(
            src_ref=colbuf.at[side],
            dst_ref=cols.at[1 - side, azimuth],
            send_sem=csend.at[side, step],
            recv_sem=crecv.at[side, step],
            device_id=(before if side == 0 else after, there),
            device_id_type=MESH,
        )

    def start(step, _):
        col_copy(0, step).start()
        col_copy(1, step).start()
        return _

    def finish(step, _):
        col_copy(0, step).wait()
        col_copy(1, step).wait()
        return _

    row_copy(0).start()
    row_copy(1).start()
    lax.fori_loop(0, gy, start, 0)
    row_copy(0).wait()
    row_copy(1).wait()
    lax.fori_loop(0, gy, finish, 0)


def halo(fields, gx, gy, ident):
    height, width = fields[0].shape
    return pl.pallas_call(
        functools.partial(halo_kernel, gx, gy),
        out_shape=(
            jax.ShapeDtypeStruct((2, gy, 8, height), jnp.float32),
            jax.ShapeDtypeStruct((2, 8, width), jnp.float32),
        ),
        in_specs=[VMEM] * 3,
        out_specs=(VMEM, VMEM),
        scratch_shapes=[
            pltpu.VMEM((2, 8, height), jnp.float32),
            pltpu.VMEM((2, 8, width), jnp.float32),
            pltpu.SemaphoreType.DMA((2, gy)),
            pltpu.SemaphoreType.DMA((2, gy)),
            pltpu.SemaphoreType.DMA((2,)),
            pltpu.SemaphoreType.DMA((2,)),
        ],
        compiler_params=pltpu.CompilerParams(collective_id=ident, has_side_effects=True),
    )(*fields)


def flux_of(state, normal):
    velocity = state[normal] / state[0]
    parts = [state[0] * velocity, state[1] * velocity, state[2] * velocity]
    parts[normal] = parts[normal] + sound_speed * sound_speed * state[0]
    return parts, jnp.abs(velocity)


def rusanov(left, right, left_flux, right_flux, left_speed, right_speed):
    speed = jnp.maximum(left_speed, right_speed) + sound_speed
    return [
        0.5 * (fl + fr) - 0.5 * speed * (r - l)
        for l, r, fl, fr in zip(left, right, left_flux, right_flux)
    ]


def mass_flux(low, high, low_momentum, high_momentum, low_speed, high_speed):
    speed = jnp.maximum(low_speed, high_speed) + sound_speed
    return 0.5 * (low_momentum + high_momentum) - 0.5 * speed * (high - low)


def gas_update(now, down, up, west, east):
    change = [None] * 3
    for low, high, normal in ((west, east, 1), (down, up, 2)):
        low_f, low_s = flux_of(low, normal)
        mid_f, mid_s = flux_of(now, normal)
        high_f, high_s = flux_of(high, normal)
        left = rusanov(low, now, low_f, mid_f, low_s, mid_s)
        right = rusanov(now, high, mid_f, high_f, mid_s, high_s)
        for f in range(3):
            term = right[f] - left[f]
            change[f] = term if change[f] is None else change[f] + term
    return (
        now[0] - time_step * change[0],
        now[1] - time_step * change[1] + time_step * 2.0 * omega_rate * now[2],
        now[2] - time_step * change[2] - time_step * (2.0 - shear_rate) * omega_rate * now[1],
    )


def gas_kernel(d_ref, x_ref, y_ref, rows, cols, d_out, x_out, y_out):
    height, width = d_ref.shape
    refs = (d_ref, x_ref, y_ref)
    blocks = height // 8
    ghost = cols[...]
    ghost = jnp.concatenate([ghost[0], ghost[1]], axis=0).T
    sub = lax.broadcasted_iota(jnp.int32, (8, width), 0)
    lane = lax.broadcasted_iota(jnp.int32, (8, width), 1)
    for block in range(blocks):
        at = block * 8
        now = [ref[at : at + 8, :] for ref in refs]
        sides = ghost[at : at + 8]
        down, up, west, east = [], [], [], []
        for f in range(3):
            edge = refs[f][at - 1 : at, :] if block else rows[0, f : f + 1, :]
            down.append(jnp.where(sub == 0, edge, pltpu.roll(now[f], 1, 0)))
            edge = refs[f][at + 8 : at + 9, :] if block < blocks - 1 else rows[1, f : f + 1, :]
            up.append(jnp.where(sub == 7, edge, pltpu.roll(now[f], 7, 0)))
            west.append(jnp.where(lane == 0, sides[:, f : f + 1], pltpu.roll(now[f], 1, 1)))
            east.append(
                jnp.where(lane == width - 1, sides[:, 8 + f : 9 + f], pltpu.roll(now[f], width - 1, 1))
            )
        fresh = gas_update(now, down, up, west, east)
        d_out[at : at + 8, :], x_out[at : at + 8, :], y_out[at : at + 8, :] = fresh


def gas(fields, rows, cols):
    shape = jax.ShapeDtypeStruct(fields[0].shape, jnp.float32)
    return pl.pallas_call(
        gas_kernel,
        out_shape=(shape, shape, shape),
        in_specs=[VMEM] * 5,
        out_specs=(VMEM, VMEM, VMEM),
    )(*fields, rows, cols)


def unpack_kernel(d_in, x_in, y_in, src, d_out, x_out, y_out, out, packed_out, sem):
    gy, packed, _ = src.shape
    low = lax.broadcasted_iota(jnp.int32, (packed, LANES), 1) < LANES // 2
    copies = [
        pltpu.make_async_copy(source, target, sem.at[f])
        for f, (source, target) in enumerate(zip((d_in, x_in, y_in), (d_out, x_out, y_out)))
    ]
    copies.append(pltpu.make_async_copy(packed_out, out, sem.at[3]))
    for copy in copies[:3]:
        copy.start()
    for tile in range(gy // 2):
        span = slice(tile * LANES, (tile + 1) * LANES)
        near, far = src[2 * tile], src[2 * tile + 1]
        packed_out[0:packed, span] = jnp.where(low, near, flip(far))
        packed_out[packed : 2 * packed, span] = jnp.where(low, flip(near), far)
    copies[3].start()
    for copy in copies:
        copy.wait()


def unpack(fields, blocks):
    shape = jax.ShapeDtypeStruct(fields[0].shape, jnp.float32)
    return pl.pallas_call(
        unpack_kernel,
        out_shape=(shape,) * 4,
        in_specs=[HBM] * 3 + [VMEM],
        out_specs=(HBM,) * 4,
        scratch_shapes=[pltpu.VMEM(fields[0].shape, jnp.float32), pltpu.SemaphoreType.DMA((4,))],
        compiler_params=pltpu.CompilerParams(vmem_limit_bytes=8 << 20),
    )(*fields, blocks)


def slot_wave(group, index, gy, height):
    half = height // 2
    first = jnp.where(index < half, gy * index, gy // 2 + gy * (index - half))
    return jnp.where(group == 0, first, group + gy * index)


def azimuth_table(gy, height):
    ny = gy * height
    b = np.arange(height)
    out = np.zeros((gy // 2, 2 * height, 2 * height))
    for group in range(1, gy // 2):
        m = group + gy * np.arange(height)
        angle = 2.0 * np.pi * ((m[:, None] * b[None, :]) % ny) / ny
        c, s = np.cos(angle), np.sin(angle)
        out[group] = np.block([[c, s], [-s, c]])
    half = height // 2
    for part, residue in enumerate((0, gy // 2)):
        m = residue + gy * np.arange(half)
        angle = 2.0 * np.pi * ((m[:, None] * b[None, :]) % ny) / ny
        c, s = np.cos(angle), -np.sin(angle)
        if part == 0:
            s[0] = 1.0 - 2.0 * (b % 2)
        out[0, part * half : (part + 1) * half, part * height : (part + 1) * height] = c
        out[0, height + part * half : height + (part + 1) * half, part * height : (part + 1) * height] = s
    return split_np(out)


def azimuth_kernel(xb, src, table, out, stage):
    gy, packed, _ = src.shape
    height = table.shape[2] // 2
    fold = height // packed
    lane = lax.broadcasted_iota(jnp.int32, (height, LANES), 1)
    half = gy // 2
    step = 8 if packed % 8 == 0 else packed

    def put(group, base, at, value):
        for h in range(fold):
            row = base + h * packed + at
            stage[group, row : row + step, :] = (
                value if h == 0 else pltpu.roll(value, LANES - h * xb, 1)
            )

    for at in range(0, packed, step):
        f = [src[a, at : at + step, :] for a in range(gy)]
        plus = [None] + [f[a] + f[gy - a] for a in range(1, half)]
        minus = [None] + [f[a] - f[gy - a] for a in range(1, half)]
        for g in range(half + 1):
            re = f[0] + f[half] if g % 2 == 0 else f[0] - f[half]
            im = None
            for a in range(1, half):
                re = re + float(np.cos(2.0 * np.pi * ((a * g) % gy) / gy)) * plus[a]
                if 0 < g < half:
                    term = float(-np.sin(2.0 * np.pi * ((a * g) % gy) / gy)) * minus[a]
                    im = term if im is None else im + term
            if g == half:
                put(0, height, at, re)
            else:
                put(g, 0, at, re)
                if g:
                    put(g, height, at, im)
    for g in range(half):
        both = dot3((table[0, g], table[1, g]), split(stage[g]), ((1,), (0,)))
        out[g] = jnp.where(lane < xb, both[:height], pltpu.roll(both[height:], xb, 1))


def azimuth_forward(blocks, table, xb):
    gy, packed, _ = blocks.shape
    height = table.shape[2] // 2
    return pl.pallas_call(
        functools.partial(azimuth_kernel, xb),
        out_shape=jax.ShapeDtypeStruct((gy // 2, height, LANES), jnp.float32),
        in_specs=[VMEM] * 2,
        out_specs=VMEM,
        scratch_shapes=[pltpu.VMEM((gy // 2, 2 * height, LANES), jnp.float32)],
    )(blocks, table)


def azimuth_back_kernel(xb, src, table, out, stage):
    gy, packed, _ = out.shape
    height = table.shape[2] // 2
    fold = height // packed
    half = gy // 2
    step = 8 if packed % 8 == 0 else packed
    lane = lax.broadcasted_iota(jnp.int32, (step, LANES), 1)
    for g in range(half):
        value = src[g]
        value = jnp.concatenate([value, pltpu.roll(value, LANES - xb, 1)], axis=0)
        stage[g] = dot3((table[0, g], table[1, g]), split(value), ((0,), (0,)))

    def take(group, base, at):
        total = None
        for h in range(fold):
            row = base + h * packed + at
            value = stage[group, row : row + step, :]
            value = value if h == 0 else pltpu.roll(value, h * xb, 1)
            total = value if h == 0 else jnp.where(lane < h * xb, total, value)
        return total

    for at in range(0, packed, step):
        re = [take(g, 0, at) for g in range(half)]
        im = [None] + [take(g, height, at) for g in range(1, half)]
        last = take(0, height, at)
        for a in range(half + 1):
            even = re[0] + last if a % 2 == 0 else re[0] - last
            odd = None
            for g in range(1, half):
                angle = 2.0 * np.pi * ((a * g) % gy) / gy
                even = even + float(np.cos(angle)) * re[g]
                if 0 < a < half:
                    term = float(np.sin(angle)) * im[g]
                    odd = term if odd is None else odd + term
            if odd is None:
                out[a, at : at + step, :] = even
            else:
                out[a, at : at + step, :] = even - odd
                out[gy - a, at : at + step, :] = even + odd


def azimuth_back(slots, table, xb, gy, packed):
    height = table.shape[2] // 2
    return pl.pallas_call(
        functools.partial(azimuth_back_kernel, xb),
        out_shape=jax.ShapeDtypeStruct((gy, packed, LANES), jnp.float32),
        in_specs=[VMEM] * 2,
        out_specs=VMEM,
        scratch_shapes=[pltpu.VMEM((gy // 2, 2 * height, LANES), jnp.float32)],
    )(slots, table)


def flip(value):
    return pltpu.roll(value, LANES // 2, value.ndim - 1)


def fft_packed(parts, sign, signs):
    count = len(parts)
    if count == 1:
        return parts
    even = fft_packed(parts[0::2], sign, signs)
    odd = fft_packed(parts[1::2], sign, signs)
    low, high = [], []
    for k in range(count // 2):
        value = odd[k]
        if k:
            angle = sign * 2.0 * np.pi * k / count
            turned = flip(value) * signs
            if 4 * k == count:
                value = turned * float(np.sin(angle))
            else:
                value = value * float(np.cos(angle)) + turned * float(np.sin(angle))
        low.append(even[k] + value)
        high.append(even[k] - value)
    return low + high


def radial_tables(nx):
    wide = LANES // 2
    outer = nx // wide
    j = np.arange(wide)
    angle = 2.0 * np.pi * (np.outer(np.arange(outer), j) % nx) / nx
    c, s = np.cos(angle), np.sin(angle)
    turn = np.stack([np.concatenate([c, c], 1), np.concatenate([s, -s], 1)])
    angle = 2.0 * np.pi * (np.outer(j, j) % wide) / wide
    c, s = np.cos(angle), np.sin(angle)
    return turn.astype(np.float32), split_np(np.block([[c, -s], [s, c]]))


def radial_kernel(nx, ny, lines, src, wave, sigma, outer_turn, inner_turn, turn, table, out, stage):
    outer = src.shape[0]
    padded = stage.shape[1]
    half = LANES // 2
    gy = lax.axis_size("gy")
    first = jnp.logical_and(lax.axis_index("gx") == 0, lax.axis_index("gy") == 0)
    keep = jnp.where(first, 0.0, 1.0)
    lane8 = lax.broadcasted_iota(jnp.int32, (8, LANES), 1)
    sub8 = lax.broadcasted_iota(jnp.int32, (8, LANES), 0)
    signs = jnp.where(lane8 < half, -1.0, 1.0)
    low = lane8 < half

    def load(d, at):
        if at + 8 <= lines:
            value = src[d, at : at + 8, :]
            if at == 0:
                value = jnp.where(jnp.logical_and(sub8 == 0, lane8 >= half), value * keep, value)
            return value
        top = src[d, 0:1, :]
        extra = jnp.where(low[0:1], flip(jnp.broadcast_to(top, (8, LANES)))[0:1], 0.0)
        if at >= lines:
            return jnp.where(sub8 == 0, extra, 0.0)
        body = jnp.concatenate([src[d, at:lines, :], jnp.zeros((8 - lines + at, LANES), jnp.float32)], 0)
        if at == 0:
            body = jnp.where(jnp.logical_and(sub8 == 0, lane8 >= half), body * keep, body)
        return jnp.where(sub8 == lines - at, extra, body)

    def turned(value, c, s):
        return value * c + flip(value) * s

    for at in range(0, padded, 8):
        ci, si = inner_turn[0, at : at + 8, :], inner_turn[1, at : at + 8, :]
        parts = []
        for d in range(outer):
            co = outer_turn[0, at : at + 8, d : d + 1]
            so = outer_turn[1, at : at + 8, d : d + 1]
            parts.append(turned(load(d, at), co, -so * signs))
        parts = fft_packed(parts, -1.0, signs)
        for n in range(outer):
            value = turned(parts[n], ci, -si * signs)
            stage[n, at : at + 8, :] = turned(value, turn[0, n : n + 1, :], turn[1, n : n + 1, :])

    column = lax.broadcasted_iota(jnp.int32, (padded, LANES), 1)
    column = jnp.where(column < half, column, column - half)
    m = jnp.broadcast_to(wave[:, 0:1], (padded, LANES))
    shear = jnp.broadcast_to(sigma[:, 0:1], (padded, LANES)).astype(jnp.float32) / ny
    signed = jnp.where(m < ny // 2, m, m - ny).astype(jnp.float32)
    wave_y = 2.0 * jnp.pi / ny * signed
    wave_y = wave_y * wave_y
    weight = jnp.where(jnp.logical_or(m == 0, m == ny // 2), 1.0, 2.0) / (nx * ny)

    def convolve(n, _):
        modes = dot3(split(stage[n]), (table[0], table[1]), ((1,), (0,)))
        x_wave = n + outer * column
        x_signed = jnp.where(x_wave < nx // 2, x_wave, x_wave - nx).astype(jnp.float32)
        wave_x = 2.0 * jnp.pi / nx * (x_signed + shear)
        magnitude = jnp.sqrt(wave_x * wave_x + wave_y)
        anchor = jnp.logical_and(m == 0, x_wave == 0)
        safe = jnp.where(anchor, 1.0, magnitude)
        green = jnp.where(anchor, 0.0, -jnp.exp(-thickness * safe) / safe)
        modes = modes * (green * weight)
        stage[n] = dot3(split(modes), (table[0], table[1]), ((1,), (1,)))
        return _

    lax.fori_loop(0, outer, convolve, 0)

    for at in range(0, lines, 8):
        high = min(at + 8, lines)
        ci, si = inner_turn[0, at : at + 8, :], inner_turn[1, at : at + 8, :]
        more = lines - lines % 8
        parts = []
        for n in range(outer):
            value = turned(stage[n, at : at + 8, :], turn[0, n : n + 1, :], -turn[1, n : n + 1, :])
            parts.append(turned(value, ci, si * signs))
        parts = fft_packed(parts, 1.0, signs)
        if at == 0:
            ce, se = inner_turn[0, more : more + 8, :], inner_turn[1, more : more + 8, :]
            extras = []
            for n in range(outer):
                value = turned(stage[n, more : more + 8, :], turn[0, n : n + 1, :], -turn[1, n : n + 1, :])
                extras.append(turned(value, ce, se * signs))
            extras = fft_packed(extras, 1.0, signs)
        for d in range(outer):
            co = outer_turn[0, at : at + 8, d : d + 1]
            so = outer_turn[1, at : at + 8, d : d + 1]
            value = turned(parts[d], co, so * signs)
            if at == 0:
                co = outer_turn[0, more : more + 8, d : d + 1]
                so = outer_turn[1, more : more + 8, d : d + 1]
                extra = flip(turned(extras[d], co, so * signs))[lines % 8 : lines % 8 + 1]
                mask = jnp.logical_and(jnp.logical_and(sub8 == 0, lane8 >= half), first)
                value = jnp.where(mask, extra, value)
            out[d, at:high, :] = value[: high - at]


def radial(blocks, wave, sigma, outer_turn, inner_turn, turn, table, nx, ny):
    outer, lines, _ = blocks.shape
    padded = wave.shape[0]
    return pl.pallas_call(
        functools.partial(radial_kernel, nx, ny, lines),
        out_shape=jax.ShapeDtypeStruct(blocks.shape, jnp.float32),
        in_specs=[VMEM] * 7,
        out_specs=VMEM,
        scratch_shapes=[pltpu.VMEM((outer, padded, LANES), jnp.float32)],
    )(blocks, wave, sigma, outer_turn, inner_turn, turn, table)


def modulo(value, size):
    return value & (size - 1) if size & (size - 1) == 0 else lax.rem(value, size)


def fused_kernel(
    nx, ny, shift_in, d_in, x_in, y_in, y_table_in, turn_in, x_table_in, d_final, x_final, y_final, out,
    shift_ref, d_ref, x_ref, y_ref, d_out, x_out, y_out, y_table, turn, x_table,
    shift_sem, load_sem, table_sem, field_sem, own_sem,
    cols, rows, colbuf, colbuf2, rowbuf, outer_turn, inner_turn, src,
    got1, stage, give2, got2, green, mid, extra, give3, got3, give4,
    csend, crecv, rsend, rrecv, send1, recv1, send2, recv2, send3, recv3, send4, recv4,
):
    gx, gy = lax.axis_size("gx"), lax.axis_size("gy")
    radial_at, azimuth = lax.axis_index("gx"), lax.axis_index("gy")
    count = gx * gy
    me = radial_at * gy + azimuth
    height, width = d_ref.shape
    packed = src.shape[1]
    half_gy = gy // 2
    outer, lines, _ = got2.shape
    padded = inner_turn.shape[1]
    wide = LANES // 2
    step1 = packed // 4
    parts2 = lines // 8
    first = me == 0
    keep = jnp.where(first, 0.0, 1.0)
    lane8 = lax.broadcasted_iota(jnp.int32, (8, LANES), 1)
    sub8 = lax.broadcasted_iota(jnp.int32, (8, LANES), 0)
    signs = jnp.where(lane8 < wide, -1.0, 1.0)
    low = lane8 < wide
    fields = (d_ref, x_ref, y_ref)
    fresh = (d_out, x_out, y_out)
    before = lax.rem(radial_at + gx - 1, gx)
    after = lax.rem(radial_at + 1, gx)
    below = lax.rem(azimuth + gy - 1, gy)
    above = lax.rem(azimuth + 1, gy)
    inner_edge = radial_at == 0
    outer_edge = radial_at == gx - 1

    def device_of(peer):
        return lax.div(peer, gy), lax.rem(peer, gy)

    loads = [
        pltpu.make_async_copy(source, ref, load_sem.at[f])
        for f, (source, ref) in enumerate(zip((d_in, x_in, y_in), fields))
    ]
    shift_load = pltpu.make_async_copy(shift_in, shift_ref, shift_sem)
    table_loads = [
        pltpu.make_async_copy(source, ref, table_sem.at[f])
        for f, (source, ref) in enumerate(zip((y_table_in, turn_in, x_table_in), (y_table, turn, x_table)))
    ]
    cols[...] = jnp.zeros_like(cols)
    barrier = pltpu.get_barrier_semaphore()

    def greet(k, _):
        there = device_of(lax.rem(me + k, count))
        pl.semaphore_signal(barrier, inc=1, device_id=there, device_id_type=MESH)
        return _

    for load in loads:
        load.start()
    shift_load.start()
    lax.fori_loop(1, count, greet, 0)
    for load in table_loads:
        load.start()

    rowbuf[...] = jnp.zeros_like(rowbuf)
    colbuf[...] = jnp.zeros_like(colbuf)
    for load in loads:
        load.wait()
    for at, ref in enumerate(fields):
        rowbuf[0, at : at + 1, :] = ref[0:1, :]
        rowbuf[1, at : at + 1, :] = ref[height - 1 : height, :]
        colbuf[0, at : at + 1, :] = ref[:, 0:LANES].T[0:1, :]
        colbuf[1, at : at + 1, :] = ref[:, width - LANES : width].T[LANES - 1 : LANES, :]

    def row_copy(side):
        return pltpu.make_async_remote_copy(
            src_ref=rowbuf.at[side],
            dst_ref=rows.at[1 - side],
            send_sem=rsend.at[side],
            recv_sem=rrecv.at[side],
            device_id=(radial_at, below if side == 0 else above),
            device_id_type=MESH,
        )

    def col_copy(side, k):
        return pltpu.make_async_remote_copy(
            src_ref=colbuf.at[side],
            dst_ref=cols.at[1 - side, azimuth],
            send_sem=csend.at[side],
            recv_sem=crecv.at[side],
            device_id=(before if side == 0 else after, lax.rem(azimuth + k, gy)),
            device_id_type=MESH,
        )

    outgoing = (jnp.where(inner_edge, gy, 1), jnp.where(outer_edge, gy, 1))

    def col_start(side):
        def body(k, _):
            col_copy(side, k).start()
            return _

        lax.fori_loop(0, outgoing[side], body, 0)

    def col_wait(side, many, sem):
        @pl.when(many)
        def _all():
            pltpu.make_async_copy(cols.at[side], cols.at[side], sem.at[side]).wait()

        @pl.when(jnp.logical_not(many))
        def _one():
            pltpu.make_async_copy(cols.at[side, 0], cols.at[side, 0], sem.at[side]).wait()

    def line_copy(give, got, send, recv, rows, part, k):
        peer = lax.rem(azimuth + k, gy)
        span = pl.ds(pl.multiple_of(part * rows, rows), rows)
        return pltpu.make_async_remote_copy(
            src_ref=give.at[peer, span],
            dst_ref=got.at[azimuth, span],
            send_sem=send,
            recv_sem=recv.at[part],
            device_id=(radial_at, peer),
            device_id_type=MESH,
        )

    def all_copy(give, got, send, recv, rows, part, k):
        peer = lax.rem(me + k, count)
        span = pl.ds(pl.multiple_of(part * rows, rows), rows)
        return pltpu.make_async_remote_copy(
            src_ref=give.at[peer, span],
            dst_ref=got.at[me, span],
            send_sem=send,
            recv_sem=recv.at[part],
            device_id=device_of(peer),
            device_id_type=MESH,
        )

    def each(copy, peers):
        def body(k, _):
            copy(k).start()
            return _

        lax.fori_loop(peers // 2, peers, body, 0)
        lax.fori_loop(1, peers // 2, body, 0)

    def arrive(got, recv, rows, part):
        span = pl.ds(pl.multiple_of(part * rows, rows), rows)
        whole = got.at[pl.ds(0, got.shape[0] - 1), span]
        pltpu.make_async_copy(whole, whole, recv.at[part]).wait()

    def leave(give, send):
        whole = give.at[pl.ds(0, give.shape[0] - 1)]
        pltpu.make_async_copy(whole, whole, send).wait()

    one = functools.partial(line_copy, src, got1, send1, recv1, step1)
    two = functools.partial(all_copy, give2, got2, send2, recv2, 8)
    three = functools.partial(all_copy, give3, got3, send3, recv3, 8)
    four = functools.partial(line_copy, give4, out, send4, recv4, step1)

    pl.semaphore_wait(barrier, count - 1)
    for side in range(2):
        row_copy(side).start()
        col_start(side)

    blocks = height // 8
    sub_wide = lax.broadcasted_iota(jnp.int32, (8, width), 0)
    lane_wide = lax.broadcasted_iota(jnp.int32, (8, width), 1)

    def density_rows(span, edge_down, edge_up):
        now = [ref[span, :] for ref in fields]
        rho, along, across = now
        speed = jnp.abs(along / rho)
        west = mass_flux(
            pltpu.roll(rho, 1, 1), rho, pltpu.roll(along, 1, 1), along, pltpu.roll(speed, 1, 1), speed
        )
        west = jnp.where(lane_wide == 0, 0.0, west)
        change = pltpu.roll(west, width - 1, 1) - west
        down = [
            jnp.where(sub_wide == 0, edge_down[f], pltpu.roll(now[f], 1, 0)) for f in (0, 2)
        ]
        up = [jnp.where(sub_wide == 7, edge_up[f], pltpu.roll(now[f], 7, 0)) for f in (0, 2)]
        speed = jnp.abs(across / rho)
        low_speed, high_speed = jnp.abs(down[1] / down[0]), jnp.abs(up[1] / up[0])
        change = change + (
            mass_flux(rho, up[0], across, up[1], speed, high_speed)
            - mass_flux(down[0], rho, down[1], across, low_speed, speed)
        )
        d_out[span, :] = rho - time_step * change

    def density_inner(block, _):
        span = pl.ds(pl.multiple_of(block * 8, 8), 8)
        span_down = pl.ds(pl.multiple_of(block * 8 - 8, 8), 8)
        span_up = pl.ds(pl.multiple_of(block * 8 + 8, 8), 8)
        density_rows(
            span,
            [pltpu.roll(ref[span_down, :], 1, 0) for ref in fields],
            [pltpu.roll(ref[span_up, :], 7, 0) for ref in fields],
        )
        return _

    lax.fori_loop(1, blocks - 1, density_inner, 0)
    shift_load.wait()

    column = lax.broadcasted_iota(jnp.int32, (padded, LANES), 1)
    row = lax.broadcasted_iota(jnp.int32, (padded, LANES), 0)
    group = lax.div(me * lines, height)
    index = lax.rem(me * lines, height) + row
    half = height // 2
    at_zero = jnp.where(index < half, gy * index, gy // 2 + gy * (index - half))
    m = jnp.where(group == 0, at_zero, group + gy * index)
    m = jnp.where(row == lines, ny // 2, jnp.where(row > lines, 1, m))
    shift = shift_ref[0]
    sigma = modulo(m * shift, ny)
    column = jnp.where(column < wide, column, column - wide)
    unit = 2.0 * jnp.pi / (nx * ny)
    points = (column * wide, column)
    for turns, point in zip((outer_turn, inner_turn), points):
        angle = modulo(sigma * point, nx * ny).astype(jnp.float32) * unit
        turns[0] = jnp.cos(angle)
        turns[1] = jnp.sin(angle)
    shear = sigma.astype(jnp.float32) / ny
    signed = jnp.where(m < ny // 2, m, m - ny).astype(jnp.float32)
    wave_y = 2.0 * jnp.pi / ny * signed
    wave_y = wave_y * wave_y
    weight = jnp.where(jnp.logical_or(m == 0, m == ny // 2), 1.0, 2.0) / (nx * ny)

    def fill(n, _):
        x_wave = n + outer * column
        x_signed = jnp.where(x_wave < nx // 2, x_wave, x_wave - nx).astype(jnp.float32)
        wave_x = 2.0 * jnp.pi / nx * (x_signed + shear)
        magnitude = jnp.sqrt(wave_x * wave_x + wave_y)
        anchor = jnp.logical_and(m == 0, x_wave == 0)
        safe = jnp.where(anchor, 1.0, magnitude)
        green[n] = jnp.where(anchor, 0.0, -jnp.exp(-thickness * safe) / safe) * weight
        return _

    for side in range(2):
        row_copy(side).wait_recv()
    for block in (0, blocks - 1):
        at = block * 8
        edge_down = [ref[at - 1 : at, :] if block else rows[0, f : f + 1, :] for f, ref in enumerate(fields)]
        edge_up = [ref[at + 8 : at + 9, :] if block == 0 else rows[1, f : f + 1, :] for f, ref in enumerate(fields)]
        density_rows(slice(at, at + 8), edge_down, edge_up)
    def pack(peer, at):
        span = slice(peer // 2 * LANES, (peer // 2 + 1) * LANES)
        near = d_out[at : at + 8, span]
        far = d_out[at + packed : at + packed + 8, span]
        src[peer, at : at + 8, :] = jnp.where(low, flip(near) if peer % 2 else near, far if peer % 2 else flip(far))

    ends = (0, gy - 1)
    for part in range(4):
        for at in range(part * step1, (part + 1) * step1, 8):
            for peer in range(1, gy - 1):
                pack(peer, at)

        def send(k, _):
            peer = lax.rem(azimuth + k, gy)

            @pl.when(jnp.logical_and(peer != ends[0], peer != ends[1]))
            def _middle():
                one(part, k).start()

            return _

        lax.fori_loop(gy // 2, gy, send, 0)
        lax.fori_loop(1, gy // 2, send, 0)

    for side in range(2):
        col_wait(side, outer_edge if side == 0 else inner_edge, crecv)
    here = azimuth * height

    def slid(side, amount, wraps):
        line = jnp.concatenate([cols[side, a] for a in range(gy)], axis=1)
        line = pltpu.roll(line, amount, 1)[:, :height]
        return jnp.where(wraps, line, cols[side, azimuth])

    ghost = jnp.concatenate(
        [
            slid(0, lax.rem(2 * ny - here - shift, ny), inner_edge),
            slid(1, lax.rem(ny - here + shift, ny), outer_edge),
        ],
        axis=0,
    ).T
    colbuf2[...] = ghost
    lane_tile = lax.broadcasted_iota(jnp.int32, (height, LANES), 1)
    for end in range(2):
        span = slice(0, LANES) if end == 0 else slice(width - LANES, width)
        mine = (d_ref[:, span], x_ref[:, span])
        other = (ghost[:, 8 * end : 8 * end + 1], ghost[:, 8 * end + 1 : 8 * end + 2])
        low_cell, high_cell = (other, mine) if end == 0 else (mine, other)
        flux = mass_flux(
            low_cell[0], high_cell[0], low_cell[1], high_cell[1],
            jnp.abs(low_cell[1] / low_cell[0]), jnp.abs(high_cell[1] / high_cell[0]),
        )
        flux = jnp.where(lane_tile == (0 if end == 0 else LANES - 1), time_step * flux, 0.0)
        d_out[:, span] = d_out[:, span] + flux if end == 0 else d_out[:, span] - flux

    for at in range(0, packed, 8):
        for end in ends:
            pack(end, at)
    for end in ends:

        @pl.when(azimuth != end)
        def _end():
            for part in range(4):
                one(part, lax.rem(end - azimuth + gy, gy)).start()

    finals = [
        pltpu.make_async_copy(ref, final, field_sem.at[f])
        for f, (ref, final) in enumerate(zip(fresh, (d_final, x_final, y_final)))
    ]

    finals[0].start()
    got1[azimuth] = src[azimuth]

    def inner_rows(block, _):
        span = pl.ds(pl.multiple_of(block * 8, 8), 8)
        span_down = pl.ds(pl.multiple_of(block * 8 - 8, 8), 8)
        span_up = pl.ds(pl.multiple_of(block * 8 + 8, 8), 8)
        now = [ref[span, :] for ref in fields]
        down = [
            jnp.where(sub_wide == 0, pltpu.roll(ref[span_down, :], 1, 0), pltpu.roll(value, 1, 0))
            for ref, value in zip(fields, now)
        ]
        up = [
            jnp.where(sub_wide == 7, pltpu.roll(ref[span_up, :], 7, 0), pltpu.roll(value, 7, 0))
            for ref, value in zip(fields, now)
        ]
        west = [pltpu.roll(value, 1, 1) for value in now]
        east = [pltpu.roll(value, width - 1, 1) for value in now]
        for ref, value in zip(fresh[1:], gas_update(now, down, up, west, east)[1:]):
            ref[span, :] = value
        return _

    lax.fori_loop(1, blocks - 1, inner_rows, 0)

    for block in (0, blocks - 1):
        at = block * 8
        now = [ref[at : at + 8, :] for ref in fields]
        sides = colbuf2[at : at + 8]
        down, up, west, east = [], [], [], []
        for f in range(3):
            edge = fields[f][at - 1 : at, :] if block else rows[0, f : f + 1, :]
            down.append(jnp.where(sub_wide == 0, edge, pltpu.roll(now[f], 1, 0)))
            edge = fields[f][at + 8 : at + 9, :] if block == 0 else rows[1, f : f + 1, :]
            up.append(jnp.where(sub_wide == 7, edge, pltpu.roll(now[f], 7, 0)))
            west.append(jnp.where(lane_wide == 0, sides[:, f : f + 1], pltpu.roll(now[f], 1, 1)))
            edge = pltpu.roll(now[f], width - 1, 1)
            east.append(jnp.where(lane_wide == width - 1, sides[:, 8 + f : 9 + f], edge))
        for ref, value in zip(fresh[1:], gas_update(now, down, up, west, east)[1:]):
            ref[at : at + 8, :] = value
    sub2 = lax.broadcasted_iota(jnp.int32, (8, 2 * LANES), 0)
    lane2 = lax.broadcasted_iota(jnp.int32, (8, 2 * LANES), 1)

    def side_cells(block, _):
        span = pl.ds(pl.multiple_of(block * 8, 8), 8)
        span_down = pl.ds(pl.multiple_of(block * 8 - 8, 8), 8)
        span_up = pl.ds(pl.multiple_of(block * 8 + 8, 8), 8)
        sides = colbuf2[span, :]
        for end in range(2):
            start_lane = 0 if end == 0 else width - 2 * LANES
            window = slice(start_lane, start_lane + 2 * LANES)
            now, down, up, west, east = [], [], [], [], []
            for f, ref in enumerate(fields):
                value = ref[span, window]
                now.append(value)
                edge = pltpu.roll(ref[span_down, window], 1, 0)
                down.append(jnp.where(sub2 == 0, edge, pltpu.roll(value, 1, 0)))
                edge = pltpu.roll(ref[span_up, window], 7, 0)
                up.append(jnp.where(sub2 == 7, edge, pltpu.roll(value, 7, 0)))
                left = pltpu.roll(value, 1, 1)
                right = pltpu.roll(value, 2 * LANES - 1, 1)
                if end == 0:
                    left = jnp.where(lane2 == 0, sides[:, f : f + 1], left)
                else:
                    right = jnp.where(lane2 == 2 * LANES - 1, sides[:, 8 + f : 9 + f], right)
                west.append(left)
                east.append(right)
            target = slice(0, LANES) if end == 0 else slice(width - LANES, width)
            kept = slice(0, LANES) if end == 0 else slice(LANES, 2 * LANES)
            for ref, value in zip(fresh[1:], gas_update(now, down, up, west, east)[1:]):
                ref[span, target] = value[:, kept]
        return _

    lax.fori_loop(1, blocks - 1, side_cells, 0)

    for final in finals[1:]:
        final.start()
    lax.fori_loop(0, outer, fill, 0)
    for load in table_loads:
        load.wait()

    for part in range(4):
        arrive(got1, recv1, step1, part)
        for at in range(part * step1, (part + 1) * step1, 8):
            f = [got1[a, at : at + 8, :] for a in range(gy)]
            plus = [None] + [f[a] + f[gy - a] for a in range(1, half_gy)]
            minus = [None] + [f[a] - f[gy - a] for a in range(1, half_gy)]

            def put(group, base, value):
                stage[group, base + at : base + at + 8, :] = value
                stage[group, base + packed + at : base + packed + at + 8, :] = flip(value)

            for g in range(half_gy + 1):
                re = f[0] + f[half_gy] if g % 2 == 0 else f[0] - f[half_gy]
                im = None
                for a in range(1, half_gy):
                    angle = 2.0 * np.pi * ((a * g) % gy) / gy
                    re = re + float(np.cos(angle)) * plus[a]
                    if 0 < g < half_gy:
                        term = float(-np.sin(angle)) * minus[a]
                        im = term if im is None else im + term
                if g == half_gy:
                    put(0, height, re)
                else:
                    put(g, 0, re)
                    if g:
                        put(g, height, im)
    lane = lax.broadcasted_iota(jnp.int32, (height, LANES), 1)
    ratio = height // lines
    for g in range(half_gy):
        both = dot_wide((y_table[0, g], y_table[1, g]), stage[g], ((1,), (0,)))
        value = jnp.where(lane < wide, both[:height], flip(both[height:]))
        for q in range(ratio):
            give2[g * ratio + q] = value[q * lines : (q + 1) * lines]
    for part in range(parts2):
        each(functools.partial(two, part), count)
    got2[me] = give2[me]

    def turned(value, c, s):
        return value * c + flip(value) * s

    def solve(load, rows, store):
        ci, si = inner_turn[0, rows, :], inner_turn[1, rows, :] * signs
        co, so = outer_turn[0, rows, :], outer_turn[1, rows, :]
        parts = [turned(load(d), co[:, d : d + 1], -so[:, d : d + 1] * signs) for d in range(outer)]
        parts = fft_packed(parts, -1.0, signs)
        for n in range(outer):
            value = turned(parts[n], ci, -si)
            mid[n] = turned(value, turn[0, n : n + 1, :], turn[1, n : n + 1, :])
        modes = dot_square(mid[...].reshape(outer * 8, LANES), x_table[0])
        modes = modes * green[:, rows, :].reshape(outer * 8, LANES)
        modes = dot_square(modes, x_table[1])
        mid[...] = modes.reshape(outer, 8, LANES)
        parts = []
        for n in range(outer):
            value = turned(mid[n], turn[0, n : n + 1, :], -turn[1, n : n + 1, :])
            parts.append(turned(value, ci, si))
        parts = fft_packed(parts, 1.0, signs)
        for d in range(outer):
            store(d, turned(parts[d], co[:, d : d + 1], so[:, d : d + 1] * signs))

    def load_extra(d):
        return jnp.where(jnp.logical_and(sub8 == 0, low), flip(got2[d, 0:8, :]), 0.0)

    def store_extra(d, value):
        extra[d] = flip(value)

    def chunk(part, _):
        arrive(got2, recv2, 8, part)
        rows = pl.ds(pl.multiple_of(part * 8, 8), 8)

        @pl.when(jnp.logical_and(part == 0, first))
        def _extra():
            solve(load_extra, pl.ds(lines, 8), store_extra)

        corner = jnp.logical_and(jnp.logical_and(sub8 == 0, lane8 >= wide), part == 0)
        damp = jnp.where(corner, keep, 1.0)
        mine = jnp.logical_and(corner, first)

        def load(d):
            return got2[d, rows, :] * damp

        def store(d, value):
            give3[d, rows, :] = jnp.where(mine, extra[d], value)

        solve(load, rows, store)
        each(functools.partial(three, part), count)
        return _

    lax.fori_loop(0, parts2, chunk, 0)
    got3[me] = give3[me]
    for part in range(parts2):
        arrive(got3, recv3, 8, part)

    for g in range(half_gy):
        value = got3[g * ratio : (g + 1) * ratio].reshape(height, LANES)
        value = jnp.concatenate([value, flip(value)], axis=0)
        stage[g] = dot_wide((y_table[0, g], y_table[1, g]), value, ((0,), (0,)))

    def take(group, base, at):
        near = stage[group, base + at : base + at + 8, :]
        far = stage[group, base + packed + at : base + packed + at + 8, :]
        return jnp.where(low, near, flip(far))

    for part in range(4):
        for at in range(part * step1, (part + 1) * step1, 8):
            re = [take(g, 0, at) for g in range(half_gy)]
            im = [None] + [take(g, height, at) for g in range(1, half_gy)]
            last = take(0, height, at)
            for a in range(half_gy + 1):
                even = re[0] + last if a % 2 == 0 else re[0] - last
                odd = None
                for g in range(1, half_gy):
                    angle = 2.0 * np.pi * ((a * g) % gy) / gy
                    even = even + float(np.cos(angle)) * re[g]
                    if 0 < a < half_gy:
                        term = float(np.sin(angle)) * im[g]
                        odd = term if odd is None else odd + term
                if odd is None:
                    give4[a, at : at + 8, :] = even
                else:
                    give4[a, at : at + 8, :] = even - odd
                    give4[gy - a, at : at + 8, :] = even + odd
        each(functools.partial(four, part), gy)
    own = pltpu.make_async_copy(give4.at[azimuth], out.at[azimuth], own_sem)
    own.start()
    for final in finals:
        final.wait()
    for side in range(2):
        row_copy(side).wait_send()
        col_wait(side, inner_edge if side == 0 else outer_edge, csend)
    leave(src, send1)
    leave(give2, send2)
    leave(give3, send3)
    for part in range(4):
        arrive(out, recv4, step1, part)
    leave(give4, send4)
    own.wait()


def fused_step(shift, fields, tables, nx, ny, gx, gy, ident):
    height, width = fields[0].shape
    packed = height // 2
    count = gx * gy
    lines = ny // 2 // count
    padded = lines + 8
    f32 = jnp.float32
    blocks = (gy, packed, LANES)
    sems = [pltpu.SemaphoreType.DMA((2,))] * 4
    for parts in (4, lines // 8, lines // 8, 4):
        sems += [pltpu.SemaphoreType.DMA, pltpu.SemaphoreType.DMA((parts,))]
    shape = jax.ShapeDtypeStruct((height, width), f32)
    return pl.pallas_call(
        functools.partial(fused_kernel, nx, ny),
        out_shape=(shape, shape, shape, jax.ShapeDtypeStruct(blocks, f32)),
        in_specs=[pl.BlockSpec(memory_space=pltpu.HBM)] * 7,
        out_specs=(HBM,) * 4,
        scratch_shapes=[pltpu.SMEM((1,), jnp.int32)]
        + [pltpu.VMEM((height, width), f32)] * 6
        + [pltpu.VMEM(table.shape, table.dtype) for table in tables]
        + [
            pltpu.SemaphoreType.DMA,
            pltpu.SemaphoreType.DMA((3,)),
            pltpu.SemaphoreType.DMA((3,)),
            pltpu.SemaphoreType.DMA((3,)),
            pltpu.SemaphoreType.DMA,
            pltpu.VMEM((2, gy, 8, height), f32),
            pltpu.VMEM((2, 8, width), f32),
            pltpu.VMEM((2, 8, height), f32),
            pltpu.VMEM((height, 16), f32),
            pltpu.VMEM((2, 8, width), f32),
            pltpu.VMEM((2, padded, LANES), f32),
            pltpu.VMEM((2, padded, LANES), f32),
            pltpu.VMEM(blocks, f32),
            pltpu.VMEM(blocks, f32),
            pltpu.VMEM((gy // 2, 2 * height, LANES), f32),
            pltpu.VMEM((count, lines, LANES), f32),
            pltpu.VMEM((count, lines, LANES), f32),
            pltpu.VMEM((count, padded, LANES), f32),
            pltpu.VMEM((count, 8, LANES), f32),
            pltpu.VMEM((count, 8, LANES), f32),
            pltpu.VMEM((count, lines, LANES), f32),
            pltpu.VMEM((count, lines, LANES), f32),
            pltpu.VMEM(blocks, f32),
        ]
        + sems,
        compiler_params=pltpu.CompilerParams(
            collective_id=ident, has_side_effects=True, vmem_limit_bytes=28 << 20
        ),
    )(shift, *[pltpu.with_memory_space_constraint(a, pltpu.HBM) for a in (*fields, *tables)])


def shards(density, xmomentum, ymomentum, shear_shift):
    gx, gy = lax.axis_size("gx"), lax.axis_size("gy")
    here_x, here_y = lax.axis_index("gx"), lax.axis_index("gy")
    height, width = density.shape[1:]
    nx, ny = width * gx, height * gy
    count = gx * gy
    xb = width // gy
    lines = ny // 2 // count
    shift = shear_shift[0]
    fields = [density[0], xmomentum[0], ymomentum[0]]

    fold = LANES // xb
    packed = height // fold
    wide = LANES // 2
    outer = nx // wide
    group = wide // xb
    y_table = jnp.asarray(azimuth_table(gy, height))
    turn, table = radial_tables(nx)
    square = jnp.asarray(square_np(table))
    turn, table = jnp.asarray(turn), jnp.asarray(table)
    if group == 1 and packed % 32 == 0 and lines % 8 == 0 and height % lines == 0:
        results = fused_step(shear_shift, fields, (y_table, turn, square), nx, ny, gx, gy, 1)
        return tuple(r[None] for r in unpack(results[:3], results[3]))

    cols, rows = halo(fields, gx, gy, 0)
    cols = jnp.transpose(cols, (0, 2, 1, 3)).reshape(2, 8, ny)
    cols = jnp.concatenate([cols, cols], axis=2)
    start_left = (here_y * height + jnp.where(here_x == 0, shift, 0)) % ny
    start_right = (here_y * height - jnp.where(here_x == gx - 1, shift, 0)) % ny
    ghost = jnp.stack(
        [
            lax.dynamic_slice_in_dim(cols[0], start_left, height, 1),
            lax.dynamic_slice_in_dim(cols[1], start_right, height, 1),
        ]
    )
    density_new, xmomentum_new, ymomentum_new = gas(fields, rows, ghost)
    padded = (lines + 8) // 8 * 8
    row = jnp.arange(padded, dtype=jnp.int32)
    slot = (here_x * gy + here_y) * lines + row
    wave = slot_wave(slot // height, slot % height, gy, height)
    wave = jnp.where(row == lines, ny // 2, jnp.where(row > lines, 1, wave))
    sigma = wave * shift % ny
    unit = 2.0 * jnp.pi / (nx * ny)

    def phases(points):
        angle = (sigma[:, None] * points[None, :] % (nx * ny)).astype(jnp.float32) * unit
        return jnp.stack([jnp.cos(angle), jnp.sin(angle)])

    lane = jnp.arange(LANES, dtype=jnp.int32)
    outer_turn = phases(jnp.where(lane < outer, lane, 0) * wide)
    inner_turn = phases(lane % wide)
    full = (padded, LANES)
    line_tables = (
        jnp.broadcast_to(wave[:, None], full),
        jnp.broadcast_to(sigma[:, None], full),
        outer_turn,
        inner_turn,
        turn,
        table,
    )

    blocks = jnp.transpose(density_new.reshape(fold, packed, gy, xb), (2, 1, 0, 3))
    blocks = exchange(blocks.reshape(gy, packed, LANES), gy, False, 1)
    slots = azimuth_forward(blocks, y_table, xb)
    slots = slots[:, :, : 2 * xb].reshape(count, lines, 2 * xb)
    slots = exchange(slots, gy, True, 2)
    if group > 1:
        slots = slots.reshape(outer, group, lines, 2, xb)
        slots = jnp.transpose(slots, (0, 2, 3, 1, 4)).reshape(outer, lines, LANES)
    solved = radial(slots, *line_tables, nx, ny)
    if group > 1:
        solved = solved.reshape(outer, lines, 2, group, xb)
        solved = jnp.transpose(solved, (0, 3, 1, 2, 4)).reshape(count, lines, 2 * xb)
    solved = exchange(solved, gy, True, 3).reshape(gy // 2, height, 2 * xb)
    solved = jnp.pad(solved, ((0, 0), (0, 0), (0, LANES - 2 * xb)))
    lined = azimuth_back(solved, y_table, xb, gy, packed)
    lined = exchange(lined, gy, False, 4)
    potential = jnp.transpose(lined.reshape(gy, packed, fold, xb), (2, 1, 0, 3))
    potential = potential.reshape(height, width)
    return (density_new[None], xmomentum_new[None], ymomentum_new[None], potential[None])


def solution(mesh):
    split_spec = P(None, "gy", "gx")
    return jax.shard_map(
        shards,
        mesh=mesh,
        in_specs=(split_spec, split_spec, split_spec, P()),
        out_specs=(split_spec,) * 4,
        check_vma=False,
    )
```
